32 devices in a mesh: slab: 8 (over y, x, core), probe: 4 (over z).
Axes of the slice: x: 2, y: 2, z: 4, core: 2. Of those that a mesh axis runs over, the one named last changes fastest.
Arguments:
- probe_fields: bfloat16 [256, 32, 8192], P('probe', 'slab'), may hold values from -6 to 6
- sensor_rows: int32 [4096], replicated, may hold values from 0 to 30, as said below
- sensor_cols: int32 [4096], replicated, may hold values from 0 to 8190
- row_frac: float32 [4096], replicated, may hold values from 0 to 1
- col_frac: float32 [4096], replicated, may hold values from 0 to 1
- sensor_weights: float32 [4096], replicated, may hold values from 0.05 to 1
- owner_order: int32 [4096], replicated, may hold values from 0 to 4095, as said below
Outputs:
- adjoint_sources: bfloat16 [256, 32, 8192], P('probe', 'slab')
- observed: float32 [256, 4096], P('probe', 'slab')
- trace_mean: float32 [], replicated
The draws below stay inside these ranges and needn't reach their ends.
Inputs may be any that keep to these rules, and one draw needn't show every extreme that they name: `sensor_rows`: rows run from 0 to 30. The sensors whose row lies in one slab of 4 rows number at most 2048, and some slab holds exactly 2048. `owner_order`: A permutation. The 4096 // 8 slots of one owner name at most 256 sensors whose row lies in any one slab, and every owner reaches 256 for some slab.
All inputs are finite; a program needn't handle non-finite values.
Results may differ from the reference program's by a relative error of at most 0.0068.
Values sent between devices are 32-bit elements; how exact they have to be, the bound alone decides.
A program may use at most 64 MiB of HBM per device.

```python
import math
import jax
import jax.numpy as jnp
from jax import lax

ROWS_DEV = 4
NCOL = 8192
SENSORS = 4096
NX = 32
PROBES = 256


def sensor_layout(key):
    slab_total = NX // ROWS_DEV
    slab_most = 4 * SENSORS // slab_total
    own_count = SENSORS // slab_total
    busiest = jax.random.randint(jax.random.fold_in(key, 11), (), 0, slab_total)
    position = jnp.arange(SENSORS, dtype=jnp.int32)
    others = (position - slab_most) % (slab_total - 1)
    others = others + (others >= busiest).astype(jnp.int32)
    slab_seq = jnp.sort(jnp.where(position < slab_most, busiest, others))
    row_inside = jax.random.randint(jax.random.fold_in(key, 12), (SENSORS,), 0, ROWS_DEV)
    row_inside = jnp.where((slab_seq == slab_total - 1) & (row_inside == ROWS_DEV - 1), row_inside - 1, row_inside)
    rows_seq = (slab_seq * ROWS_DEV + row_inside).astype(jnp.int32)
    sensor_ids = jax.random.permutation(jax.random.fold_in(key, 13), SENSORS).astype(jnp.int32)
    sensor_rows = jnp.zeros((SENSORS,), jnp.int32).at[sensor_ids].set(rows_seq)
    owner_perm = jax.random.permutation(jax.random.fold_in(key, 14), slab_total).astype(jnp.int32)
    shuffle = jax.random.permutation(jax.random.fold_in(key, 15), own_count).astype(jnp.int32)
    rotate = jax.random.randint(jax.random.fold_in(key, 16), (slab_total,), 0, own_count)
    owner_of = owner_perm[position % slab_total]
    inside = (shuffle[position // slab_total] + rotate[owner_of]) % own_count
    slot_of = (owner_of * own_count + inside).astype(jnp.int32)
    owner_order = jnp.zeros((SENSORS,), jnp.int32).at[slot_of].set(sensor_ids)
    return (sensor_rows, owner_order)


def draw_sensor_rows(key, part):
    return sensor_layout(key)[0]


def draw_owner_order(key, part):
    return sensor_layout(key)[1]


def with_ends(result, key, low, top_value):
    longest = result.shape.index(max(result.shape))
    spots = []
    for shift in (0, 1):
        where = [jax.random.randint(jax.random.fold_in(key, axis), (), 0, length) for axis, length in enumerate(result.shape)]
        where[longest] = (where[longest] + shift) % result.shape[longest]
        spots.append(tuple(where))
    return result.at[spots[0]].set(low).at[spots[1]].set(top_value)


def block_levels(rng, dims, split, least, high):
    def one(dim, shards_of):
        steps = jax.random.uniform(jax.random.fold_in(jax.random.fold_in(rng, 6), dim), (shards_of,), jnp.float32, least / len(split), high / len(split))
        return jnp.repeat(jnp.exp(steps), dims[dim] // shards_of).reshape((-1,) + (1,) * (len(dims) - dim - 1))

    loudness = one(*split[0])
    for cut in split[1:]:
        loudness = loudness * one(*cut)
    return loudness


def bell_draw(rng, extent, scale, most, pieces=(), kind=jnp.bfloat16):
    level = block_levels(rng, extent, pieces, -0.22, 0.18) if pieces else 1.0
    entries = jax.random.normal(rng, extent, jnp.float32) * scale * level
    return jnp.minimum(jnp.maximum(entries, -most), most).astype(kind)


def setup_inputs(seed: int = 0) -> dict:
    keys = jax.random.split(jax.random.key(seed), 8)
    return {
        "probe_fields": bell_draw(keys[0], (PROBES, NX, NCOL), 1.0, 6.0, ((0, 4), (1, 8))),
        "sensor_rows": draw_sensor_rows(jax.random.fold_in(keys[7], 71), 0),
        "sensor_cols": with_ends(jax.random.randint(keys[2], (SENSORS,), 0, NCOL - 1), jax.random.fold_in(keys[2], 1), 0, (NCOL - 1) - 1).astype(jnp.int32),
        "row_frac": jnp.clip(jax.random.uniform(keys[3], (SENSORS,), jnp.float32, 0.0, 1.0), 0.0, 1.0),
        "col_frac": jnp.clip(jax.random.uniform(keys[4], (SENSORS,), jnp.float32, 0.0, 1.0), 0.0, 1.0),
        "sensor_weights": jnp.clip(jnp.exp(jax.random.uniform(keys[5], (SENSORS,), jnp.float32, math.log(0.05), math.log(1.0))), 0.05, 1.0),
        "owner_order": draw_owner_order(jax.random.fold_in(keys[7], 71), 0),
    }


def reference(probe_fields, sensor_rows, sensor_cols, row_frac, col_frac, sensor_weights, owner_order):
    rlow = 1.0 - row_frac
    rhigh = row_frac
    clow = lax.optimization_barrier((1.0 - col_frac).astype(jnp.bfloat16)).astype(jnp.float32)
    chigh = lax.optimization_barrier(col_frac.astype(jnp.bfloat16)).astype(jnp.float32)
    rows_next = sensor_rows + 1
    cols_next = sensor_cols + 1

    def sample(field):
        field = field.astype(jnp.float32)
        top = clow * field[sensor_rows, sensor_cols] + chigh * field[sensor_rows, cols_next]
        bottom = clow * field[rows_next, sensor_cols] + chigh * field[rows_next, cols_next]
        return rlow * top + rhigh * bottom

    values = lax.map(sample, probe_fields)
    observed = values[:, owner_order]
    weights = sensor_weights[owner_order]
    spread = observed * weights[None, :]
    trace_mean = jnp.sum(spread * observed) / (PROBES * SENSORS)
    owned_rows = sensor_rows[owner_order]
    owned_cols = sensor_cols[owner_order]
    owned_low = rlow[owner_order]
    owned_high = rhigh[owner_order]
    clow_owned = clow[owner_order]
    chigh_owned = chigh[owner_order]

    def place(spread_row):
        lower = (spread_row * owned_low).astype(jnp.bfloat16).astype(jnp.float32)
        upper = (spread_row * owned_high).astype(jnp.bfloat16).astype(jnp.float32)
        grid = jnp.zeros((NX, NCOL), jnp.float32)
        grid = grid.at[owned_rows, owned_cols].add(lower * clow_owned)
        grid = grid.at[owned_rows, owned_cols + 1].add(lower * chigh_owned)
        grid = grid.at[owned_rows + 1, owned_cols].add(upper * clow_owned)
        grid = grid.at[owned_rows + 1, owned_cols + 1].add(upper * chigh_owned)
        return grid.astype(jnp.bfloat16)

    adjoint_sources = lax.map(place, spread)
    return adjoint_sources, observed, trace_mean
```

```python
import functools

import jax
import jax.numpy as jnp
from jax import lax
from jax.experimental import pallas as pl
from jax.experimental.pallas import tpu as pltpu
from jax.sharding import PartitionSpec as P

LANES = 128
BLOCK = 256
FIELDS = 11
F32 = jnp.float32
BF16 = jnp.bfloat16
NT = (((1,), (1,)), ((), ()))
VMEM = pltpu.VMEM
SMEM = pltpu.SMEM
LIMIT = pltpu.CompilerParams(vmem_limit_bytes=60 * 1024 * 1024)


def iota(shape, dim):
    return lax.broadcasted_iota(jnp.int32, shape, dim)


def nt_dot(a, b):
    return lax.dot_general(a, b, NT, preferred_element_type=F32)


def plan_kernel(rows, cap_chunks, blocks, first_ref, r_ref, c_ref, rf_ref, cf_ref, w_ref, order_ref, plan_ref, lo_ref, hi_ref):
    lines = r_ref.shape[0]
    sensors = lines * LANES
    step = min(4, lines)
    first = first_ref[0]
    keys_group = 2 * blocks
    keys = 3 * keys_group
    chunks = 3 * cap_chunks

    def wide(x, i):
        return jnp.concatenate([x[i + j : i + j + 1, :] for j in range(step)], axis=1)

    order = order_ref[...]
    slot = iota((lines, LANES), 0) * LANES + iota((lines, LANES), 1)
    found = jnp.zeros((2 * lines, LANES), F32)
    for i in range(0, lines, step):
        target = wide(order, i)
        mine = wide(slot, i)
        here = iota((lines, step * LANES), 0) == (target >> 7)
        stack = jnp.concatenate(
            [jnp.where(here, (mine >> 7).astype(F32), 0.0), jnp.where(here, (mine & 127).astype(F32), 0.0)], axis=0
        ).astype(BF16)
        place = jnp.where(iota((LANES, step * LANES), 0) == (target & 127), 1.0, 0.0).astype(BF16)
        found = found + nt_dot(stack, place)
    slot_hi = found[:lines, :]
    slot_lo = found[lines:, :]

    r = r_ref[...]
    c = c_ref[...]
    rel = r - first + 1
    valid = (rel >= 0) & (rel <= rows)
    group = jnp.where(rel == 0, 0, jnp.where(rel == rows, 2, 1))
    block = c // BLOCK
    inner = c - block * BLOCK
    key = group * keys_group + 2 * block + jnp.where(inner == BLOCK - 1, 1, 0)
    key = jnp.where(valid, key, -1)

    count = jnp.zeros((keys, 1), F32)
    for i in range(lines):
        count = count + jnp.sum(jnp.where(iota((keys, LANES), 0) == key[i : i + 1, :], 1.0, 0.0), axis=1, keepdims=True)
    big = jnp.floor(count * (1.0 / 64.0))
    small = count - 64.0 * big
    ka, kb = iota((keys, keys), 0), iota((keys, keys), 1)
    below = jnp.where((kb < ka) & (kb // keys_group == ka // keys_group), 1.0, 0.0).astype(BF16)
    start = 64.0 * jnp.dot(below, jnp.broadcast_to(big, (keys, LANES)).astype(BF16), preferred_element_type=F32)
    start = start + jnp.dot(below, jnp.broadcast_to(small, (keys, LANES)).astype(BF16), preferred_element_type=F32)
    start = start + ((iota((keys, LANES), 0) // keys_group) * (cap_chunks * LANES)).astype(F32)
    lo_ref[...] = start.astype(jnp.int32)
    hi_ref[...] = (start + count).astype(jnp.int32)

    upper = jnp.where(iota((LANES, LANES), 0) < iota((LANES, LANES), 1), 1.0, 0.0).astype(BF16)
    carry = start[:, :1]
    spots = []
    for i in range(lines):
        hot = jnp.where(iota((keys, LANES), 0) == key[i : i + 1, :], 1.0, 0.0)
        before = jnp.dot(hot.astype(BF16), upper, preferred_element_type=F32)
        spots.append(jnp.sum(hot * (before + carry), axis=0, keepdims=True))
        carry = carry + jnp.sum(hot, axis=1, keepdims=True)
    spot = jnp.concatenate(spots, axis=0).astype(jnp.int32)
    spot = jnp.where(valid, spot, -1)

    rf = rf_ref[...]
    cf = cf_ref[...]
    w = w_ref[...]
    rf_top = rf.astype(BF16).astype(F32)
    w_top = w.astype(BF16).astype(F32)
    values = [
        block.astype(F32),
        inner.astype(F32),
        (1.0 - cf).astype(BF16).astype(F32),
        cf.astype(BF16).astype(F32),
        rf_top,
        rf - rf_top,
        w_top,
        w - w_top,
        rel.astype(F32),
        slot_hi,
        slot_lo,
    ]
    total = jnp.zeros((FIELDS * chunks, LANES), F32)
    for i in range(0, lines, step):
        target = wide(spot, i)
        here = iota((chunks, step * LANES), 0) == (target >> 7)
        stack = jnp.concatenate([jnp.where(here, wide(v, i), 0.0) for v in values], axis=0).astype(BF16)
        place = jnp.where(iota((LANES, step * LANES), 0) == (target & 127), 1.0, 0.0).astype(BF16)
        total = total + nt_dot(stack, place)
    for f in range(FIELDS):
        plan_ref[f] = total[f * chunks : (f + 1) * chunks, :]


def column_table(plan_ref, chunk, number):
    line = pl.ds(chunk, 1)
    column = ((plan_ref[0, line, :] - number.astype(F32)) * BLOCK + plan_ref[1, line, :]).astype(jnp.int32)
    cells = iota((BLOCK, LANES), 0)
    return jnp.where(
        cells == column, plan_ref[2, line, :], jnp.where(cells == column + 1, plan_ref[3, line, :], 0.0)
    ).astype(BF16)


def row_pattern(plan_ref, chunk, rows, depth):
    line = pl.ds(chunk, 1)
    rf = plan_ref[4, line, :] + plan_ref[5, line, :]
    rel = plan_ref[8, line, :].astype(jnp.int32)
    row = iota((depth, LANES), 0) % rows + 1
    return jnp.where(row == rel, 1.0 - rf, jnp.where(row == rel + 1, rf, 0.0))


def group_chunks(hi_ref, group, keys_group, base):
    return (hi_ref[(group + 1) * keys_group - 1] - base + LANES - 1) // LANES


def chunk_range(lo_ref, hi_ref, group, number, keys_group):
    at = group * keys_group + 2 * number
    begin = lo_ref[jnp.maximum(at - 1, group * keys_group)]
    end = hi_ref[at + 1]
    return begin // LANES, jnp.where(end > begin, (end + LANES - 1) // LANES, begin // LANES)


def forward_kernel(cap_chunks, field_ref, plan_ref, lo_ref, hi_ref, value_ref, slots_ref, flat, sums, parts):
    probes, rows, width = field_ref.shape
    depth = probes * rows
    blocks = width // BLOCK
    keys_group = 2 * blocks
    lines = parts.shape[0]
    parts[...] = jnp.zeros_like(parts)
    counts = [group_chunks(hi_ref, g, keys_group, g * cap_chunks * LANES) for g in range(3)]
    for g in range(3):

        @pl.loop(0, counts[g])
        def _(k):
            sums[g * cap_chunks + k] = jnp.zeros((depth, LANES), F32)

    @pl.loop(0, blocks)
    def _(number):
        cols = pl.ds(pl.multiple_of(number * BLOCK, BLOCK), BLOCK)
        flat[...] = field_ref[:, :, cols].astype(F32).reshape(depth, BLOCK).astype(BF16)
        for g in range(3):
            begin, end = chunk_range(lo_ref, hi_ref, g, number, keys_group)

            @pl.loop(begin, end)
            def _(chunk):
                table = column_table(plan_ref, chunk, number)
                sums[chunk] += jnp.dot(flat[...], table, preferred_element_type=F32)

    fold = jnp.where(iota((probes, depth), 1) // rows == iota((probes, depth), 0), 1.0, 0.0).astype(BF16)
    for g in range(3):

        @pl.loop(0, counts[g])
        def _(k):
            chunk = g * cap_chunks + k
            scaled = (sums[chunk] * row_pattern(plan_ref, chunk, rows, depth)).astype(BF16)
            value = jnp.dot(fold, scaled, preferred_element_type=F32)
            value_ref[:, pl.ds(pl.multiple_of(chunk * LANES, LANES), LANES)] = value
            line = pl.ds(chunk, 1)
            high = plan_ref[9, line, :].astype(jnp.int32)
            low = plan_ref[10, line, :].astype(jnp.int32)
            place = jnp.where(iota((LANES, LANES), 0) == low, 1.0, 0.0).astype(BF16)
            stack = jnp.concatenate([jnp.where(high == d, value, 0.0) for d in range(lines)], axis=0).astype(BF16)
            parts[...] += nt_dot(stack, place).reshape(lines, probes, LANES)

    for d in range(lines):
        slots_ref[:, d * LANES : (d + 1) * LANES] = parts[d]


def adjoint_kernel(cap_chunks, value_ref, above_ref, below_ref, plan_ref, lo_ref, hi_ref, out_ref, trace_ref, sources, total, squares):
    probes, rows, width = out_ref.shape
    depth = probes * rows
    blocks = width // BLOCK
    keys_group = 2 * blocks
    squares[...] = jnp.zeros_like(squares)
    spread_out = jnp.where(iota((depth, probes), 0) // rows == iota((depth, probes), 1), 1.0, 0.0).astype(BF16)
    for g in range(3):
        count = group_chunks(hi_ref, g, keys_group, g * cap_chunks * LANES)

        @pl.loop(0, count)
        def _(k):
            chunk = g * cap_chunks + k
            value = value_ref[:, pl.ds(pl.multiple_of(chunk * LANES, LANES), LANES)]
            near = pl.ds(pl.multiple_of(k * LANES, LANES), LANES)
            if g == 0:
                value = value + below_ref[:, near]
            if g == 2:
                value = value + above_ref[:, near]
            line = pl.ds(chunk, 1)
            spread = value * (plan_ref[6, line, :] + plan_ref[7, line, :])
            if g > 0:
                squares[...] += spread * value
            raised = jnp.dot(spread_out, spread.astype(BF16), preferred_element_type=F32)
            sources[chunk] = (raised * row_pattern(plan_ref, chunk, rows, depth)).astype(BF16)

    trace_ref[...] = jnp.sum(squares[...], axis=0, keepdims=True)

    @pl.loop(0, blocks)
    def _(number):
        total[...] = jnp.zeros_like(total)
        for g in range(3):
            begin, end = chunk_range(lo_ref, hi_ref, g, number, keys_group)

            @pl.loop(begin, end)
            def _(chunk):
                total[...] += nt_dot(sources[chunk], column_table(plan_ref, chunk, number))

        cols = pl.ds(pl.multiple_of(number * BLOCK, BLOCK), BLOCK)
        out_ref[:, :, cols] = total[...].reshape(probes, rows, BLOCK).astype(BF16)


def body(slab_count, probe_groups, probe_fields, sensor_rows, sensor_cols, row_frac, col_frac, sensor_weights, owner_order):
    probes, rows, width = probe_fields.shape
    sensors = sensor_rows.shape[0]
    depth = probes * rows
    lines = sensors // LANES
    blocks = width // BLOCK
    keys = 6 * blocks
    most = min(sensors, 4 * sensors // slab_count)
    cap_chunks = -(-most // (8 * LANES)) * 8
    cap = cap_chunks * LANES
    chunks = 3 * cap_chunks
    slab_index = lax.axis_index("slab")
    first = jnp.reshape(slab_index * rows, (1,)).astype(jnp.int32)
    boxed = [x.reshape(lines, LANES) for x in (sensor_rows, sensor_cols, row_frac, col_frac, sensor_weights, owner_order)]
    vmem = pl.BlockSpec(memory_space=VMEM)
    smem = pl.BlockSpec(memory_space=SMEM)
    plan, lo, hi = pl.pallas_call(
        functools.partial(plan_kernel, rows, cap_chunks, blocks),
        out_shape=(
            jax.ShapeDtypeStruct((FIELDS, chunks, LANES), F32),
            jax.ShapeDtypeStruct((keys, LANES), jnp.int32),
            jax.ShapeDtypeStruct((keys, LANES), jnp.int32),
        ),
        in_specs=[smem] + [vmem] * 6,
        out_specs=(vmem, vmem, vmem),
        compiler_params=LIMIT,
        name="plan",
    )(first, *boxed)
    lo = lo[:, 0]
    hi = hi[:, 0]
    value, slots = pl.pallas_call(
        functools.partial(forward_kernel, cap_chunks),
        out_shape=(
            jax.ShapeDtypeStruct((probes, chunks * LANES), F32),
            jax.ShapeDtypeStruct((probes, sensors), F32),
        ),
        in_specs=[vmem, vmem, smem, smem],
        out_specs=(vmem, vmem),
        scratch_shapes=[
            VMEM((depth, BLOCK), BF16),
            VMEM((chunks, depth, LANES), F32),
            VMEM((lines, probes, LANES), F32),
        ],
        compiler_params=LIMIT,
        name="forward",
    )(probe_fields, plan, lo, hi)
    observed = lax.psum_scatter(slots, "slab", scatter_dimension=1, tiled=True)
    down = [(j, (j - 1) % slab_count) for j in range(slab_count)]
    up = [(j, (j + 1) % slab_count) for j in range(slab_count)]
    above = lax.ppermute(value[:, :cap], "slab", down)
    below = lax.ppermute(value[:, 2 * cap :], "slab", up)
    adjoint, trace = pl.pallas_call(
        functools.partial(adjoint_kernel, cap_chunks),
        out_shape=(
            jax.ShapeDtypeStruct((probes, rows, width), BF16),
            jax.ShapeDtypeStruct((1, LANES), F32),
        ),
        in_specs=[vmem, vmem, vmem, vmem, smem, smem],
        out_specs=(vmem, vmem),
        scratch_shapes=[
            VMEM((chunks, depth, LANES), BF16),
            VMEM((depth, BLOCK), F32),
            VMEM((probes, LANES), F32),
        ],
        compiler_params=LIMIT,
        name="adjoint",
    )(value, above, below, plan, lo, hi)
    trace_mean = lax.psum(jnp.sum(trace), ("slab", "probe")) / (probes * probe_groups * sensors)
    return adjoint, observed, trace_mean


def solution(mesh):
    placed = (P("probe", "slab", None), P(), P(), P(), P(), P(), P())
    return jax.shard_map(
        functools.partial(body, mesh.shape["slab"], mesh.shape["probe"]),
        mesh=mesh,
        in_specs=placed,
        out_specs=(P("probe", "slab", None), P("probe", "slab"), P()),
        check_vma=False,
    )
```

```python
import functools

import jax
import jax.numpy as jnp
from jax import lax
from jax.experimental import pallas as pl
from jax.experimental.pallas import tpu as pltpu
from jax.sharding import PartitionSpec as P

LANES = 128
BLOCK = 512
HALF = 256
FIELDS = 11
F32 = jnp.float32
BF16 = jnp.bfloat16
NT = (((1,), (1,)), ((), ()))
VMEM = pltpu.VMEM
SMEM = pltpu.SMEM
LIMIT = pltpu.CompilerParams(vmem_limit_bytes=60 * 1024 * 1024)


def iota(shape, dim):
    return lax.broadcasted_iota(jnp.int32, shape, dim)


def nt_dot(a, b):
    return lax.dot_general(a, b, NT, preferred_element_type=F32)


def plan_kernel(rows, cap_chunks, blocks, slabs, pair_lines, me_ref, r_ref, c_ref, rf_ref, cf_ref, w_ref, order_ref, plan_ref, marks_ref, places_ref):
    lines = r_ref.shape[0]
    sensors = lines * LANES
    step = min(4, lines)
    me = me_ref[0]
    first = me * rows
    owned = lines * LANES // slabs
    keys_group = 2 * blocks
    keys = 3 * keys_group
    chunks = 3 * cap_chunks

    def wide(x, i):
        return jnp.concatenate([x[i + j : i + j + 1, :] for j in range(step)], axis=1)

    order = order_ref[...]
    slot = iota((lines, LANES), 0) * LANES + iota((lines, LANES), 1)
    found = jnp.zeros((2 * lines, LANES), F32)
    for i in range(0, lines, step):
        target = wide(order, i)
        mine = wide(slot, i)
        here = iota((lines, step * LANES), 0) == (target >> 7)
        stack = jnp.concatenate(
            [jnp.where(here, (mine >> 7).astype(F32), 0.0), jnp.where(here, (mine & 127).astype(F32), 0.0)], axis=0
        ).astype(BF16)
        place = jnp.where(iota((LANES, step * LANES), 0) == (target & 127), 1.0, 0.0).astype(BF16)
        found = found + nt_dot(stack, place)
    slot_hi = found[:lines, :]
    slot_lo = found[lines:, :]

    r = r_ref[...]
    c = c_ref[...]
    rel = r - first + 1
    valid = (rel >= 0) & (rel <= rows)
    group = jnp.where(rel == 0, 0, jnp.where(rel == rows, 2, 1))
    block = c // BLOCK
    inner = c - block * BLOCK
    half = c // HALF
    slot_of = (slot_hi * LANES + slot_lo).astype(jnp.int32)
    owner = slot_of // owned
    home = r // rows
    send_key = jnp.where(home == me, owner, -1)
    recv_key = jnp.where(owner == me, home, -1)
    key = group * keys_group + 2 * block + jnp.where(inner == BLOCK - 1, 1, 0)
    key = jnp.where(valid, key, -1)

    count = jnp.zeros((keys, 1), F32)
    for i in range(lines):
        count = count + jnp.sum(jnp.where(iota((keys, LANES), 0) == key[i : i + 1, :], 1.0, 0.0), axis=1, keepdims=True)
    big = jnp.floor(count * (1.0 / 64.0))
    small = count - 64.0 * big
    ka, kb = iota((keys, keys), 0), iota((keys, keys), 1)
    below = jnp.where((kb < ka) & (kb // keys_group == ka // keys_group), 1.0, 0.0).astype(BF16)
    start = 64.0 * jnp.dot(below, jnp.broadcast_to(big, (keys, LANES)).astype(BF16), preferred_element_type=F32)
    start = start + jnp.dot(below, jnp.broadcast_to(small, (keys, LANES)).astype(BF16), preferred_element_type=F32)
    start = start + ((iota((keys, LANES), 0) // keys_group) * (cap_chunks * LANES)).astype(F32)
    marks_ref[0] = start.astype(jnp.int32)
    marks_ref[1] = (start + count).astype(jnp.int32)

    upper = jnp.where(iota((LANES, LANES), 0) < iota((LANES, LANES), 1), 1.0, 0.0).astype(BF16)
    carry = jnp.concatenate([start[:, :1], jnp.zeros((2 * slabs, 1), F32)], axis=0)
    spots, sends, recvs = [], [], []
    for i in range(lines):
        hot = jnp.concatenate(
            [
                jnp.where(iota((keys, LANES), 0) == key[i : i + 1, :], 1.0, 0.0),
                jnp.where(iota((slabs, LANES), 0) == send_key[i : i + 1, :], 1.0, 0.0),
                jnp.where(iota((slabs, LANES), 0) == recv_key[i : i + 1, :], 1.0, 0.0),
            ],
            axis=0,
        )
        before = jnp.dot(hot.astype(BF16), upper, preferred_element_type=F32)
        ranks = hot * (before + carry)
        spots.append(jnp.sum(ranks[:keys], axis=0, keepdims=True))
        sends.append(jnp.sum(ranks[keys : keys + slabs], axis=0, keepdims=True))
        recvs.append(jnp.sum(ranks[keys + slabs :], axis=0, keepdims=True))
        carry = carry + jnp.sum(hot, axis=1, keepdims=True)
    spot = jnp.concatenate(spots, axis=0).astype(jnp.int32)
    spot = jnp.where(valid, spot, -1)
    send = jnp.concatenate(sends, axis=0).astype(jnp.int32)
    recv = jnp.concatenate(recvs, axis=0).astype(jnp.int32)
    send_line = jnp.where(send_key >= 0, owner * pair_lines + (send >> 7), 200)
    recv_line = jnp.where(recv_key >= 0, home * pair_lines + (recv >> 7), -1)

    rf = rf_ref[...]
    cf = cf_ref[...]
    w = w_ref[...]
    rf_top = rf.astype(BF16).astype(F32)
    w_top = w.astype(BF16).astype(F32)
    values = [
        half.astype(F32),
        (c - half * HALF).astype(F32),
        (1.0 - cf).astype(BF16).astype(F32),
        cf.astype(BF16).astype(F32),
        rf_top,
        rf - rf_top,
        w_top,
        w - w_top,
        rel.astype(F32),
        send_line.astype(F32),
        (send & 127).astype(F32),
    ]
    total = jnp.zeros((FIELDS * chunks, LANES), F32)
    for i in range(0, lines, step):
        target = wide(spot, i)
        here = iota((chunks, step * LANES), 0) == (target >> 7)
        stack = jnp.concatenate([jnp.where(here, wide(v, i), 0.0) for v in values], axis=0).astype(BF16)
        place = jnp.where(iota((LANES, step * LANES), 0) == (target & 127), 1.0, 0.0).astype(BF16)
        total = total + nt_dot(stack, place)
    for f in range(FIELDS):
        plan_ref[f] = total[f * chunks : (f + 1) * chunks, :]

    slot_here = slot_of - me * owned
    received = slabs * pair_lines
    found = jnp.zeros((2 * received, LANES), F32)
    for i in range(0, lines, step):
        here = iota((received, step * LANES), 0) == wide(recv_line, i)
        target = wide(slot_here, i)
        stack = jnp.concatenate(
            [jnp.where(here, (target >> 7).astype(F32), 0.0), jnp.where(here, (target & 127).astype(F32), 0.0)], axis=0
        ).astype(BF16)
        place = jnp.where(iota((LANES, step * LANES), 0) == (wide(recv, i) & 127), 1.0, 0.0).astype(BF16)
        found = found + nt_dot(stack, place)
    places_ref[...] = (found[:received] * LANES + found[received:]).astype(jnp.int32)


def column_table(plan_ref, chunk, number):
    line = pl.ds(chunk, 1)
    column = (plan_ref[0, line, :] * HALF + plan_ref[1, line, :]).astype(jnp.int32) - number * BLOCK
    cells = iota((BLOCK, LANES), 0)
    return jnp.where(
        cells == column, plan_ref[2, line, :], jnp.where(cells == column + 1, plan_ref[3, line, :], 0.0)
    ).astype(BF16)


def row_pattern(plan_ref, chunk, rows, depth):
    line = pl.ds(chunk, 1)
    rf = plan_ref[4, line, :] + plan_ref[5, line, :]
    rel = plan_ref[8, line, :].astype(jnp.int32)
    row = iota((depth, LANES), 0) % rows + 1
    return jnp.where(row == rel, 1.0 - rf, jnp.where(row == rel + 1, rf, 0.0))


def group_chunks(marks_ref, group, keys_group, base):
    return (marks_ref[1, (group + 1) * keys_group - 1, 0] - base + LANES - 1) // LANES


def chunk_range(marks_ref, group, number, keys_group):
    at = group * keys_group + 2 * number
    begin = marks_ref[0, jnp.maximum(at - 1, group * keys_group), 0]
    end = marks_ref[1, at + 1, 0]
    return begin // LANES, jnp.where(end > begin, (end + LANES - 1) // LANES, begin // LANES)


def forward_kernel(cap_chunks, field_ref, plan_ref, marks_ref, value_ref, flat, sums):
    probes, rows, width = field_ref.shape
    depth = probes * rows
    blocks = width // BLOCK
    keys_group = 2 * blocks
    counts = [group_chunks(marks_ref, g, keys_group, g * cap_chunks * LANES) for g in range(3)]
    for g in range(3):

        @pl.loop(0, counts[g])
        def _(k):
            sums[g * cap_chunks + k] = jnp.zeros((depth, LANES), F32)

    @pl.loop(0, blocks)
    def _(number):
        cols = pl.ds(pl.multiple_of(number * BLOCK, BLOCK), BLOCK)
        flat[...] = field_ref[:, :, cols].astype(F32).reshape(depth, BLOCK).astype(BF16)
        for g in range(3):
            begin, end = chunk_range(marks_ref, g, number, keys_group)

            @pl.loop(begin, end)
            def _(chunk):
                table = column_table(plan_ref, chunk, number)
                sums[chunk] += jnp.dot(flat[...], table, preferred_element_type=F32)

    fold = jnp.where(iota((probes, depth), 1) // rows == iota((probes, depth), 0), 1.0, 0.0).astype(BF16)
    for g in range(3):

        @pl.loop(0, counts[g])
        def _(k):
            chunk = g * cap_chunks + k
            scaled = (sums[chunk] * row_pattern(plan_ref, chunk, rows, depth)).astype(BF16)
            value_ref[:, pl.ds(pl.multiple_of(chunk * LANES, LANES), LANES)] = jnp.dot(
                fold, scaled, preferred_element_type=F32
            )


def merge_kernel(cap_chunks, blocks, value_ref, above_ref, below_ref, plan_ref, marks_ref, spread_ref, packed_ref, trace_ref, squares):
    outgoing, probes, _ = packed_ref.shape
    keys_group = 2 * blocks
    squares[...] = jnp.zeros_like(squares)
    packed_ref[...] = jnp.zeros_like(packed_ref)
    for g in range(3):
        count = group_chunks(marks_ref, g, keys_group, g * cap_chunks * LANES)

        @pl.loop(0, count)
        def _(k):
            chunk = g * cap_chunks + k
            value = value_ref[:, pl.ds(pl.multiple_of(chunk * LANES, LANES), LANES)]
            near = pl.ds(pl.multiple_of(k * LANES, LANES), LANES)
            if g == 0:
                value = value + below_ref[:, near]
            if g == 2:
                value = value + above_ref[:, near]
            line = pl.ds(chunk, 1)
            spread = value * (plan_ref[6, line, :] + plan_ref[7, line, :])
            spread_ref[chunk] = spread.astype(BF16)
            if g > 0:
                squares[...] += spread * value
                high = plan_ref[9, line, :].astype(jnp.int32)
                low = plan_ref[10, line, :].astype(jnp.int32)
                place = jnp.where(iota((LANES, LANES), 0) == low, 1.0, 0.0).astype(BF16)
                stack = jnp.concatenate([jnp.where(high == d, value, 0.0) for d in range(outgoing)], axis=0).astype(BF16)
                packed_ref[...] += nt_dot(stack, place).reshape(outgoing, probes, LANES)

    trace_ref[...] = jnp.sum(squares[...], axis=0, keepdims=True)


def unpack_kernel(packed_ref, places_ref, observed_ref):
    received, probes, _ = packed_ref.shape
    owned = observed_ref.shape[1]
    total = jnp.zeros((probes, owned), F32)
    for d in range(received):
        place = jnp.where(iota((owned, LANES), 0) == places_ref[d : d + 1, :], 1.0, 0.0).astype(BF16)
        total = total + nt_dot(packed_ref[d].astype(BF16), place)
    observed_ref[...] = total


def adjoint_kernel(cap_chunks, spread_ref, plan_ref, marks_ref, out_ref, sources, total):
    probes, rows, width = out_ref.shape
    depth = probes * rows
    blocks = width // BLOCK
    keys_group = 2 * blocks
    raise_rows = jnp.where(iota((depth, probes), 0) // rows == iota((depth, probes), 1), 1.0, 0.0).astype(BF16)
    for g in range(3):
        count = group_chunks(marks_ref, g, keys_group, g * cap_chunks * LANES)

        @pl.loop(0, count)
        def _(k):
            chunk = g * cap_chunks + k
            raised = jnp.dot(raise_rows, spread_ref[chunk], preferred_element_type=F32)
            sources[chunk] = (raised * row_pattern(plan_ref, chunk, rows, depth)).astype(BF16)

    @pl.loop(0, blocks)
    def _(number):
        total[...] = jnp.zeros_like(total)
        for g in range(3):
            begin, end = chunk_range(marks_ref, g, number, keys_group)

            @pl.loop(begin, end)
            def _(chunk):
                total[...] += nt_dot(sources[chunk], column_table(plan_ref, chunk, number))

        cols = pl.ds(pl.multiple_of(number * BLOCK, BLOCK), BLOCK)
        out_ref[:, :, cols] = total[...].reshape(probes, rows, BLOCK).astype(BF16)


def body(slab_count, probe_groups, probe_fields, sensor_rows, sensor_cols, row_frac, col_frac, sensor_weights, owner_order):
    probes, rows, width = probe_fields.shape
    sensors = sensor_rows.shape[0]
    depth = probes * rows
    lines = sensors // LANES
    blocks = width // BLOCK
    keys = 6 * blocks
    most = min(sensors, 4 * sensors // slab_count)
    cap_chunks = -(-most // (8 * LANES)) * 8
    cap = cap_chunks * LANES
    chunks = 3 * cap_chunks
    pair_lines = -(-most // (slab_count * LANES))
    outgoing = slab_count * pair_lines
    me = jnp.reshape(lax.axis_index("slab"), (1,)).astype(jnp.int32)
    boxed = [x.reshape(lines, LANES) for x in (sensor_rows, sensor_cols, row_frac, col_frac, sensor_weights, owner_order)]
    vmem = pl.BlockSpec(memory_space=VMEM)
    smem = pl.BlockSpec(memory_space=SMEM)
    plan, marks, places = pl.pallas_call(
        functools.partial(plan_kernel, rows, cap_chunks, blocks, slab_count, pair_lines),
        out_shape=(
            jax.ShapeDtypeStruct((FIELDS, chunks, LANES), F32),
            jax.ShapeDtypeStruct((2, keys, LANES), jnp.int32),
            jax.ShapeDtypeStruct((outgoing, LANES), jnp.int32),
        ),
        in_specs=[smem] + [vmem] * 6,
        out_specs=(vmem, vmem, vmem),
        compiler_params=LIMIT,
        name="plan",
    )(me, *boxed)
    value = pl.pallas_call(
        functools.partial(forward_kernel, cap_chunks),
        out_shape=jax.ShapeDtypeStruct((probes, chunks * LANES), F32),
        in_specs=[vmem, vmem, smem],
        out_specs=vmem,
        scratch_shapes=[
            VMEM((depth, BLOCK), BF16),
            VMEM((chunks, depth, LANES), F32),
        ],
        compiler_params=LIMIT,
        name="forward",
    )(probe_fields, plan, marks)
    down = [(j, (j - 1) % slab_count) for j in range(slab_count)]
    up = [(j, (j + 1) % slab_count) for j in range(slab_count)]
    above = lax.ppermute(value[:, :cap], "slab", down)
    below = lax.ppermute(value[:, 2 * cap :], "slab", up)
    spread, packed, trace = pl.pallas_call(
        functools.partial(merge_kernel, cap_chunks, blocks),
        out_shape=(
            jax.ShapeDtypeStruct((chunks, probes, LANES), BF16),
            jax.ShapeDtypeStruct((outgoing, probes, LANES), F32),
            jax.ShapeDtypeStruct((1, LANES), F32),
        ),
        in_specs=[vmem, vmem, vmem, vmem, smem],
        out_specs=(vmem, vmem, vmem),
        scratch_shapes=[VMEM((probes, LANES), F32)],
        compiler_params=LIMIT,
        name="merge",
    )(value, above, below, plan, marks)
    arrived = lax.all_to_all(packed, "slab", 0, 0, tiled=True)
    adjoint = pl.pallas_call(
        functools.partial(adjoint_kernel, cap_chunks),
        out_shape=jax.ShapeDtypeStruct((probes, rows, width), BF16),
        in_specs=[vmem, vmem, smem],
        out_specs=vmem,
        scratch_shapes=[
            VMEM((chunks, depth, LANES), BF16),
            VMEM((depth, BLOCK), F32),
        ],
        compiler_params=LIMIT,
        cost_estimate=pl.CostEstimate(flops=4 * 10**9, bytes_accessed=8 * 10**6, transcendentals=0),
        name="adjoint",
    )(spread, plan, marks)
    observed = pl.pallas_call(
        unpack_kernel,
        out_shape=jax.ShapeDtypeStruct((probes, sensors // slab_count), F32),
        in_specs=[vmem, vmem],
        out_specs=vmem,
        compiler_params=LIMIT,
        name="unpack",
    )(arrived, places)
    trace_mean = lax.psum(jnp.sum(trace), ("slab", "probe")) / (probes * probe_groups * sensors)
    return adjoint, observed, trace_mean


def solution(mesh):
    placed = (P("probe", "slab", None), P(), P(), P(), P(), P(), P())
    return jax.shard_map(
        functools.partial(body, mesh.shape["slab"], mesh.shape["probe"]),
        mesh=mesh,
        in_specs=placed,
        out_specs=(P("probe", "slab", None), P("probe", "slab"), P()),
        check_vma=False,
    )
```

```python
import functools

import jax
import jax.numpy as jnp
from jax import lax
from jax.experimental import pallas as pl
from jax.experimental.pallas import tpu as pltpu
from jax.sharding import PartitionSpec as P

LANES = 128
BLOCK = 512
HALF = 256
FIELDS = 11
F32 = jnp.float32
BF16 = jnp.bfloat16
NT = (((1,), (1,)), ((), ()))
VMEM = pltpu.VMEM
SMEM = pltpu.SMEM
LIMIT = pltpu.CompilerParams(vmem_limit_bytes=60 * 1024 * 1024)


def iota(shape, dim):
    return lax.broadcasted_iota(jnp.int32, shape, dim)


def nt_dot(a, b):
    return lax.dot_general(a, b, NT, preferred_element_type=F32)


def plan_kernel(rows, cap_chunks, blocks, slabs, pair_lines, me_ref, r_ref, c_ref, rf_ref, cf_ref, w_ref, order_ref, plan_ref, marks_ref, places_ref, peak_ref):
    lines = r_ref.shape[0]
    sensors = lines * LANES
    step = min(4, lines)
    me = me_ref[0]
    first = me * rows
    owned = lines * LANES // slabs
    keys_group = 2 * blocks
    keys = 3 * keys_group
    chunks = 3 * cap_chunks

    def wide(x, i):
        return jnp.concatenate([x[i + j : i + j + 1, :] for j in range(step)], axis=1)

    order = order_ref[...]
    slot = iota((lines, LANES), 0) * LANES + iota((lines, LANES), 1)
    found = jnp.zeros((2 * lines, LANES), F32)
    for i in range(0, lines, step):
        target = wide(order, i)
        mine = wide(slot, i)
        here = iota((lines, step * LANES), 0) == (target >> 7)
        stack = jnp.concatenate(
            [jnp.where(here, (mine >> 7).astype(F32), 0.0), jnp.where(here, (mine & 127).astype(F32), 0.0)], axis=0
        ).astype(BF16)
        place = jnp.where(iota((LANES, step * LANES), 0) == (target & 127), 1.0, 0.0).astype(BF16)
        found = found + nt_dot(stack, place)
    slot_hi = found[:lines, :]
    slot_lo = found[lines:, :]

    r = r_ref[...]
    c = c_ref[...]
    rel = r - first + 1
    valid = (rel >= 0) & (rel <= rows)
    group = jnp.where(rel == 0, 0, jnp.where(rel == rows, 2, 1))
    block = c // BLOCK
    inner = c - block * BLOCK
    half = c // HALF
    slot_of = (slot_hi * LANES + slot_lo).astype(jnp.int32)
    owner = slot_of // owned
    home = r // rows
    send_key = jnp.where(home == me, owner, -1)
    recv_key = jnp.where(owner == me, home, -1)
    edge = jnp.where(r - home * rows == rows - 1, home, -1)
    edges = jnp.zeros((slabs, LANES), F32)
    for i in range(lines):
        edges = edges + jnp.where(iota((slabs, LANES), 0) == edge[i : i + 1, :], 1.0, 0.0)
    peak = jnp.max(jnp.sum(edges, axis=1, keepdims=True), axis=0, keepdims=True)
    peak_ref[...] = jnp.broadcast_to(peak, (8, LANES)).astype(jnp.int32)
    key = group * keys_group + 2 * block + jnp.where(inner == BLOCK - 1, 1, 0)
    key = jnp.where(valid, key, -1)

    count = jnp.zeros((keys, 1), F32)
    for i in range(lines):
        count = count + jnp.sum(jnp.where(iota((keys, LANES), 0) == key[i : i + 1, :], 1.0, 0.0), axis=1, keepdims=True)
    big = jnp.floor(count * (1.0 / 64.0))
    small = count - 64.0 * big
    ka, kb = iota((keys, keys), 0), iota((keys, keys), 1)
    below = jnp.where((kb < ka) & (kb // keys_group == ka // keys_group), 1.0, 0.0).astype(BF16)
    start = 64.0 * jnp.dot(below, jnp.broadcast_to(big, (keys, LANES)).astype(BF16), preferred_element_type=F32)
    start = start + jnp.dot(below, jnp.broadcast_to(small, (keys, LANES)).astype(BF16), preferred_element_type=F32)
    start = start + ((iota((keys, LANES), 0) // keys_group) * (cap_chunks * LANES)).astype(F32)
    marks_ref[0] = start.astype(jnp.int32)
    marks_ref[1] = (start + count).astype(jnp.int32)

    upper = jnp.where(iota((LANES, LANES), 0) < iota((LANES, LANES), 1), 1.0, 0.0).astype(BF16)
    carry = jnp.concatenate([start[:, :1], jnp.zeros((2 * slabs, 1), F32)], axis=0)
    spots, sends, recvs = [], [], []
    for i in range(lines):
        hot = jnp.concatenate(
            [
                jnp.where(iota((keys, LANES), 0) == key[i : i + 1, :], 1.0, 0.0),
                jnp.where(iota((slabs, LANES), 0) == send_key[i : i + 1, :], 1.0, 0.0),
                jnp.where(iota((slabs, LANES), 0) == recv_key[i : i + 1, :], 1.0, 0.0),
            ],
            axis=0,
        )
        before = jnp.dot(hot.astype(BF16), upper, preferred_element_type=F32)
        ranks = hot * (before + carry)
        spots.append(jnp.sum(ranks[:keys], axis=0, keepdims=True))
        sends.append(jnp.sum(ranks[keys : keys + slabs], axis=0, keepdims=True))
        recvs.append(jnp.sum(ranks[keys + slabs :], axis=0, keepdims=True))
        carry = carry + jnp.sum(hot, axis=1, keepdims=True)
    spot = jnp.concatenate(spots, axis=0).astype(jnp.int32)
    spot = jnp.where(valid, spot, -1)
    send = jnp.concatenate(sends, axis=0).astype(jnp.int32)
    recv = jnp.concatenate(recvs, axis=0).astype(jnp.int32)
    send_line = jnp.where(send_key >= 0, owner * pair_lines + (send >> 7), 200)
    recv_line = jnp.where(recv_key >= 0, home * pair_lines + (recv >> 7), -1)

    rf = rf_ref[...]
    cf = cf_ref[...]
    w = w_ref[...]
    rf_top = rf.astype(BF16).astype(F32)
    w_top = w.astype(BF16).astype(F32)
    values = [
        half.astype(F32),
        (c - half * HALF).astype(F32),
        (1.0 - cf).astype(BF16).astype(F32),
        cf.astype(BF16).astype(F32),
        rf_top,
        rf - rf_top,
        w_top,
        w - w_top,
        rel.astype(F32),
        send_line.astype(F32),
        (send & 127).astype(F32),
    ]
    total = jnp.zeros((FIELDS * chunks, LANES), F32)
    for i in range(0, lines, step):
        target = wide(spot, i)
        here = iota((chunks, step * LANES), 0) == (target >> 7)
        stack = jnp.concatenate([jnp.where(here, wide(v, i), 0.0) for v in values], axis=0).astype(BF16)
        place = jnp.where(iota((LANES, step * LANES), 0) == (target & 127), 1.0, 0.0).astype(BF16)
        total = total + nt_dot(stack, place)
    for f in range(FIELDS):
        plan_ref[f] = total[f * chunks : (f + 1) * chunks, :]

    slot_here = slot_of - me * owned
    received = slabs * pair_lines
    found = jnp.zeros((2 * received, LANES), F32)
    for i in range(0, lines, step):
        here = iota((received, step * LANES), 0) == wide(recv_line, i)
        target = wide(slot_here, i)
        stack = jnp.concatenate(
            [jnp.where(here, (target >> 7).astype(F32), 0.0), jnp.where(here, (target & 127).astype(F32), 0.0)], axis=0
        ).astype(BF16)
        place = jnp.where(iota((LANES, step * LANES), 0) == (wide(recv, i) & 127), 1.0, 0.0).astype(BF16)
        found = found + nt_dot(stack, place)
    places_ref[...] = (found[:received] * LANES + found[received:]).astype(jnp.int32)


def column_table(plan_ref, chunk, number):
    line = pl.ds(chunk, 1)
    column = (plan_ref[0, line, :] * HALF + plan_ref[1, line, :]).astype(jnp.int32) - number * BLOCK
    cells = iota((BLOCK, LANES), 0)
    return jnp.where(
        cells == column, plan_ref[2, line, :], jnp.where(cells == column + 1, plan_ref[3, line, :], 0.0)
    ).astype(BF16)


def row_pattern(plan_ref, chunk, rows, depth):
    line = pl.ds(chunk, 1)
    rf = plan_ref[4, line, :] + plan_ref[5, line, :]
    rel = plan_ref[8, line, :].astype(jnp.int32)
    row = iota((depth, LANES), 0) % rows + 1
    return jnp.where(row == rel, 1.0 - rf, jnp.where(row == rel + 1, rf, 0.0))


def group_chunks(marks_ref, group, keys_group, base):
    count = (marks_ref[1, (group + 1) * keys_group - 1, 0] - base + LANES - 1) // LANES
    return jnp.maximum(count, 1)


def chunk_range(marks_ref, group, number, keys_group, cap_chunks):
    at = group * keys_group + 2 * number
    begin = marks_ref[0, jnp.maximum(at - 1, group * keys_group), 0]
    end = marks_ref[1, at + 1, 0]
    base = group * cap_chunks
    last = base + group_chunks(marks_ref, group, keys_group, base * LANES) - 1
    return jnp.minimum(begin // LANES, last), jnp.where(end > begin, (end + LANES - 1) // LANES, 0)


def forward_kernel(cap_chunks, blocks, field_ref, plan_ref, marks_ref, value_ref, sums):
    probes, rows, _ = field_ref.shape
    depth = probes * rows
    keys_group = 2 * blocks
    number = pl.program_id(0)
    counts = [group_chunks(marks_ref, g, keys_group, g * cap_chunks * LANES) for g in range(3)]

    @pl.when(number == 0)
    def _():
        for g in range(3):

            @pl.loop(0, counts[g])
            def _(k):
                sums[g * cap_chunks + k] = jnp.zeros((depth, LANES), F32)

    flat = field_ref[...].astype(F32).reshape(depth, BLOCK).astype(BF16)
    ranges = [chunk_range(marks_ref, g, number, keys_group, cap_chunks) for g in range(3)]
    table = jnp.concatenate([column_table(plan_ref, begin, number) for begin, _ in ranges], axis=1)
    part = jnp.dot(flat, table, preferred_element_type=F32)
    for g in range(3):
        sums[ranges[g][0]] += part[:, g * LANES : (g + 1) * LANES]
    for g in range(3):

        @pl.loop(ranges[g][0] + 1, ranges[g][1])
        def _(chunk):
            again = field_ref[...].astype(F32).reshape(depth, BLOCK).astype(BF16)
            sums[chunk] += jnp.dot(again, column_table(plan_ref, chunk, number), preferred_element_type=F32)

    @pl.when(number == blocks - 1)
    def _():
        fold = jnp.where(iota((probes, depth), 1) // rows == iota((probes, depth), 0), 1.0, 0.0).astype(BF16)
        for g in range(3):

            @pl.loop(0, counts[g])
            def _(k):
                chunk = g * cap_chunks + k
                scaled = (sums[chunk] * row_pattern(plan_ref, chunk, rows, depth)).astype(BF16)
                value_ref[chunk] = jnp.dot(fold, scaled, preferred_element_type=F32)


def swap_kernel(slabs, top, value_ref, above_ref, below_ref, send_sem, recv_sem):
    probe, me = lax.axis_index("probe"), lax.axis_index("slab")
    width = above_ref.shape[0]
    down, up = lax.rem(me + slabs - 1, slabs), lax.rem(me + 1, slabs)
    barrier = pltpu.get_barrier_semaphore()
    for peer in (down, up):
        pl.semaphore_signal(barrier, inc=1, device_id=(peer, probe), device_id_type=pl.DeviceIdType.MESH)
    pl.semaphore_wait(barrier, 2)
    copies = []
    for k, (peer, begin, target) in enumerate(((down, 0, above_ref), (up, top, below_ref))):
        copies.append(
            pltpu.make_async_remote_copy(
                src_ref=value_ref.at[begin : begin + width],
                dst_ref=target,
                send_sem=send_sem.at[k],
                recv_sem=recv_sem.at[k],
                device_id=(peer, probe),
                device_id_type=pl.DeviceIdType.MESH,
            )
        )
    for copy in copies:
        copy.start()
    for copy in copies:
        copy.wait()


def swap(slabs, cap_chunks, width, number, value):
    part = (width, *value.shape[1:])
    any_space = pl.BlockSpec(memory_space=pl.ANY)
    above, below = pl.pallas_call(
        functools.partial(swap_kernel, slabs, 2 * cap_chunks),
        out_shape=(jax.ShapeDtypeStruct(part, F32), jax.ShapeDtypeStruct(part, F32)),
        in_specs=[any_space],
        out_specs=(any_space, any_space),
        scratch_shapes=[pltpu.SemaphoreType.DMA((2,)), pltpu.SemaphoreType.DMA((2,))],
        compiler_params=pltpu.CompilerParams(collective_id=number, has_side_effects=True),
        name="swap",
    )(value)
    return above, below


def exchange_kernel(slabs, groups, scale, packed_ref, trace_ref, arrived_ref, mean_ref, traces, send_sem, recv_sem, tsend_sem, trecv_sem, local_sem):
    me, probe = lax.axis_index("slab"), lax.axis_index("probe")
    lines = packed_ref.shape[0] // slabs
    devices = slabs * groups
    mine = me * groups + probe
    mesh_id = pl.DeviceIdType.MESH

    def peer_at(k):
        other = lax.rem(mine + k, devices)
        return other, other // groups, lax.rem(other, groups)

    barrier = pltpu.get_barrier_semaphore()

    def greet(k, carry):
        _, s, p = peer_at(k)
        pl.semaphore_signal(barrier, inc=1, device_id=(s, p), device_id_type=mesh_id)
        return carry

    lax.fori_loop(1, devices, greet, 0)
    pl.semaphore_wait(barrier, devices - 1)

    def lists(k):
        s = lax.rem(me + k, slabs)
        return pltpu.make_async_remote_copy(
            src_ref=packed_ref.at[pl.ds(s * lines, lines)],
            dst_ref=arrived_ref.at[pl.ds(me * lines, lines)],
            send_sem=send_sem.at[k],
            recv_sem=recv_sem.at[k],
            device_id=(s, probe),
            device_id_type=mesh_id,
        )

    def arriving(k):
        s = lax.rem(me + slabs - k, slabs)
        return pltpu.make_async_remote_copy(
            src_ref=packed_ref.at[pl.ds(s * lines, lines)],
            dst_ref=arrived_ref.at[pl.ds(s * lines, lines)],
            send_sem=send_sem.at[k],
            recv_sem=recv_sem.at[k],
            device_id=(s, probe),
            device_id_type=mesh_id,
        )

    def tile(k, slot, s, p):
        return pltpu.make_async_remote_copy(
            src_ref=trace_ref,
            dst_ref=traces.at[slot],
            send_sem=tsend_sem.at[k],
            recv_sem=trecv_sem.at[k],
            device_id=(s, p),
            device_id_type=mesh_id,
        )

    for k in range(1, slabs):
        lists(k).start()
    own = pltpu.make_async_copy(
        packed_ref.at[pl.ds(me * lines, lines)], arrived_ref.at[pl.ds(me * lines, lines)], local_sem.at[0]
    )
    own.start()
    own_tile = pltpu.make_async_copy(trace_ref, traces.at[mine], local_sem.at[1])
    own_tile.start()

    def send_tile(k, carry):
        _, s, p = peer_at(k)
        tile(k, mine, s, p).start()
        return carry

    def wait_tile(k, carry):
        other = lax.rem(mine + devices - k, devices)
        tile(k, other, other // groups, lax.rem(other, groups)).wait()
        return carry

    lax.fori_loop(1, devices, send_tile, 0)
    own_tile.wait()
    lax.fori_loop(1, devices, wait_tile, 0)
    total = jnp.sum(jnp.sum(traces[...], axis=0), axis=0, keepdims=True)
    mean_ref[...] = jnp.broadcast_to(jnp.sum(total, axis=1, keepdims=True) * scale, mean_ref.shape)
    own.wait()
    for k in range(1, slabs):
        arriving(k).wait()


def merge_kernel(cap_chunks, blocks, value_ref, above_ref, below_ref, plan_ref, marks_ref, spread_ref, packed_ref, trace_ref, squares):
    outgoing, probes, _ = packed_ref.shape
    keys_group = 2 * blocks
    squares[...] = jnp.zeros_like(squares)
    packed_ref[...] = jnp.zeros_like(packed_ref)
    for g in range(3):
        count = group_chunks(marks_ref, g, keys_group, g * cap_chunks * LANES)

        @pl.loop(0, count)
        def _(k):
            chunk = g * cap_chunks + k
            value = value_ref[chunk]
            if g == 0:
                value = value + below_ref[k]
            if g == 2:
                value = value + above_ref[k]
            line = pl.ds(chunk, 1)
            spread = value * (plan_ref[6, line, :] + plan_ref[7, line, :])
            spread_ref[chunk] = spread.astype(BF16)
            if g > 0:
                squares[...] += spread * value
                high = plan_ref[9, line, :].astype(jnp.int32)
                low = plan_ref[10, line, :].astype(jnp.int32)
                place = jnp.where(iota((LANES, LANES), 0) == low, 1.0, 0.0).astype(BF16)
                stack = jnp.concatenate([jnp.where(high == d, value, 0.0) for d in range(outgoing)], axis=0).astype(BF16)
                packed_ref[...] += nt_dot(stack, place).reshape(outgoing, probes, LANES)

    folded = squares[:8, :]
    for d in range(8, probes, 8):
        folded = folded + squares[d : d + 8, :]
    trace_ref[...] = folded


def unpack_kernel(packed_ref, places_ref, observed_ref):
    received, probes, _ = packed_ref.shape
    owned = observed_ref.shape[1]
    total = jnp.zeros((probes, owned), F32)
    for d in range(received):
        place = jnp.where(iota((owned, LANES), 0) == places_ref[d : d + 1, :], 1.0, 0.0).astype(BF16)
        total = total + nt_dot(packed_ref[d].astype(BF16), place)
    observed_ref[...] = total


def adjoint_kernel(cap_chunks, blocks, spread_ref, plan_ref, marks_ref, out_ref, sources, total):
    probes, rows, _ = out_ref.shape
    depth = probes * rows
    keys_group = 2 * blocks
    number = pl.program_id(0)

    @pl.when(number == 0)
    def _():
        raise_rows = jnp.where(iota((depth, probes), 0) // rows == iota((depth, probes), 1), 1.0, 0.0).astype(BF16)
        for g in range(3):
            count = group_chunks(marks_ref, g, keys_group, g * cap_chunks * LANES)

            @pl.loop(0, count)
            def _(k):
                chunk = g * cap_chunks + k
                raised = jnp.dot(raise_rows, spread_ref[chunk], preferred_element_type=F32)
                sources[chunk] = (raised * row_pattern(plan_ref, chunk, rows, depth)).astype(BF16)

    ranges = [chunk_range(marks_ref, g, number, keys_group, cap_chunks) for g in range(3)]
    table = jnp.concatenate([column_table(plan_ref, begin, number) for begin, _ in ranges], axis=1)
    source = jnp.concatenate([sources[begin] for begin, _ in ranges], axis=1)
    total[...] = nt_dot(source, table)
    for g in range(3):

        @pl.loop(ranges[g][0] + 1, ranges[g][1])
        def _(chunk):
            total[...] += nt_dot(sources[chunk], column_table(plan_ref, chunk, number))

    out_ref[...] = total[...].reshape(probes, rows, BLOCK).astype(BF16)


def body(slab_count, probe_groups, probe_fields, sensor_rows, sensor_cols, row_frac, col_frac, sensor_weights, owner_order):
    probes, rows, width = probe_fields.shape
    sensors = sensor_rows.shape[0]
    depth = probes * rows
    lines = sensors // LANES
    blocks = width // BLOCK
    keys = 6 * blocks
    most = min(sensors, 4 * sensors // slab_count)
    cap_chunks = -(-most // (8 * LANES)) * 8
    chunks = 3 * cap_chunks
    pair_lines = -(-most // (slab_count * LANES))
    outgoing = slab_count * pair_lines
    me = jnp.reshape(lax.axis_index("slab"), (1,)).astype(jnp.int32)
    boxed = [x.reshape(lines, LANES) for x in (sensor_rows, sensor_cols, row_frac, col_frac, sensor_weights, owner_order)]
    vmem = pl.BlockSpec(memory_space=VMEM)
    smem = pl.BlockSpec(memory_space=SMEM)
    plan, marks, places, peak = pl.pallas_call(
        functools.partial(plan_kernel, rows, cap_chunks, blocks, slab_count, pair_lines),
        out_shape=(
            jax.ShapeDtypeStruct((FIELDS, chunks, LANES), F32),
            jax.ShapeDtypeStruct((2, keys, LANES), jnp.int32),
            jax.ShapeDtypeStruct((outgoing, LANES), jnp.int32),
            jax.ShapeDtypeStruct((8, LANES), jnp.int32),
        ),
        in_specs=[smem] + [vmem] * 6,
        out_specs=(vmem, vmem, vmem, vmem),
        compiler_params=LIMIT,
        name="plan",
    )(me, *boxed)
    value = pl.pallas_call(
        functools.partial(forward_kernel, cap_chunks, blocks),
        out_shape=jax.ShapeDtypeStruct((chunks, probes, LANES), F32),
        grid=(blocks,),
        in_specs=[pl.BlockSpec((probes, rows, BLOCK), lambda n: (0, 0, n)), vmem, smem],
        out_specs=vmem,
        scratch_shapes=[VMEM((chunks, depth, LANES), F32)],
        compiler_params=LIMIT,
        name="forward",
    )(probe_fields, plan, marks)
    few = min(cap_chunks, -(-5 * most // (4 * rows * LANES)))

    def merged(above, below):
        return pl.pallas_call(
            functools.partial(merge_kernel, cap_chunks, blocks),
            out_shape=(
                jax.ShapeDtypeStruct((chunks, probes, LANES), BF16),
                jax.ShapeDtypeStruct((outgoing, probes, LANES), F32),
                jax.ShapeDtypeStruct((8, LANES), F32),
            ),
            in_specs=[vmem, vmem, vmem, vmem, smem],
            out_specs=(vmem, vmem, vmem),
            scratch_shapes=[VMEM((probes, LANES), F32)],
            compiler_params=LIMIT,
            name="merge",
        )(value, above, below, plan, marks)

    spread, packed, trace = lax.cond(
        peak[0, 0] <= few * LANES,
        lambda: merged(*swap(slab_count, cap_chunks, few, 0, value)),
        lambda: merged(*swap(slab_count, cap_chunks, cap_chunks, 1, value)),
    )
    devices = slab_count * probe_groups
    arrived, mean = pl.pallas_call(
        functools.partial(exchange_kernel, slab_count, probe_groups, 1.0 / (probes * probe_groups * sensors)),
        out_shape=(jax.ShapeDtypeStruct(packed.shape, F32), jax.ShapeDtypeStruct((1, LANES), F32)),
        in_specs=[vmem, vmem],
        out_specs=(vmem, vmem),
        scratch_shapes=[
            VMEM((devices, 8, LANES), F32),
            pltpu.SemaphoreType.DMA((slab_count,)),
            pltpu.SemaphoreType.DMA((slab_count,)),
            pltpu.SemaphoreType.DMA((devices,)),
            pltpu.SemaphoreType.DMA((devices,)),
            pltpu.SemaphoreType.DMA((2,)),
        ],
        compiler_params=pltpu.CompilerParams(collective_id=2, has_side_effects=True, vmem_limit_bytes=40 * 1024 * 1024),
        name="exchange",
    )(packed, trace)
    adjoint = pl.pallas_call(
        functools.partial(adjoint_kernel, cap_chunks, blocks),
        out_shape=jax.ShapeDtypeStruct((probes, rows, width), BF16),
        grid=(blocks,),
        in_specs=[vmem, vmem, smem],
        out_specs=pl.BlockSpec((probes, rows, BLOCK), lambda n: (0, 0, n)),
        scratch_shapes=[
            VMEM((chunks, depth, LANES), BF16),
            VMEM((depth, BLOCK), F32),
        ],
        compiler_params=LIMIT,
        name="adjoint",
    )(spread, plan, marks)
    observed = pl.pallas_call(
        unpack_kernel,
        out_shape=jax.ShapeDtypeStruct((probes, sensors // slab_count), F32),
        in_specs=[vmem, vmem],
        out_specs=vmem,
        compiler_params=LIMIT,
        name="unpack",
    )(arrived, places)
    return adjoint, observed, mean[0, 0]


def solution(mesh):
    placed = (P("probe", "slab", None), P(), P(), P(), P(), P(), P())
    return jax.shard_map(
        functools.partial(body, mesh.shape["slab"], mesh.shape["probe"]),
        mesh=mesh,
        in_specs=placed,
        out_specs=(P("probe", "slab", None), P("probe", "slab"), P()),
        check_vma=False,
    )
```

```python
import functools

import jax
import jax.numpy as jnp
from jax import lax
from jax.experimental import pallas as pl
from jax.experimental.pallas import tpu as pltpu
from jax.sharding import PartitionSpec as P

LANES = 128
BLOCK = 512
HALF = 256
FIELDS = 11
F32 = jnp.float32
BF16 = jnp.bfloat16
NT = (((1,), (1,)), ((), ()))
VMEM = pltpu.VMEM
SMEM = pltpu.SMEM
LIMIT = pltpu.CompilerParams(vmem_limit_bytes=60 * 1024 * 1024)


def iota(shape, dim):
    return lax.broadcasted_iota(jnp.int32, shape, dim)


def nt_dot(a, b):
    return lax.dot_general(a, b, NT, preferred_element_type=F32)


def plan_kernel(rows, cap_chunks, blocks, slabs, pair_lines, me_ref, r_ref, c_ref, rf_ref, cf_ref, w_ref, order_ref, plan_ref, marks_ref, places_ref, peak_ref):
    lines = r_ref.shape[0]
    sensors = lines * LANES
    step = min(4, lines)
    me = me_ref[0]
    first = me * rows
    owned = lines * LANES // slabs
    keys_group = 2 * blocks
    keys = 3 * keys_group
    chunks = 3 * cap_chunks

    def wide(x, i):
        return jnp.concatenate([x[i + j : i + j + 1, :] for j in range(step)], axis=1)

    order = order_ref[...]
    slot = iota((lines, LANES), 0) * LANES + iota((lines, LANES), 1)
    found = jnp.zeros((2 * lines, LANES), F32)
    for i in range(0, lines, step):
        target = wide(order, i)
        mine = wide(slot, i)
        here = iota((lines, step * LANES), 0) == (target >> 7)
        stack = jnp.concatenate(
            [jnp.where(here, (mine >> 7).astype(F32), 0.0), jnp.where(here, (mine & 127).astype(F32), 0.0)], axis=0
        ).astype(BF16)
        place = jnp.where(iota((LANES, step * LANES), 0) == (target & 127), 1.0, 0.0).astype(BF16)
        found = found + nt_dot(stack, place)
    slot_hi = found[:lines, :]
    slot_lo = found[lines:, :]

    r = r_ref[...]
    c = c_ref[...]
    rel = r - first + 1
    valid = (rel >= 0) & (rel <= rows)
    group = jnp.where(rel == 0, 0, jnp.where(rel == rows, 2, 1))
    block = c // BLOCK
    inner = c - block * BLOCK
    half = c // HALF
    slot_of = (slot_hi * LANES + slot_lo).astype(jnp.int32)
    owner = slot_of // owned
    home = r // rows
    send_key = jnp.where(home == me, owner, -1)
    recv_key = jnp.where(owner == me, home, -1)
    edge = jnp.where(r - home * rows == rows - 1, home, -1)
    edges = jnp.zeros((slabs, LANES), F32)
    for i in range(lines):
        edges = edges + jnp.where(iota((slabs, LANES), 0) == edge[i : i + 1, :], 1.0, 0.0)
    peak = jnp.max(jnp.sum(edges, axis=1, keepdims=True), axis=0, keepdims=True)
    peak_ref[...] = jnp.broadcast_to(peak, (8, LANES)).astype(jnp.int32)
    key = group * keys_group + 2 * block + jnp.where(inner == BLOCK - 1, 1, 0)
    key = jnp.where(valid, key, -1)

    count = jnp.zeros((keys, 1), F32)
    for i in range(lines):
        count = count + jnp.sum(jnp.where(iota((keys, LANES), 0) == key[i : i + 1, :], 1.0, 0.0), axis=1, keepdims=True)
    big = jnp.floor(count * (1.0 / 64.0))
    small = count - 64.0 * big
    ka, kb = iota((keys, keys), 0), iota((keys, keys), 1)
    below = jnp.where((kb < ka) & (kb // keys_group == ka // keys_group), 1.0, 0.0).astype(BF16)
    start = 64.0 * jnp.dot(below, jnp.broadcast_to(big, (keys, LANES)).astype(BF16), preferred_element_type=F32)
    start = start + jnp.dot(below, jnp.broadcast_to(small, (keys, LANES)).astype(BF16), preferred_element_type=F32)
    start = start + ((iota((keys, LANES), 0) // keys_group) * (cap_chunks * LANES)).astype(F32)
    marks_ref[0] = start.astype(jnp.int32)
    marks_ref[1] = (start + count).astype(jnp.int32)

    upper = jnp.where(iota((LANES, LANES), 0) < iota((LANES, LANES), 1), 1.0, 0.0).astype(BF16)
    carry = jnp.concatenate([start[:, :1], jnp.zeros((2 * slabs, 1), F32)], axis=0)
    spots, sends, recvs = [], [], []
    for i in range(lines):
        hot = jnp.concatenate(
            [
                jnp.where(iota((keys, LANES), 0) == key[i : i + 1, :], 1.0, 0.0),
                jnp.where(iota((slabs, LANES), 0) == send_key[i : i + 1, :], 1.0, 0.0),
                jnp.where(iota((slabs, LANES), 0) == recv_key[i : i + 1, :], 1.0, 0.0),
            ],
            axis=0,
        )
        before = jnp.dot(hot.astype(BF16), upper, preferred_element_type=F32)
        ranks = hot * (before + carry)
        spots.append(jnp.sum(ranks[:keys], axis=0, keepdims=True))
        sends.append(jnp.sum(ranks[keys : keys + slabs], axis=0, keepdims=True))
        recvs.append(jnp.sum(ranks[keys + slabs :], axis=0, keepdims=True))
        carry = carry + jnp.sum(hot, axis=1, keepdims=True)
    spot = jnp.concatenate(spots, axis=0).astype(jnp.int32)
    spot = jnp.where(valid, spot, -1)
    send = jnp.concatenate(sends, axis=0).astype(jnp.int32)
    recv = jnp.concatenate(recvs, axis=0).astype(jnp.int32)
    send_line = jnp.where(send_key >= 0, owner * pair_lines + (send >> 7), 200)
    recv_line = jnp.where(recv_key >= 0, home * pair_lines + (recv >> 7), -1)

    rf = rf_ref[...]
    cf = cf_ref[...]
    w = w_ref[...]
    rf_top = rf.astype(BF16).astype(F32)
    w_top = w.astype(BF16).astype(F32)
    values = [
        half.astype(F32),
        (c - half * HALF).astype(F32),
        (1.0 - cf).astype(BF16).astype(F32),
        cf.astype(BF16).astype(F32),
        rf_top,
        rf - rf_top,
        w_top,
        w - w_top,
        rel.astype(F32),
        send_line.astype(F32),
        (send & 127).astype(F32),
    ]
    total = jnp.zeros((FIELDS * chunks, LANES), F32)
    for i in range(0, lines, step):
        target = wide(spot, i)
        here = iota((chunks, step * LANES), 0) == (target >> 7)
        stack = jnp.concatenate([jnp.where(here, wide(v, i), 0.0) for v in values], axis=0).astype(BF16)
        place = jnp.where(iota((LANES, step * LANES), 0) == (target & 127), 1.0, 0.0).astype(BF16)
        total = total + nt_dot(stack, place)
    for f in range(FIELDS):
        plan_ref[f] = total[f * chunks : (f + 1) * chunks, :]

    slot_here = slot_of - me * owned
    received = slabs * pair_lines
    found = jnp.zeros((2 * received, LANES), F32)
    for i in range(0, lines, step):
        here = iota((received, step * LANES), 0) == wide(recv_line, i)
        target = wide(slot_here, i)
        stack = jnp.concatenate(
            [jnp.where(here, (target >> 7).astype(F32), 0.0), jnp.where(here, (target & 127).astype(F32), 0.0)], axis=0
        ).astype(BF16)
        place = jnp.where(iota((LANES, step * LANES), 0) == (wide(recv, i) & 127), 1.0, 0.0).astype(BF16)
        found = found + nt_dot(stack, place)
    places_ref[...] = (found[:received] * LANES + found[received:]).astype(jnp.int32)


def column_table(plan_ref, chunk, number):
    line = pl.ds(chunk, 1)
    column = plan_ref[0, line, :] * HALF + plan_ref[1, line, :] - (number * BLOCK).astype(F32)
    low = plan_ref[2, line, :].astype(BF16)
    high = plan_ref[3, line, :].astype(BF16)
    cells = iota((HALF, LANES), 0).astype(F32).astype(BF16)
    pieces = []
    for begin in range(0, BLOCK, HALF):
        near = jnp.clip(column - begin, -2.0, HALF).astype(BF16)
        after = jnp.clip(column - (begin - 1), -2.0, HALF).astype(BF16)
        pieces.append(jnp.where(cells == near, low, jnp.where(cells == after, high, jnp.zeros((), BF16))))
    return jnp.concatenate(pieces, axis=0)


def row_pattern(plan_ref, chunk, rows, depth):
    line = pl.ds(chunk, 1)
    rf = plan_ref[4, line, :] + plan_ref[5, line, :]
    rel = plan_ref[8, line, :].astype(jnp.int32)
    row = iota((depth, LANES), 0) % rows + 1
    return jnp.where(row == rel, 1.0 - rf, jnp.where(row == rel + 1, rf, 0.0))


def group_chunks(marks_ref, group, keys_group, base):
    count = (marks_ref[1, (group + 1) * keys_group - 1, 0] - base + LANES - 1) // LANES
    return jnp.maximum(count, 1)


def chunk_range(marks_ref, group, number, keys_group, cap_chunks):
    at = group * keys_group + 2 * number
    begin = marks_ref[0, jnp.maximum(at - 1, group * keys_group), 0]
    end = marks_ref[1, at + 1, 0]
    base = group * cap_chunks
    last = base + group_chunks(marks_ref, group, keys_group, base * LANES) - 1
    return jnp.minimum(begin // LANES, last), jnp.where(end > begin, (end + LANES - 1) // LANES, 0)


def forward_kernel(cap_chunks, blocks, field_ref, plan_ref, marks_ref, value_ref, sums):
    probes, rows, _ = field_ref.shape
    depth = probes * rows
    keys_group = 2 * blocks
    number = pl.program_id(0)
    counts = [group_chunks(marks_ref, g, keys_group, g * cap_chunks * LANES) for g in range(3)]

    @pl.when(number == 0)
    def _():
        for g in range(3):

            @pl.loop(0, counts[g])
            def _(k):
                sums[g * cap_chunks + k] = jnp.zeros((depth, LANES), F32)

    flat = field_ref[...].astype(F32).reshape(depth, BLOCK).astype(BF16)
    ranges = [chunk_range(marks_ref, g, number, keys_group, cap_chunks) for g in range(3)]
    table = jnp.concatenate([column_table(plan_ref, begin, number) for begin, _ in ranges], axis=1)
    part = jnp.dot(flat, table, preferred_element_type=F32)
    for g in range(3):
        sums[ranges[g][0]] += part[:, g * LANES : (g + 1) * LANES]
    for g in range(3):

        @pl.loop(ranges[g][0] + 1, ranges[g][1])
        def _(chunk):
            again = field_ref[...].astype(F32).reshape(depth, BLOCK).astype(BF16)
            sums[chunk] += jnp.dot(again, column_table(plan_ref, chunk, number), preferred_element_type=F32)

    @pl.when(number == blocks - 1)
    def _():
        fold = jnp.where(iota((probes, depth), 1) // rows == iota((probes, depth), 0), 1.0, 0.0).astype(BF16)
        for g in range(3):

            @pl.loop(0, counts[g])
            def _(k):
                chunk = g * cap_chunks + k
                scaled = (sums[chunk] * row_pattern(plan_ref, chunk, rows, depth)).astype(BF16)
                value_ref[chunk] = jnp.dot(fold, scaled, preferred_element_type=F32)


def swap_kernel(slabs, top, value_ref, above_ref, below_ref, send_sem, recv_sem):
    probe, me = lax.axis_index("probe"), lax.axis_index("slab")
    width = above_ref.shape[0]
    down, up = lax.rem(me + slabs - 1, slabs), lax.rem(me + 1, slabs)
    barrier = pltpu.get_barrier_semaphore()
    for peer in (down, up):
        pl.semaphore_signal(barrier, inc=1, device_id=(peer, probe), device_id_type=pl.DeviceIdType.MESH)
    pl.semaphore_wait(barrier, 2)
    copies = []
    for k, (peer, begin, target) in enumerate(((down, 0, above_ref), (up, top, below_ref))):
        copies.append(
            pltpu.make_async_remote_copy(
                src_ref=value_ref.at[begin : begin + width],
                dst_ref=target,
                send_sem=send_sem.at[k],
                recv_sem=recv_sem.at[k],
                device_id=(peer, probe),
                device_id_type=pl.DeviceIdType.MESH,
            )
        )
    for copy in copies:
        copy.start()
    for copy in copies:
        copy.wait()


def swap(slabs, cap_chunks, width, number, value):
    part = (width, *value.shape[1:])
    any_space = pl.BlockSpec(memory_space=pl.ANY)
    above, below = pl.pallas_call(
        functools.partial(swap_kernel, slabs, 2 * cap_chunks),
        out_shape=(jax.ShapeDtypeStruct(part, F32), jax.ShapeDtypeStruct(part, F32)),
        in_specs=[any_space],
        out_specs=(any_space, any_space),
        scratch_shapes=[pltpu.SemaphoreType.DMA((2,)), pltpu.SemaphoreType.DMA((2,))],
        compiler_params=pltpu.CompilerParams(collective_id=number, has_side_effects=True),
        name="swap",
    )(value)
    return above, below


def merge_kernel(cap_chunks, blocks, value_ref, above_ref, below_ref, plan_ref, marks_ref, spread_ref, packed_ref, squares, parts):
    slabs = packed_ref.shape[0]
    outgoing, probes, _ = parts.shape
    lines = outgoing // slabs
    keys_group = 2 * blocks
    squares[...] = jnp.zeros_like(squares)
    parts[...] = jnp.zeros_like(parts)
    for g in range(3):
        count = group_chunks(marks_ref, g, keys_group, g * cap_chunks * LANES)

        @pl.loop(0, count)
        def _(k):
            chunk = g * cap_chunks + k
            value = value_ref[chunk]
            if g == 0:
                value = value + below_ref[k]
            if g == 2:
                value = value + above_ref[k]
            line = pl.ds(chunk, 1)
            spread = value * (plan_ref[6, line, :] + plan_ref[7, line, :])
            spread_ref[chunk] = spread.astype(BF16)
            if g > 0:
                squares[...] += spread * value
                high = plan_ref[9, line, :].astype(jnp.int32)
                low = plan_ref[10, line, :].astype(jnp.int32)
                place = jnp.where(iota((LANES, LANES), 0) == low, 1.0, 0.0).astype(BF16)
                stack = jnp.concatenate([jnp.where(high == d, value, 0.0) for d in range(outgoing)], axis=0).astype(BF16)
                parts[...] += nt_dot(stack, place).reshape(outgoing, probes, LANES)

    folded = squares[:8, :]
    for d in range(8, probes, 8):
        folded = folded + squares[d : d + 8, :]
    for d in range(slabs):
        for e in range(lines):
            packed_ref[d, e * probes : (e + 1) * probes, :] = parts[d * lines + e]
        packed_ref[d, lines * probes :, :] = folded


def unpack_kernel(groups, scale, packed_ref, places_ref, observed_ref, mean_ref, traces, send_sem, recv_sem):
    slab, me = lax.axis_index("slab"), lax.axis_index("probe")
    slabs = packed_ref.shape[0]
    probes, owned = observed_ref.shape
    lines = places_ref.shape[0] // slabs
    barrier = pltpu.get_barrier_semaphore()
    for k in range(1, groups):
        peer = lax.rem(me + k, groups)
        pl.semaphore_signal(barrier, inc=1, device_id=(slab, peer), device_id_type=pl.DeviceIdType.MESH)
    own = packed_ref[0, lines * probes :, :]
    for d in range(1, slabs):
        own = own + packed_ref[d, lines * probes :, :]
    traces[me] = own
    pl.semaphore_wait(barrier, groups - 1)

    def tile(k, source, peer):
        return pltpu.make_async_remote_copy(
            src_ref=traces.at[me],
            dst_ref=traces.at[source],
            send_sem=send_sem.at[k],
            recv_sem=recv_sem.at[k],
            device_id=(slab, peer),
            device_id_type=pl.DeviceIdType.MESH,
        )

    for k in range(1, groups):
        tile(k, me, lax.rem(me + k, groups)).start()
    total = jnp.zeros((probes, owned), F32)
    for d in range(slabs):
        for e in range(lines):
            at = d * lines + e
            place = jnp.where(iota((owned, LANES), 0) == places_ref[at : at + 1, :], 1.0, 0.0).astype(BF16)
            total = total + nt_dot(packed_ref[d, e * probes : (e + 1) * probes, :].astype(BF16), place)
    observed_ref[...] = total
    for k in range(1, groups):
        source = lax.rem(me + groups - k, groups)
        tile(k, source, source).wait()
    summed = jnp.sum(jnp.sum(traces[...], axis=0), axis=0, keepdims=True)
    mean_ref[...] = jnp.broadcast_to(jnp.sum(summed, axis=1, keepdims=True) * scale, mean_ref.shape)


def adjoint_kernel(cap_chunks, blocks, spread_ref, plan_ref, marks_ref, out_ref, sources, total):
    probes, rows, _ = out_ref.shape
    depth = probes * rows
    keys_group = 2 * blocks
    number = pl.program_id(0)

    @pl.when(number == 0)
    def _():
        raise_rows = jnp.where(iota((depth, probes), 0) // rows == iota((depth, probes), 1), 1.0, 0.0).astype(BF16)
        for g in range(3):
            count = group_chunks(marks_ref, g, keys_group, g * cap_chunks * LANES)

            @pl.loop(0, count)
            def _(k):
                chunk = g * cap_chunks + k
                raised = jnp.dot(raise_rows, spread_ref[chunk], preferred_element_type=F32)
                sources[chunk] = (raised * row_pattern(plan_ref, chunk, rows, depth)).astype(BF16)

    ranges = [chunk_range(marks_ref, g, number, keys_group, cap_chunks) for g in range(3)]
    table = jnp.concatenate([column_table(plan_ref, begin, number) for begin, _ in ranges], axis=1)
    source = jnp.concatenate([sources[begin] for begin, _ in ranges], axis=1)
    total[...] = nt_dot(source, table)
    for g in range(3):

        @pl.loop(ranges[g][0] + 1, ranges[g][1])
        def _(chunk):
            total[...] += nt_dot(sources[chunk], column_table(plan_ref, chunk, number))

    out_ref[...] = total[...].reshape(probes, rows, BLOCK).astype(BF16)


def body(slab_count, probe_groups, probe_fields, sensor_rows, sensor_cols, row_frac, col_frac, sensor_weights, owner_order):
    probes, rows, width = probe_fields.shape
    sensors = sensor_rows.shape[0]
    depth = probes * rows
    lines = sensors // LANES
    blocks = width // BLOCK
    keys = 6 * blocks
    most = min(sensors, 4 * sensors // slab_count)
    cap_chunks = -(-most // (8 * LANES)) * 8
    chunks = 3 * cap_chunks
    pair_lines = -(-most // (slab_count * LANES))
    outgoing = slab_count * pair_lines
    me = jnp.reshape(lax.axis_index("slab"), (1,)).astype(jnp.int32)
    boxed = [x.reshape(lines, LANES) for x in (sensor_rows, sensor_cols, row_frac, col_frac, sensor_weights, owner_order)]
    vmem = pl.BlockSpec(memory_space=VMEM)
    smem = pl.BlockSpec(memory_space=SMEM)
    plan, marks, places, peak = pl.pallas_call(
        functools.partial(plan_kernel, rows, cap_chunks, blocks, slab_count, pair_lines),
        out_shape=(
            jax.ShapeDtypeStruct((FIELDS, chunks, LANES), F32),
            jax.ShapeDtypeStruct((2, keys, LANES), jnp.int32),
            jax.ShapeDtypeStruct((outgoing, LANES), jnp.int32),
            jax.ShapeDtypeStruct((8, LANES), jnp.int32),
        ),
        in_specs=[smem] + [vmem] * 6,
        out_specs=(vmem, vmem, vmem, vmem),
        compiler_params=LIMIT,
        name="plan",
    )(me, *boxed)
    value = pl.pallas_call(
        functools.partial(forward_kernel, cap_chunks, blocks),
        out_shape=jax.ShapeDtypeStruct((chunks, probes, LANES), F32),
        grid=(blocks,),
        in_specs=[pl.BlockSpec((probes, rows, BLOCK), lambda n: (0, 0, n)), vmem, smem],
        out_specs=vmem,
        scratch_shapes=[VMEM((chunks, depth, LANES), F32)],
        compiler_params=LIMIT,
        name="forward",
    )(probe_fields, plan, marks)
    few = min(cap_chunks, -(-5 * most // (4 * rows * LANES)))

    def merged(above, below):
        return pl.pallas_call(
            functools.partial(merge_kernel, cap_chunks, blocks),
            out_shape=(
                jax.ShapeDtypeStruct((chunks, probes, LANES), BF16),
                jax.ShapeDtypeStruct((slab_count, pair_lines * probes + 8, LANES), F32),
            ),
            in_specs=[vmem, vmem, vmem, vmem, smem],
            out_specs=(vmem, vmem),
            scratch_shapes=[VMEM((probes, LANES), F32), VMEM((outgoing, probes, LANES), F32)],
            compiler_params=LIMIT,
            name="merge",
        )(value, above, below, plan, marks)

    spread, packed = lax.cond(
        peak[0, 0] <= few * LANES,
        lambda: merged(*swap(slab_count, cap_chunks, few, 0, value)),
        lambda: merged(*swap(slab_count, cap_chunks, cap_chunks, 1, value)),
    )
    arrived = lax.all_to_all(packed, "slab", 0, 0, tiled=True)
    adjoint = pl.pallas_call(
        functools.partial(adjoint_kernel, cap_chunks, blocks),
        out_shape=jax.ShapeDtypeStruct((probes, rows, width), BF16),
        grid=(blocks,),
        in_specs=[vmem, vmem, smem],
        out_specs=pl.BlockSpec((probes, rows, BLOCK), lambda n: (0, 0, n)),
        scratch_shapes=[
            VMEM((chunks, depth, LANES), BF16),
            VMEM((depth, BLOCK), F32),
        ],
        compiler_params=LIMIT,
        cost_estimate=pl.CostEstimate(flops=4 * 10**9, bytes_accessed=8 * 10**6, transcendentals=0),
        name="adjoint",
    )(spread, plan, marks)
    observed, mean = pl.pallas_call(
        functools.partial(unpack_kernel, probe_groups, 1.0 / (probes * probe_groups * sensors)),
        out_shape=(
            jax.ShapeDtypeStruct((probes, sensors // slab_count), F32),
            jax.ShapeDtypeStruct((1, LANES), F32),
        ),
        in_specs=[vmem, vmem],
        out_specs=(vmem, vmem),
        scratch_shapes=[
            VMEM((probe_groups, 8, LANES), F32),
            pltpu.SemaphoreType.DMA((probe_groups,)),
            pltpu.SemaphoreType.DMA((probe_groups,)),
        ],
        compiler_params=pltpu.CompilerParams(collective_id=2, has_side_effects=True, vmem_limit_bytes=40 * 1024 * 1024),
        name="unpack",
    )(arrived, places)
    return adjoint, observed, mean[0, 0]


def solution(mesh):
    placed = (P("probe", "slab", None), P(), P(), P(), P(), P(), P())
    return jax.shard_map(
        functools.partial(body, mesh.shape["slab"], mesh.shape["probe"]),
        mesh=mesh,
        in_specs=placed,
        out_specs=(P("probe", "slab", None), P("probe", "slab"), P()),
        check_vma=False,
    )
```

```python
import functools

import jax
import jax.numpy as jnp
from jax import lax
from jax.experimental import pallas as pl
from jax.experimental.pallas import tpu as pltpu
from jax.sharding import PartitionSpec as P

LANES = 128
BLOCK = 512
HALF = 256
FIELDS = 11
F32 = jnp.float32
BF16 = jnp.bfloat16
NT = (((1,), (1,)), ((), ()))
VMEM = pltpu.VMEM
SMEM = pltpu.SMEM
LIMIT = pltpu.CompilerParams(vmem_limit_bytes=60 * 1024 * 1024)


def iota(shape, dim):
    return lax.broadcasted_iota(jnp.int32, shape, dim)


def nt_dot(a, b):
    return lax.dot_general(a, b, NT, preferred_element_type=F32)


def plan_kernel(rows, cap_chunks, blocks, slabs, pair_lines, me_ref, r_ref, c_ref, rf_ref, cf_ref, w_ref, order_ref, plan_ref, marks_ref, places_ref, peak_ref):
    lines = r_ref.shape[0]
    sensors = lines * LANES
    step = min(4, lines)
    me = me_ref[0]
    first = me * rows
    owned = lines * LANES // slabs
    keys_group = 2 * blocks
    keys = 3 * keys_group
    chunks = 3 * cap_chunks

    def wide(x, i):
        return jnp.concatenate([x[i + j : i + j + 1, :] for j in range(step)], axis=1)

    order = order_ref[...]
    slot = iota((lines, LANES), 0) * LANES + iota((lines, LANES), 1)
    found = jnp.zeros((2 * lines, LANES), F32)
    for i in range(0, lines, step):
        target = wide(order, i)
        mine = wide(slot, i)
        here = iota((lines, step * LANES), 0) == (target >> 7)
        stack = jnp.concatenate(
            [jnp.where(here, (mine >> 7).astype(F32), 0.0), jnp.where(here, (mine & 127).astype(F32), 0.0)], axis=0
        ).astype(BF16)
        place = jnp.where(iota((LANES, step * LANES), 0) == (target & 127), 1.0, 0.0).astype(BF16)
        found = found + nt_dot(stack, place)
    slot_hi = found[:lines, :]
    slot_lo = found[lines:, :]

    r = r_ref[...]
    c = c_ref[...]
    rel = r - first + 1
    valid = (rel >= 0) & (rel <= rows)
    group = jnp.where(rel == 0, 0, jnp.where(rel == rows, 2, 1))
    block = c // BLOCK
    inner = c - block * BLOCK
    half = c // HALF
    slot_of = (slot_hi * LANES + slot_lo).astype(jnp.int32)
    owner = slot_of // owned
    home = r // rows
    send_key = jnp.where(home == me, owner, -1)
    recv_key = jnp.where(owner == me, home, -1)
    edge = jnp.where(r - home * rows == rows - 1, home, -1)
    edges = jnp.zeros((slabs, LANES), F32)
    for i in range(lines):
        edges = edges + jnp.where(iota((slabs, LANES), 0) == edge[i : i + 1, :], 1.0, 0.0)
    peak = jnp.max(jnp.sum(edges, axis=1, keepdims=True), axis=0, keepdims=True)
    peak_ref[...] = jnp.broadcast_to(peak, (8, LANES)).astype(jnp.int32)
    key = group * keys_group + 2 * block + jnp.where(inner == BLOCK - 1, 1, 0)
    key = jnp.where(valid, key, -1)

    count = jnp.zeros((keys, 1), F32)
    for i in range(lines):
        count = count + jnp.sum(jnp.where(iota((keys, LANES), 0) == key[i : i + 1, :], 1.0, 0.0), axis=1, keepdims=True)
    big = jnp.floor(count * (1.0 / 64.0))
    small = count - 64.0 * big
    ka, kb = iota((keys, keys), 0), iota((keys, keys), 1)
    below = jnp.where((kb < ka) & (kb // keys_group == ka // keys_group), 1.0, 0.0).astype(BF16)
    start = 64.0 * jnp.dot(below, jnp.broadcast_to(big, (keys, LANES)).astype(BF16), preferred_element_type=F32)
    start = start + jnp.dot(below, jnp.broadcast_to(small, (keys, LANES)).astype(BF16), preferred_element_type=F32)
    start = start + ((iota((keys, LANES), 0) // keys_group) * (cap_chunks * LANES)).astype(F32)
    wide_keys = marks_ref.shape[1]
    diagonal = iota((keys, wide_keys), 0) == iota((keys, wide_keys), 1)
    marks_ref[...] = jnp.concatenate(
        [jnp.sum(jnp.where(diagonal, x, 0.0), axis=0, keepdims=True) for x in (start[:, :1], start[:, :1] + count)], axis=0
    ).astype(jnp.int32)

    upper = jnp.where(iota((LANES, LANES), 0) < iota((LANES, LANES), 1), 1.0, 0.0).astype(BF16)
    carry = jnp.concatenate([start[:, :1], jnp.zeros((2 * slabs, 1), F32)], axis=0)
    spots, sends, recvs = [], [], []
    for i in range(lines):
        hot = jnp.concatenate(
            [
                jnp.where(iota((keys, LANES), 0) == key[i : i + 1, :], 1.0, 0.0),
                jnp.where(iota((slabs, LANES), 0) == send_key[i : i + 1, :], 1.0, 0.0),
                jnp.where(iota((slabs, LANES), 0) == recv_key[i : i + 1, :], 1.0, 0.0),
            ],
            axis=0,
        )
        before = jnp.dot(hot.astype(BF16), upper, preferred_element_type=F32)
        ranks = hot * (before + carry)
        spots.append(jnp.sum(ranks[:keys], axis=0, keepdims=True))
        sends.append(jnp.sum(ranks[keys : keys + slabs], axis=0, keepdims=True))
        recvs.append(jnp.sum(ranks[keys + slabs :], axis=0, keepdims=True))
        carry = carry + jnp.sum(hot, axis=1, keepdims=True)
    spot = jnp.concatenate(spots, axis=0).astype(jnp.int32)
    spot = jnp.where(valid, spot, -1)
    send = jnp.concatenate(sends, axis=0).astype(jnp.int32)
    recv = jnp.concatenate(recvs, axis=0).astype(jnp.int32)
    send_line = jnp.where(send_key >= 0, owner * pair_lines + (send >> 7), 200)
    recv_line = jnp.where(recv_key >= 0, home * pair_lines + (recv >> 7), -1)

    rf = rf_ref[...]
    cf = cf_ref[...]
    w = w_ref[...]
    rf_top = rf.astype(BF16).astype(F32)
    w_top = w.astype(BF16).astype(F32)
    values = [
        half.astype(F32),
        (c - half * HALF).astype(F32),
        (1.0 - cf).astype(BF16).astype(F32),
        cf.astype(BF16).astype(F32),
        rf_top,
        rf - rf_top,
        w_top,
        w - w_top,
        rel.astype(F32),
        send_line.astype(F32),
        (send & 127).astype(F32),
    ]
    total = jnp.zeros((FIELDS * chunks, LANES), F32)
    for i in range(0, lines, step):
        target = wide(spot, i)
        here = iota((chunks, step * LANES), 0) == (target >> 7)
        stack = jnp.concatenate([jnp.where(here, wide(v, i), 0.0) for v in values], axis=0).astype(BF16)
        place = jnp.where(iota((LANES, step * LANES), 0) == (target & 127), 1.0, 0.0).astype(BF16)
        total = total + nt_dot(stack, place)
    for f in range(FIELDS):
        plan_ref[f] = total[f * chunks : (f + 1) * chunks, :]

    slot_here = slot_of - me * owned
    received = slabs * pair_lines
    found = jnp.zeros((2 * received, LANES), F32)
    for i in range(0, lines, step):
        here = iota((received, step * LANES), 0) == wide(recv_line, i)
        target = wide(slot_here, i)
        stack = jnp.concatenate(
            [jnp.where(here, (target >> 7).astype(F32), 0.0), jnp.where(here, (target & 127).astype(F32), 0.0)], axis=0
        ).astype(BF16)
        place = jnp.where(iota((LANES, step * LANES), 0) == (wide(recv, i) & 127), 1.0, 0.0).astype(BF16)
        found = found + nt_dot(stack, place)
    places_ref[...] = (found[:received] * LANES + found[received:]).astype(jnp.int32)


def column_table(plan_ref, chunk, number):
    line = pl.ds(chunk, 1)
    column = plan_ref[0, line, :] * HALF + plan_ref[1, line, :] - (number * BLOCK).astype(F32)
    low = plan_ref[2, line, :].astype(BF16)
    high = plan_ref[3, line, :].astype(BF16)
    cells = iota((HALF, LANES), 0).astype(F32).astype(BF16)
    pieces = []
    for begin in range(0, BLOCK, HALF):
        near = jnp.clip(column - begin, -2.0, HALF).astype(BF16)
        after = jnp.clip(column - (begin - 1), -2.0, HALF).astype(BF16)
        pieces.append(jnp.where(cells == near, low, jnp.where(cells == after, high, jnp.zeros((), BF16))))
    return jnp.concatenate(pieces, axis=0)


def row_pattern(plan_ref, chunk, rows, depth):
    line = pl.ds(chunk, 1)
    rf = plan_ref[4, line, :] + plan_ref[5, line, :]
    rel = plan_ref[8, line, :].astype(jnp.int32)
    row = iota((depth, LANES), 0) % rows + 1
    return jnp.where(row == rel, 1.0 - rf, jnp.where(row == rel + 1, rf, 0.0))


def group_chunks(marks_ref, group, keys_group, base):
    count = (marks_ref[1, (group + 1) * keys_group - 1] - base + LANES - 1) // LANES
    return jnp.maximum(count, 1)


def chunk_range(marks_ref, group, number, keys_group, cap_chunks):
    at = group * keys_group + 2 * number
    begin = marks_ref[0, jnp.maximum(at - 1, group * keys_group)]
    end = marks_ref[1, at + 1]
    base = group * cap_chunks
    last = base + group_chunks(marks_ref, group, keys_group, base * LANES) - 1
    return jnp.minimum(begin // LANES, last), jnp.where(end > begin, (end + LANES - 1) // LANES, 0)


def forward_kernel(cap_chunks, blocks, field_ref, plan_ref, marks_ref, value_ref, sums):
    probes, rows, _ = field_ref.shape
    depth = probes * rows
    keys_group = 2 * blocks
    number = pl.program_id(0)
    counts = [group_chunks(marks_ref, g, keys_group, g * cap_chunks * LANES) for g in range(3)]

    @pl.when(number == 0)
    def _():
        for g in range(3):

            @pl.loop(0, counts[g])
            def _(k):
                sums[g * cap_chunks + k] = jnp.zeros((depth, LANES), F32)

    flat = field_ref[...].reshape(depth, BLOCK)
    ranges = [chunk_range(marks_ref, g, number, keys_group, cap_chunks) for g in range(3)]
    table = jnp.concatenate([column_table(plan_ref, begin, number) for begin, _ in ranges], axis=1)
    part = jnp.dot(flat, table, preferred_element_type=F32)
    for g in range(3):
        sums[ranges[g][0]] += part[:, g * LANES : (g + 1) * LANES]
    for g in range(3):

        @pl.loop(ranges[g][0] + 1, ranges[g][1])
        def _(chunk):
            again = field_ref[...].reshape(depth, BLOCK)
            sums[chunk] += jnp.dot(again, column_table(plan_ref, chunk, number), preferred_element_type=F32)

    @pl.when(number == blocks - 1)
    def _():
        fold = jnp.where(iota((probes, depth), 1) // rows == iota((probes, depth), 0), 1.0, 0.0).astype(BF16)
        for g in range(3):

            @pl.loop(0, counts[g])
            def _(k):
                chunk = g * cap_chunks + k
                scaled = (sums[chunk] * row_pattern(plan_ref, chunk, rows, depth)).astype(BF16)
                value_ref[chunk] = jnp.dot(fold, scaled, preferred_element_type=F32)


def swap_kernel(slabs, top, value_ref, above_ref, below_ref, send_sem, recv_sem):
    probe, me = lax.axis_index("probe"), lax.axis_index("slab")
    width = above_ref.shape[0]
    down, up = lax.rem(me + slabs - 1, slabs), lax.rem(me + 1, slabs)
    barrier = pltpu.get_barrier_semaphore()
    for peer in (down, up):
        pl.semaphore_signal(barrier, inc=1, device_id=(peer, probe), device_id_type=pl.DeviceIdType.MESH)
    pl.semaphore_wait(barrier, 2)
    copies = []
    for k, (peer, begin, target) in enumerate(((down, 0, above_ref), (up, top, below_ref))):
        copies.append(
            pltpu.make_async_remote_copy(
                src_ref=value_ref.at[begin : begin + width],
                dst_ref=target,
                send_sem=send_sem.at[k],
                recv_sem=recv_sem.at[k],
                device_id=(peer, probe),
                device_id_type=pl.DeviceIdType.MESH,
            )
        )
    for copy in copies:
        copy.start()
    for copy in copies:
        copy.wait()


def swap(slabs, cap_chunks, width, number, value):
    part = (width, *value.shape[1:])
    any_space = pl.BlockSpec(memory_space=pl.ANY)
    above, below = pl.pallas_call(
        functools.partial(swap_kernel, slabs, 2 * cap_chunks),
        out_shape=(jax.ShapeDtypeStruct(part, F32), jax.ShapeDtypeStruct(part, F32)),
        in_specs=[any_space],
        out_specs=(any_space, any_space),
        scratch_shapes=[pltpu.SemaphoreType.DMA((2,)), pltpu.SemaphoreType.DMA((2,))],
        compiler_params=pltpu.CompilerParams(collective_id=number, has_side_effects=True),
        name="swap",
    )(value)
    return above, below


def merge_kernel(cap_chunks, blocks, value_ref, above_ref, below_ref, plan_ref, marks_ref, spread_ref, packed_ref, squares, parts):
    slabs = packed_ref.shape[0]
    outgoing, probes, _ = parts.shape
    lines = outgoing // slabs
    keys_group = 2 * blocks
    squares[...] = jnp.zeros_like(squares)
    parts[...] = jnp.zeros_like(parts)
    for g in range(3):
        count = group_chunks(marks_ref, g, keys_group, g * cap_chunks * LANES)

        @pl.loop(0, count)
        def _(k):
            chunk = g * cap_chunks + k
            value = value_ref[chunk]
            if g == 0:
                value = value + below_ref[k]
            if g == 2:
                value = value + above_ref[k]
            line = pl.ds(chunk, 1)
            spread = value * (plan_ref[6, line, :] + plan_ref[7, line, :])
            spread_ref[chunk] = spread.astype(BF16)
            if g > 0:
                squares[...] += spread * value
                high = plan_ref[9, line, :].astype(jnp.int32)
                low = plan_ref[10, line, :].astype(jnp.int32)
                place = jnp.where(iota((LANES, LANES), 0) == low, 1.0, 0.0).astype(BF16)
                stack = jnp.concatenate([jnp.where(high == d, value, 0.0) for d in range(outgoing)], axis=0).astype(BF16)
                parts[...] += nt_dot(stack, place).reshape(outgoing, probes, LANES)

    folded = squares[:8, :]
    for d in range(8, probes, 8):
        folded = folded + squares[d : d + 8, :]
    for d in range(slabs):
        for e in range(lines):
            packed_ref[d, e * probes : (e + 1) * probes, :] = parts[d * lines + e]
        packed_ref[d, lines * probes :, :] = folded


def unpack_kernel(groups, scale, packed_ref, places_ref, observed_ref, mean_ref, traces, send_sem, recv_sem):
    slab, me = lax.axis_index("slab"), lax.axis_index("probe")
    slabs = packed_ref.shape[0]
    probes, owned = observed_ref.shape
    lines = places_ref.shape[0] // slabs
    barrier = pltpu.get_barrier_semaphore()
    for k in range(1, groups):
        peer = lax.rem(me + k, groups)
        pl.semaphore_signal(barrier, inc=1, device_id=(slab, peer), device_id_type=pl.DeviceIdType.MESH)
    own = packed_ref[0, lines * probes :, :]
    for d in range(1, slabs):
        own = own + packed_ref[d, lines * probes :, :]
    traces[me] = own
    pl.semaphore_wait(barrier, groups - 1)

    def tile(k, source, peer):
        return pltpu.make_async_remote_copy(
            src_ref=traces.at[me],
            dst_ref=traces.at[source],
            send_sem=send_sem.at[k],
            recv_sem=recv_sem.at[k],
            device_id=(slab, peer),
            device_id_type=pl.DeviceIdType.MESH,
        )

    for k in range(1, groups):
        tile(k, me, lax.rem(me + k, groups)).start()
    total = jnp.zeros((probes, owned), F32)
    for d in range(slabs):
        for e in range(lines):
            at = d * lines + e
            place = jnp.where(iota((owned, LANES), 0) == places_ref[at : at + 1, :], 1.0, 0.0).astype(BF16)
            total = total + nt_dot(packed_ref[d, e * probes : (e + 1) * probes, :].astype(BF16), place)
    observed_ref[...] = total
    for k in range(1, groups):
        source = lax.rem(me + groups - k, groups)
        tile(k, source, source).wait()
    summed = jnp.sum(jnp.sum(traces[...], axis=0), axis=0, keepdims=True)
    mean_ref[...] = jnp.broadcast_to(jnp.sum(summed, axis=1, keepdims=True) * scale, mean_ref.shape)


def adjoint_kernel(cap_chunks, blocks, spread_ref, plan_ref, marks_ref, out_ref, sources, total):
    probes, rows, _ = out_ref.shape
    depth = probes * rows
    keys_group = 2 * blocks
    number = pl.program_id(0)

    @pl.when(number == 0)
    def _():
        raise_rows = jnp.where(iota((depth, probes), 0) // rows == iota((depth, probes), 1), 1.0, 0.0).astype(BF16)
        for g in range(3):
            count = group_chunks(marks_ref, g, keys_group, g * cap_chunks * LANES)

            @pl.loop(0, count)
            def _(k):
                chunk = g * cap_chunks + k
                raised = jnp.dot(raise_rows, spread_ref[chunk], preferred_element_type=F32)
                sources[chunk] = (raised * row_pattern(plan_ref, chunk, rows, depth)).astype(BF16)

    ranges = [chunk_range(marks_ref, g, number, keys_group, cap_chunks) for g in range(3)]
    table = jnp.concatenate([column_table(plan_ref, begin, number) for begin, _ in ranges], axis=1)
    source = jnp.concatenate([sources[begin] for begin, _ in ranges], axis=1)
    total[...] = nt_dot(source, table)
    for g in range(3):

        @pl.loop(ranges[g][0] + 1, ranges[g][1])
        def _(chunk):
            total[...] += nt_dot(sources[chunk], column_table(plan_ref, chunk, number))

    out_ref[...] = total[...].astype(BF16).reshape(probes, rows, BLOCK)


def body(slab_count, probe_groups, probe_fields, sensor_rows, sensor_cols, row_frac, col_frac, sensor_weights, owner_order):
    probes, rows, width = probe_fields.shape
    sensors = sensor_rows.shape[0]
    depth = probes * rows
    lines = sensors // LANES
    blocks = width // BLOCK
    keys = 6 * blocks
    most = min(sensors, 4 * sensors // slab_count)
    cap_chunks = -(-most // (8 * LANES)) * 8
    chunks = 3 * cap_chunks
    pair_lines = -(-most // (slab_count * LANES))
    outgoing = slab_count * pair_lines
    me = jnp.reshape(lax.axis_index("slab"), (1,)).astype(jnp.int32)
    boxed = [x.reshape(lines, LANES) for x in (sensor_rows, sensor_cols, row_frac, col_frac, sensor_weights, owner_order)]
    vmem = pl.BlockSpec(memory_space=VMEM)
    smem = pl.BlockSpec(memory_space=SMEM)
    plan, marks, places, peak = pl.pallas_call(
        functools.partial(plan_kernel, rows, cap_chunks, blocks, slab_count, pair_lines),
        out_shape=(
            jax.ShapeDtypeStruct((FIELDS, chunks, LANES), F32),
            jax.ShapeDtypeStruct((2, -(-keys // LANES) * LANES), jnp.int32),
            jax.ShapeDtypeStruct((outgoing, LANES), jnp.int32),
            jax.ShapeDtypeStruct((8, LANES), jnp.int32),
        ),
        in_specs=[smem] + [vmem] * 6,
        out_specs=(vmem, vmem, vmem, vmem),
        compiler_params=LIMIT,
        name="plan",
    )(me, *boxed)
    value = pl.pallas_call(
        functools.partial(forward_kernel, cap_chunks, blocks),
        out_shape=jax.ShapeDtypeStruct((chunks, probes, LANES), F32),
        grid=(blocks,),
        in_specs=[pl.BlockSpec((probes, rows, BLOCK), lambda n: (0, 0, n)), vmem, smem],
        out_specs=vmem,
        scratch_shapes=[VMEM((chunks, depth, LANES), F32)],
        compiler_params=LIMIT,
        name="forward",
    )(probe_fields, plan, marks)
    few = min(cap_chunks, -(-5 * most // (4 * rows * LANES)))

    def merged(above, below):
        return pl.pallas_call(
            functools.partial(merge_kernel, cap_chunks, blocks),
            out_shape=(
                jax.ShapeDtypeStruct((chunks, probes, LANES), BF16),
                jax.ShapeDtypeStruct((slab_count, pair_lines * probes + 8, LANES), F32),
            ),
            in_specs=[vmem, vmem, vmem, vmem, smem],
            out_specs=(vmem, vmem),
            scratch_shapes=[VMEM((probes, LANES), F32), VMEM((outgoing, probes, LANES), F32)],
            compiler_params=LIMIT,
            name="merge",
        )(value, above, below, plan, marks)

    spread, packed = lax.cond(
        peak[0, 0] <= few * LANES,
        lambda: merged(*swap(slab_count, cap_chunks, few, 0, value)),
        lambda: merged(*swap(slab_count, cap_chunks, cap_chunks, 1, value)),
    )
    arrived = lax.all_to_all(packed, "slab", 0, 0, tiled=True)
    adjoint = pl.pallas_call(
        functools.partial(adjoint_kernel, cap_chunks, blocks),
        out_shape=jax.ShapeDtypeStruct((probes, rows, width), BF16),
        grid=(blocks,),
        in_specs=[vmem, vmem, smem],
        out_specs=pl.BlockSpec((probes, rows, BLOCK), lambda n: (0, 0, n)),
        scratch_shapes=[
            VMEM((chunks, depth, LANES), BF16),
            VMEM((depth, BLOCK), F32),
        ],
        compiler_params=LIMIT,
        cost_estimate=pl.CostEstimate(flops=4 * 10**9, bytes_accessed=8 * 10**6, transcendentals=0),
        name="adjoint",
    )(spread, plan, marks)
    observed, mean = pl.pallas_call(
        functools.partial(unpack_kernel, probe_groups, 1.0 / (probes * probe_groups * sensors)),
        out_shape=(
            jax.ShapeDtypeStruct((probes, sensors // slab_count), F32),
            jax.ShapeDtypeStruct((1, LANES), F32),
        ),
        in_specs=[vmem, vmem],
        out_specs=(vmem, vmem),
        scratch_shapes=[
            VMEM((probe_groups, 8, LANES), F32),
            pltpu.SemaphoreType.DMA((probe_groups,)),
            pltpu.SemaphoreType.DMA((probe_groups,)),
        ],
        compiler_params=pltpu.CompilerParams(collective_id=2, has_side_effects=True, vmem_limit_bytes=40 * 1024 * 1024),
        name="unpack",
    )(arrived, places)
    return adjoint, observed, mean[0, 0]


def solution(mesh):
    placed = (P("probe", "slab", None), P(), P(), P(), P(), P(), P())
    return jax.shard_map(
        functools.partial(body, mesh.shape["slab"], mesh.shape["probe"]),
        mesh=mesh,
        in_specs=placed,
        out_specs=(P("probe", "slab", None), P("probe", "slab"), P()),
        check_vma=False,
    )
```

```python
import functools

import jax
import jax.numpy as jnp
from jax import lax
from jax.experimental import pallas as pl
from jax.experimental.pallas import tpu as pltpu
from jax.sharding import PartitionSpec as P

LANES = 128
BLOCK = 512
HALF = 256
FIELDS = 11
F32 = jnp.float32
BF16 = jnp.bfloat16
NT = (((1,), (1,)), ((), ()))
VMEM = pltpu.VMEM
SMEM = pltpu.SMEM
LIMIT = pltpu.CompilerParams(vmem_limit_bytes=60 * 1024 * 1024)


def iota(shape, dim):
    return lax.broadcasted_iota(jnp.int32, shape, dim)


def nt_dot(a, b):
    return lax.dot_general(a, b, NT, preferred_element_type=F32)


def plan_kernel(rows, cap_chunks, blocks, slabs, pair_lines, me_ref, r_ref, c_ref, rf_ref, cf_ref, w_ref, order_ref, plan_ref, marks_ref, places_ref, peak_ref):
    lines = r_ref.shape[0]
    sensors = lines * LANES
    step = min(4, lines)
    me = me_ref[0]
    first = me * rows
    owned = lines * LANES // slabs
    keys_group = 2 * blocks
    keys = 3 * keys_group
    chunks = 3 * cap_chunks

    def wide(x, i):
        return jnp.concatenate([x[i + j : i + j + 1, :] for j in range(step)], axis=1)

    order = order_ref[...]
    slot = iota((lines, LANES), 0) * LANES + iota((lines, LANES), 1)
    found = jnp.zeros((2 * lines, LANES), F32)
    for i in range(0, lines, step):
        target = wide(order, i)
        mine = wide(slot, i)
        here = iota((lines, step * LANES), 0) == (target >> 7)
        stack = jnp.concatenate(
            [jnp.where(here, (mine >> 7).astype(F32), 0.0), jnp.where(here, (mine & 127).astype(F32), 0.0)], axis=0
        ).astype(BF16)
        place = jnp.where(iota((LANES, step * LANES), 0) == (target & 127), 1.0, 0.0).astype(BF16)
        found = found + nt_dot(stack, place)
    slot_hi = found[:lines, :]
    slot_lo = found[lines:, :]

    r = r_ref[...]
    c = c_ref[...]
    rel = r - first + 1
    valid = (rel >= 0) & (rel <= rows)
    group = jnp.where(rel == 0, 0, jnp.where(rel == rows, 2, 1))
    block = c // BLOCK
    inner = c - block * BLOCK
    half = c // HALF
    slot_of = (slot_hi * LANES + slot_lo).astype(jnp.int32)
    owner = slot_of // owned
    home = r // rows
    send_key = jnp.where(home == me, owner, -1)
    recv_key = jnp.where(owner == me, home, -1)
    edge = jnp.where(r - home * rows == rows - 1, home, -1)
    edges = jnp.zeros((slabs, LANES), F32)
    for i in range(lines):
        edges = edges + jnp.where(iota((slabs, LANES), 0) == edge[i : i + 1, :], 1.0, 0.0)
    peak = jnp.max(jnp.sum(edges, axis=1, keepdims=True), axis=0, keepdims=True)
    peak_ref[...] = jnp.broadcast_to(peak, (8, LANES)).astype(jnp.int32)
    key = group * keys_group + 2 * block + jnp.where(inner == BLOCK - 1, 1, 0)
    key = jnp.where(valid, key, -1)

    count = jnp.zeros((keys, 1), F32)
    for i in range(lines):
        count = count + jnp.sum(jnp.where(iota((keys, LANES), 0) == key[i : i + 1, :], 1.0, 0.0), axis=1, keepdims=True)
    big = jnp.floor(count * (1.0 / 64.0))
    small = count - 64.0 * big
    ka, kb = iota((keys, keys), 0), iota((keys, keys), 1)
    below = jnp.where((kb < ka) & (kb // keys_group == ka // keys_group), 1.0, 0.0).astype(BF16)
    start = 64.0 * jnp.dot(below, jnp.broadcast_to(big, (keys, LANES)).astype(BF16), preferred_element_type=F32)
    start = start + jnp.dot(below, jnp.broadcast_to(small, (keys, LANES)).astype(BF16), preferred_element_type=F32)
    start = start + ((iota((keys, LANES), 0) // keys_group) * (cap_chunks * LANES)).astype(F32)
    wide_keys = marks_ref.shape[1]
    diagonal = iota((keys, wide_keys), 0) == iota((keys, wide_keys), 1)
    marks_ref[...] = jnp.concatenate(
        [jnp.sum(jnp.where(diagonal, x, 0.0), axis=0, keepdims=True) for x in (start[:, :1], start[:, :1] + count)], axis=0
    ).astype(jnp.int32)

    upper = jnp.where(iota((LANES, LANES), 0) < iota((LANES, LANES), 1), 1.0, 0.0).astype(BF16)
    carry = jnp.concatenate([start[:, :1], jnp.zeros((2 * slabs, 1), F32)], axis=0)
    spots, sends, recvs = [], [], []
    for i in range(lines):
        hot = jnp.concatenate(
            [
                jnp.where(iota((keys, LANES), 0) == key[i : i + 1, :], 1.0, 0.0),
                jnp.where(iota((slabs, LANES), 0) == send_key[i : i + 1, :], 1.0, 0.0),
                jnp.where(iota((slabs, LANES), 0) == recv_key[i : i + 1, :], 1.0, 0.0),
            ],
            axis=0,
        )
        before = jnp.dot(hot.astype(BF16), upper, preferred_element_type=F32)
        ranks = hot * (before + carry)
        spots.append(jnp.sum(ranks[:keys], axis=0, keepdims=True))
        sends.append(jnp.sum(ranks[keys : keys + slabs], axis=0, keepdims=True))
        recvs.append(jnp.sum(ranks[keys + slabs :], axis=0, keepdims=True))
        carry = carry + jnp.sum(hot, axis=1, keepdims=True)
    spot = jnp.concatenate(spots, axis=0).astype(jnp.int32)
    spot = jnp.where(valid, spot, -1)
    send = jnp.concatenate(sends, axis=0).astype(jnp.int32)
    recv = jnp.concatenate(recvs, axis=0).astype(jnp.int32)
    send_line = jnp.where(send_key >= 0, owner * pair_lines + (send >> 7), 200)
    recv_line = jnp.where(recv_key >= 0, home * pair_lines + (recv >> 7), -1)

    rf = rf_ref[...]
    cf = cf_ref[...]
    w = w_ref[...]
    rf_top = rf.astype(BF16).astype(F32)
    w_top = w.astype(BF16).astype(F32)
    values = [
        half.astype(F32),
        (c - half * HALF).astype(F32),
        (1.0 - cf).astype(BF16).astype(F32),
        cf.astype(BF16).astype(F32),
        rf_top,
        rf - rf_top,
        w_top,
        w - w_top,
        rel.astype(F32),
        send_line.astype(F32),
        (send & 127).astype(F32),
    ]
    total = jnp.zeros((FIELDS * chunks, LANES), F32)
    for i in range(0, lines, step):
        target = wide(spot, i)
        here = iota((chunks, step * LANES), 0) == (target >> 7)
        stack = jnp.concatenate([jnp.where(here, wide(v, i), 0.0) for v in values], axis=0).astype(BF16)
        place = jnp.where(iota((LANES, step * LANES), 0) == (target & 127), 1.0, 0.0).astype(BF16)
        total = total + nt_dot(stack, place)
    for f in range(FIELDS):
        plan_ref[f] = total[f * chunks : (f + 1) * chunks, :]

    slot_here = slot_of - me * owned
    received = slabs * pair_lines
    found = jnp.zeros((2 * received, LANES), F32)
    for i in range(0, lines, step):
        here = iota((received, step * LANES), 0) == wide(recv_line, i)
        target = wide(slot_here, i)
        stack = jnp.concatenate(
            [jnp.where(here, (target >> 7).astype(F32), 0.0), jnp.where(here, (target & 127).astype(F32), 0.0)], axis=0
        ).astype(BF16)
        place = jnp.where(iota((LANES, step * LANES), 0) == (wide(recv, i) & 127), 1.0, 0.0).astype(BF16)
        found = found + nt_dot(stack, place)
    places_ref[...] = (found[:received] * LANES + found[received:]).astype(jnp.int32)


def column_table(plan_ref, chunk, number):
    line = pl.ds(chunk, 1)
    column = plan_ref[0, line, :] * HALF + plan_ref[1, line, :] - (number * BLOCK).astype(F32)
    low = plan_ref[2, line, :].astype(BF16)
    high = plan_ref[3, line, :].astype(BF16)
    cells = iota((HALF, LANES), 0).astype(F32).astype(BF16)
    pieces = []
    for begin in range(0, BLOCK, HALF):
        near = jnp.clip(column - begin, -2.0, HALF).astype(BF16)
        after = jnp.clip(column - (begin - 1), -2.0, HALF).astype(BF16)
        pieces.append(jnp.where(cells == near, low, jnp.where(cells == after, high, jnp.zeros((), BF16))))
    return jnp.concatenate(pieces, axis=0)


def row_pattern(plan_ref, chunk, rows, depth):
    line = pl.ds(chunk, 1)
    rf = plan_ref[4, line, :] + plan_ref[5, line, :]
    rel = plan_ref[8, line, :].astype(jnp.int32)
    row = iota((depth, LANES), 0) % rows + 1
    return jnp.where(row == rel, 1.0 - rf, jnp.where(row == rel + 1, rf, 0.0))


def group_chunks(marks_ref, group, keys_group, base):
    count = (marks_ref[1, (group + 1) * keys_group - 1] - base + LANES - 1) // LANES
    return jnp.maximum(count, 1)


def chunk_range(marks_ref, group, number, keys_group, cap_chunks):
    at = group * keys_group + 2 * number
    begin = marks_ref[0, jnp.maximum(at - 1, group * keys_group)]
    end = marks_ref[1, at + 1]
    base = group * cap_chunks
    last = base + group_chunks(marks_ref, group, keys_group, base * LANES) - 1
    return jnp.minimum(begin // LANES, last), jnp.where(end > begin, (end + LANES - 1) // LANES, 0)


def forward_kernel(cap_chunks, blocks, field_ref, plan_ref, marks_ref, value_ref, sums, flat):
    probes, rows, _ = field_ref.shape
    depth = probes * rows
    keys_group = 2 * blocks
    number = pl.program_id(0)
    counts = [group_chunks(marks_ref, g, keys_group, g * cap_chunks * LANES) for g in range(3)]

    @pl.when(number == 0)
    def _():
        for g in range(3):

            @pl.loop(0, counts[g])
            def _(k):
                sums[g * cap_chunks + k] = jnp.zeros((depth, LANES), F32)

    block = field_ref[...].reshape(depth, BLOCK)
    flat[...] = block
    ranges = [chunk_range(marks_ref, g, number, keys_group, cap_chunks) for g in range(3)]
    table = jnp.concatenate([column_table(plan_ref, begin, number) for begin, _ in ranges], axis=1)
    part = jnp.dot(block, table, preferred_element_type=F32)
    for g in range(3):
        sums[ranges[g][0]] += part[:, g * LANES : (g + 1) * LANES]
    for g in range(3):

        @pl.loop(ranges[g][0] + 1, ranges[g][1])
        def _(chunk):
            sums[chunk] += jnp.dot(flat[...], column_table(plan_ref, chunk, number), preferred_element_type=F32)

    @pl.when(number == blocks - 1)
    def _():
        fold = jnp.where(iota((probes, depth), 1) // rows == iota((probes, depth), 0), 1.0, 0.0).astype(BF16)
        for g in range(3):

            @pl.loop(0, counts[g])
            def _(k):
                chunk = g * cap_chunks + k
                scaled = (sums[chunk] * row_pattern(plan_ref, chunk, rows, depth)).astype(BF16)
                value_ref[chunk] = jnp.dot(fold, scaled, preferred_element_type=F32)


def swap_kernel(slabs, top, value_ref, above_ref, below_ref, send_sem, recv_sem):
    probe, me = lax.axis_index("probe"), lax.axis_index("slab")
    width = above_ref.shape[0]
    down, up = lax.rem(me + slabs - 1, slabs), lax.rem(me + 1, slabs)
    barrier = pltpu.get_barrier_semaphore()
    for peer in (down, up):
        pl.semaphore_signal(barrier, inc=1, device_id=(peer, probe), device_id_type=pl.DeviceIdType.MESH)
    pl.semaphore_wait(barrier, 2)
    copies = []
    for k, (peer, begin, target) in enumerate(((down, 0, above_ref), (up, top, below_ref))):
        copies.append(
            pltpu.make_async_remote_copy(
                src_ref=value_ref.at[begin : begin + width],
                dst_ref=target,
                send_sem=send_sem.at[k],
                recv_sem=recv_sem.at[k],
                device_id=(peer, probe),
                device_id_type=pl.DeviceIdType.MESH,
            )
        )
    for copy in copies:
        copy.start()
    for copy in copies:
        copy.wait()


def swap(slabs, cap_chunks, width, number, value):
    part = (width, *value.shape[1:])
    any_space = pl.BlockSpec(memory_space=pl.ANY)
    above, below = pl.pallas_call(
        functools.partial(swap_kernel, slabs, 2 * cap_chunks),
        out_shape=(jax.ShapeDtypeStruct(part, F32), jax.ShapeDtypeStruct(part, F32)),
        in_specs=[any_space],
        out_specs=(any_space, any_space),
        scratch_shapes=[pltpu.SemaphoreType.DMA((2,)), pltpu.SemaphoreType.DMA((2,))],
        compiler_params=pltpu.CompilerParams(collective_id=number, has_side_effects=True),
        name="swap",
    )(value)
    return above, below


def merge_kernel(cap_chunks, blocks, value_ref, above_ref, below_ref, plan_ref, marks_ref, spread_ref, packed_ref, squares, parts):
    slabs = packed_ref.shape[0]
    outgoing, probes, _ = parts.shape
    lines = outgoing // slabs
    keys_group = 2 * blocks
    squares[...] = jnp.zeros_like(squares)
    parts[...] = jnp.zeros_like(parts)
    for g in range(3):
        count = group_chunks(marks_ref, g, keys_group, g * cap_chunks * LANES)

        @pl.loop(0, count)
        def _(k):
            chunk = g * cap_chunks + k
            value = value_ref[chunk]
            if g == 0:
                value = value + below_ref[k]
            if g == 2:
                value = value + above_ref[k]
            line = pl.ds(chunk, 1)
            spread = value * (plan_ref[6, line, :] + plan_ref[7, line, :])
            spread_ref[chunk] = spread.astype(BF16)
            if g > 0:
                squares[...] += spread * value
                high = plan_ref[9, line, :].astype(jnp.int32)
                low = plan_ref[10, line, :].astype(jnp.int32)
                place = jnp.where(iota((LANES, LANES), 0) == low, 1.0, 0.0).astype(BF16)
                stack = jnp.concatenate([jnp.where(high == d, value, 0.0) for d in range(outgoing)], axis=0).astype(BF16)
                parts[...] += nt_dot(stack, place).reshape(outgoing, probes, LANES)

    folded = squares[:8, :]
    for d in range(8, probes, 8):
        folded = folded + squares[d : d + 8, :]
    for d in range(slabs):
        for e in range(lines):
            packed_ref[d, e * probes : (e + 1) * probes, :] = parts[d * lines + e]
        packed_ref[d, lines * probes :, :] = folded


def unpack_kernel(groups, scale, packed_ref, places_ref, observed_ref, mean_ref, traces, send_sem, recv_sem):
    slab, me = lax.axis_index("slab"), lax.axis_index("probe")
    slabs = packed_ref.shape[0]
    probes, owned = observed_ref.shape
    lines = places_ref.shape[0] // slabs
    barrier = pltpu.get_barrier_semaphore()
    for k in range(1, groups):
        peer = lax.rem(me + k, groups)
        pl.semaphore_signal(barrier, inc=1, device_id=(slab, peer), device_id_type=pl.DeviceIdType.MESH)
    own = packed_ref[0, lines * probes :, :]
    for d in range(1, slabs):
        own = own + packed_ref[d, lines * probes :, :]
    traces[me] = own
    pl.semaphore_wait(barrier, groups - 1)

    def tile(k, source, peer):
        return pltpu.make_async_remote_copy(
            src_ref=traces.at[me],
            dst_ref=traces.at[source],
            send_sem=send_sem.at[k],
            recv_sem=recv_sem.at[k],
            device_id=(slab, peer),
            device_id_type=pl.DeviceIdType.MESH,
        )

    for k in range(1, groups):
        tile(k, me, lax.rem(me + k, groups)).start()
    total = jnp.zeros((probes, owned), F32)
    for d in range(slabs):
        for e in range(lines):
            at = d * lines + e
            place = jnp.where(iota((owned, LANES), 0) == places_ref[at : at + 1, :], 1.0, 0.0).astype(BF16)
            total = total + nt_dot(packed_ref[d, e * probes : (e + 1) * probes, :].astype(BF16), place)
    observed_ref[...] = total
    for k in range(1, groups):
        source = lax.rem(me + groups - k, groups)
        tile(k, source, source).wait()
    summed = jnp.sum(jnp.sum(traces[...], axis=0), axis=0, keepdims=True)
    mean_ref[...] = jnp.broadcast_to(jnp.sum(summed, axis=1, keepdims=True) * scale, mean_ref.shape)


def adjoint_kernel(cap_chunks, blocks, spread_ref, plan_ref, marks_ref, out_ref, sources, total):
    probes, rows, _ = out_ref.shape
    depth = probes * rows
    keys_group = 2 * blocks
    number = pl.program_id(0)

    @pl.when(number == 0)
    def _():
        raise_rows = jnp.where(iota((depth, probes), 0) // rows == iota((depth, probes), 1), 1.0, 0.0).astype(BF16)
        for g in range(3):
            count = group_chunks(marks_ref, g, keys_group, g * cap_chunks * LANES)

            @pl.loop(0, count)
            def _(k):
                chunk = g * cap_chunks + k
                raised = jnp.dot(raise_rows, spread_ref[chunk], preferred_element_type=F32)
                sources[chunk] = (raised * row_pattern(plan_ref, chunk, rows, depth)).astype(BF16)

    ranges = [chunk_range(marks_ref, g, number, keys_group, cap_chunks) for g in range(3)]
    table = jnp.concatenate([column_table(plan_ref, begin, number) for begin, _ in ranges], axis=1)
    source = jnp.concatenate([sources[begin] for begin, _ in ranges], axis=1)
    total[...] = nt_dot(source, table)
    for g in range(3):

        @pl.loop(ranges[g][0] + 1, ranges[g][1])
        def _(chunk):
            total[...] += nt_dot(sources[chunk], column_table(plan_ref, chunk, number))

    out_ref[...] = total[...].astype(BF16).reshape(probes, rows, BLOCK)


def body(slab_count, probe_groups, probe_fields, sensor_rows, sensor_cols, row_frac, col_frac, sensor_weights, owner_order):
    probes, rows, width = probe_fields.shape
    sensors = sensor_rows.shape[0]
    depth = probes * rows
    lines = sensors // LANES
    blocks = width // BLOCK
    keys = 6 * blocks
    most = min(sensors, 4 * sensors // slab_count)
    cap_chunks = -(-most // (8 * LANES)) * 8
    chunks = 3 * cap_chunks
    pair_lines = -(-most // (slab_count * LANES))
    outgoing = slab_count * pair_lines
    me = jnp.reshape(lax.axis_index("slab"), (1,)).astype(jnp.int32)
    boxed = [x.reshape(lines, LANES) for x in (sensor_rows, sensor_cols, row_frac, col_frac, sensor_weights, owner_order)]
    vmem = pl.BlockSpec(memory_space=VMEM)
    smem = pl.BlockSpec(memory_space=SMEM)
    plan, marks, places, peak = pl.pallas_call(
        functools.partial(plan_kernel, rows, cap_chunks, blocks, slab_count, pair_lines),
        out_shape=(
            jax.ShapeDtypeStruct((FIELDS, chunks, LANES), F32),
            jax.ShapeDtypeStruct((2, -(-keys // LANES) * LANES), jnp.int32),
            jax.ShapeDtypeStruct((outgoing, LANES), jnp.int32),
            jax.ShapeDtypeStruct((8, LANES), jnp.int32),
        ),
        in_specs=[smem] + [vmem] * 6,
        out_specs=(vmem, vmem, vmem, vmem),
        compiler_params=LIMIT,
        name="plan",
    )(me, *boxed)
    value = pl.pallas_call(
        functools.partial(forward_kernel, cap_chunks, blocks),
        out_shape=jax.ShapeDtypeStruct((chunks, probes, LANES), F32),
        grid=(blocks,),
        in_specs=[pl.BlockSpec((probes, rows, BLOCK), lambda n: (0, 0, n)), vmem, smem],
        out_specs=vmem,
        scratch_shapes=[VMEM((chunks, depth, LANES), F32), VMEM((depth, BLOCK), BF16)],
        compiler_params=LIMIT,
        name="forward",
    )(probe_fields, plan, marks)
    few = min(cap_chunks, -(-5 * most // (4 * rows * LANES)))

    def merged(above, below):
        return pl.pallas_call(
            functools.partial(merge_kernel, cap_chunks, blocks),
            out_shape=(
                jax.ShapeDtypeStruct((chunks, probes, LANES), BF16),
                jax.ShapeDtypeStruct((slab_count, pair_lines * probes + 8, LANES), F32),
            ),
            in_specs=[vmem, vmem, vmem, vmem, smem],
            out_specs=(vmem, vmem),
            scratch_shapes=[VMEM((probes, LANES), F32), VMEM((outgoing, probes, LANES), F32)],
            compiler_params=LIMIT,
            name="merge",
        )(value, above, below, plan, marks)

    spread, packed = lax.cond(
        peak[0, 0] <= few * LANES,
        lambda: merged(*swap(slab_count, cap_chunks, few, 0, value)),
        lambda: merged(*swap(slab_count, cap_chunks, cap_chunks, 1, value)),
    )
    arrived = lax.all_to_all(packed, "slab", 0, 0, tiled=True)
    adjoint = pl.pallas_call(
        functools.partial(adjoint_kernel, cap_chunks, blocks),
        out_shape=jax.ShapeDtypeStruct((probes, rows, width), BF16),
        grid=(blocks,),
        in_specs=[vmem, vmem, smem],
        out_specs=pl.BlockSpec((probes, rows, BLOCK), lambda n: (0, 0, n)),
        scratch_shapes=[
            VMEM((chunks, depth, LANES), BF16),
            VMEM((depth, BLOCK), F32),
        ],
        compiler_params=LIMIT,
        cost_estimate=pl.CostEstimate(flops=4 * 10**9, bytes_accessed=8 * 10**6, transcendentals=0),
        name="adjoint",
    )(spread, plan, marks)
    observed, mean = pl.pallas_call(
        functools.partial(unpack_kernel, probe_groups, 1.0 / (probes * probe_groups * sensors)),
        out_shape=(
            jax.ShapeDtypeStruct((probes, sensors // slab_count), F32),
            jax.ShapeDtypeStruct((1, LANES), F32),
        ),
        in_specs=[vmem, vmem],
        out_specs=(vmem, vmem),
        scratch_shapes=[
            VMEM((probe_groups, 8, LANES), F32),
            pltpu.SemaphoreType.DMA((probe_groups,)),
            pltpu.SemaphoreType.DMA((probe_groups,)),
        ],
        compiler_params=pltpu.CompilerParams(collective_id=2, has_side_effects=True, vmem_limit_bytes=40 * 1024 * 1024),
        name="unpack",
    )(arrived, places)
    return adjoint, observed, mean[0, 0]


def solution(mesh):
    placed = (P("probe", "slab", None), P(), P(), P(), P(), P(), P())
    return jax.shard_map(
        functools.partial(body, mesh.shape["slab"], mesh.shape["probe"]),
        mesh=mesh,
        in_specs=placed,
        out_specs=(P("probe", "slab", None), P("probe", "slab"), P()),
        check_vma=False,
    )
```

```python
import functools

import jax
import jax.numpy as jnp
from jax import lax
from jax.experimental import pallas as pl
from jax.experimental.pallas import tpu as pltpu
from jax.sharding import PartitionSpec as P

LANES = 128
BLOCK = 1024
HALF = 256
FIELDS = 11
F32 = jnp.float32
BF16 = jnp.bfloat16
NT = (((1,), (1,)), ((), ()))
VMEM = pltpu.VMEM
SMEM = pltpu.SMEM
LIMIT = pltpu.CompilerParams(vmem_limit_bytes=60 * 1024 * 1024)


def iota(shape, dim):
    return lax.broadcasted_iota(jnp.int32, shape, dim)


def nt_dot(a, b):
    return lax.dot_general(a, b, NT, preferred_element_type=F32)


def plan_kernel(rows, cap_chunks, blocks, slabs, pair_lines, me_ref, r_ref, c_ref, rf_ref, cf_ref, w_ref, order_ref, plan_ref, marks_ref, places_ref, peak_ref):
    lines = r_ref.shape[0]
    sensors = lines * LANES
    step = min(4, lines)
    me = me_ref[0]
    first = me * rows
    owned = lines * LANES // slabs
    keys_group = 2 * blocks
    keys = 3 * keys_group
    chunks = 3 * cap_chunks

    def wide(x, i):
        return jnp.concatenate([x[i + j : i + j + 1, :] for j in range(step)], axis=1)

    order = order_ref[...]
    slot = iota((lines, LANES), 0) * LANES + iota((lines, LANES), 1)
    found = jnp.zeros((2 * lines, LANES), F32)
    for i in range(0, lines, step):
        target = wide(order, i)
        mine = wide(slot, i)
        here = iota((lines, step * LANES), 0) == (target >> 7)
        stack = jnp.concatenate(
            [jnp.where(here, (mine >> 7).astype(F32), 0.0), jnp.where(here, (mine & 127).astype(F32), 0.0)], axis=0
        ).astype(BF16)
        place = jnp.where(iota((LANES, step * LANES), 0) == (target & 127), 1.0, 0.0).astype(BF16)
        found = found + nt_dot(stack, place)
    slot_hi = found[:lines, :]
    slot_lo = found[lines:, :]

    r = r_ref[...]
    c = c_ref[...]
    rel = r - first + 1
    valid = (rel >= 0) & (rel <= rows)
    group = jnp.where(rel == 0, 0, jnp.where(rel == rows, 2, 1))
    block = c // BLOCK
    inner = c - block * BLOCK
    half = c // HALF
    slot_of = (slot_hi * LANES + slot_lo).astype(jnp.int32)
    owner = slot_of // owned
    home = r // rows
    send_key = jnp.where(home == me, owner, -1)
    recv_key = jnp.where(owner == me, home, -1)
    edge = jnp.where(r - home * rows == rows - 1, home, -1)
    edges = jnp.zeros((slabs, LANES), F32)
    for i in range(lines):
        edges = edges + jnp.where(iota((slabs, LANES), 0) == edge[i : i + 1, :], 1.0, 0.0)
    peak = jnp.max(jnp.sum(edges, axis=1, keepdims=True), axis=0, keepdims=True)
    peak_ref[...] = jnp.broadcast_to(peak, (8, LANES)).astype(jnp.int32)
    key = group * keys_group + 2 * block + jnp.where(inner == BLOCK - 1, 1, 0)
    key = jnp.where(valid, key, -1)

    count = jnp.zeros((keys, 1), F32)
    for i in range(lines):
        count = count + jnp.sum(jnp.where(iota((keys, LANES), 0) == key[i : i + 1, :], 1.0, 0.0), axis=1, keepdims=True)
    big = jnp.floor(count * (1.0 / 64.0))
    small = count - 64.0 * big
    ka, kb = iota((keys, keys), 0), iota((keys, keys), 1)
    below = jnp.where((kb < ka) & (kb // keys_group == ka // keys_group), 1.0, 0.0).astype(BF16)
    start = 64.0 * jnp.dot(below, jnp.broadcast_to(big, (keys, LANES)).astype(BF16), preferred_element_type=F32)
    start = start + jnp.dot(below, jnp.broadcast_to(small, (keys, LANES)).astype(BF16), preferred_element_type=F32)
    start = start + ((iota((keys, LANES), 0) // keys_group) * (cap_chunks * LANES)).astype(F32)
    wide_keys = marks_ref.shape[1]
    diagonal = iota((keys, wide_keys), 0) == iota((keys, wide_keys), 1)
    marks_ref[...] = jnp.concatenate(
        [jnp.sum(jnp.where(diagonal, x, 0.0), axis=0, keepdims=True) for x in (start[:, :1], start[:, :1] + count)], axis=0
    ).astype(jnp.int32)

    upper = jnp.where(iota((LANES, LANES), 0) < iota((LANES, LANES), 1), 1.0, 0.0).astype(BF16)
    carry = jnp.concatenate([start[:, :1], jnp.zeros((2 * slabs, 1), F32)], axis=0)
    spots, sends, recvs = [], [], []
    for i in range(lines):
        hot = jnp.concatenate(
            [
                jnp.where(iota((keys, LANES), 0) == key[i : i + 1, :], 1.0, 0.0),
                jnp.where(iota((slabs, LANES), 0) == send_key[i : i + 1, :], 1.0, 0.0),
                jnp.where(iota((slabs, LANES), 0) == recv_key[i : i + 1, :], 1.0, 0.0),
            ],
            axis=0,
        )
        before = jnp.dot(hot.astype(BF16), upper, preferred_element_type=F32)
        ranks = hot * (before + carry)
        spots.append(jnp.sum(ranks[:keys], axis=0, keepdims=True))
        sends.append(jnp.sum(ranks[keys : keys + slabs], axis=0, keepdims=True))
        recvs.append(jnp.sum(ranks[keys + slabs :], axis=0, keepdims=True))
        carry = carry + jnp.sum(hot, axis=1, keepdims=True)
    spot = jnp.concatenate(spots, axis=0).astype(jnp.int32)
    spot = jnp.where(valid, spot, -1)
    send = jnp.concatenate(sends, axis=0).astype(jnp.int32)
    recv = jnp.concatenate(recvs, axis=0).astype(jnp.int32)
    send_line = jnp.where(send_key >= 0, owner * pair_lines + (send >> 7), 200)
    recv_line = jnp.where(recv_key >= 0, home * pair_lines + (recv >> 7), -1)

    rf = rf_ref[...]
    cf = cf_ref[...]
    w = w_ref[...]
    rf_top = rf.astype(BF16).astype(F32)
    w_top = w.astype(BF16).astype(F32)
    values = [
        half.astype(F32),
        (c - half * HALF).astype(F32),
        (1.0 - cf).astype(BF16).astype(F32),
        cf.astype(BF16).astype(F32),
        rf_top,
        rf - rf_top,
        w_top,
        w - w_top,
        rel.astype(F32),
        send_line.astype(F32),
        (send & 127).astype(F32),
    ]
    total = jnp.zeros((FIELDS * chunks, LANES), F32)
    for i in range(0, lines, step):
        target = wide(spot, i)
        here = iota((chunks, step * LANES), 0) == (target >> 7)
        stack = jnp.concatenate([jnp.where(here, wide(v, i), 0.0) for v in values], axis=0).astype(BF16)
        place = jnp.where(iota((LANES, step * LANES), 0) == (target & 127), 1.0, 0.0).astype(BF16)
        total = total + nt_dot(stack, place)
    for f in range(FIELDS):
        plan_ref[f] = total[f * chunks : (f + 1) * chunks, :]

    slot_here = slot_of - me * owned
    received = slabs * pair_lines
    found = jnp.zeros((2 * received, LANES), F32)
    for i in range(0, lines, step):
        here = iota((received, step * LANES), 0) == wide(recv_line, i)
        target = wide(slot_here, i)
        stack = jnp.concatenate(
            [jnp.where(here, (target >> 7).astype(F32), 0.0), jnp.where(here, (target & 127).astype(F32), 0.0)], axis=0
        ).astype(BF16)
        place = jnp.where(iota((LANES, step * LANES), 0) == (wide(recv, i) & 127), 1.0, 0.0).astype(BF16)
        found = found + nt_dot(stack, place)
    places_ref[...] = (found[:received] * LANES + found[received:]).astype(jnp.int32)


def column_table(plan_ref, chunk, number):
    line = pl.ds(chunk, 1)
    column = plan_ref[0, line, :] * HALF + plan_ref[1, line, :] - (number * BLOCK).astype(F32)
    low = plan_ref[2, line, :].astype(BF16)
    high = plan_ref[3, line, :].astype(BF16)
    cells = iota((HALF, LANES), 0).astype(F32).astype(BF16)
    pieces = []
    for begin in range(0, BLOCK, HALF):
        near = jnp.clip(column - begin, -2.0, HALF).astype(BF16)
        after = jnp.clip(column - (begin - 1), -2.0, HALF).astype(BF16)
        pieces.append(jnp.where(cells == near, low, jnp.where(cells == after, high, jnp.zeros((), BF16))))
    return jnp.concatenate(pieces, axis=0)


def row_pattern(plan_ref, chunk, rows, depth):
    line = pl.ds(chunk, 1)
    rf = plan_ref[4, line, :] + plan_ref[5, line, :]
    rel = plan_ref[8, line, :].astype(jnp.int32)
    row = iota((depth, LANES), 0) % rows + 1
    return jnp.where(row == rel, 1.0 - rf, jnp.where(row == rel + 1, rf, 0.0))


def group_chunks(marks_ref, group, keys_group, base):
    count = (marks_ref[1, (group + 1) * keys_group - 1] - base + LANES - 1) // LANES
    return jnp.maximum(count, 1)


def chunk_range(marks_ref, group, number, keys_group, cap_chunks):
    at = group * keys_group + 2 * number
    begin = marks_ref[0, jnp.maximum(at - 1, group * keys_group)]
    end = marks_ref[1, at + 1]
    base = group * cap_chunks
    last = base + group_chunks(marks_ref, group, keys_group, base * LANES) - 1
    return jnp.minimum(begin // LANES, last), jnp.where(end > begin, (end + LANES - 1) // LANES, 0)


def forward_kernel(cap_chunks, blocks, field_ref, plan_ref, marks_ref, value_ref, sums, flat):
    probes, rows, _ = field_ref.shape
    depth = probes * rows
    keys_group = 2 * blocks
    number = pl.program_id(0)
    counts = [group_chunks(marks_ref, g, keys_group, g * cap_chunks * LANES) for g in range(3)]

    @pl.when(number == 0)
    def _():
        for g in range(3):

            @pl.loop(0, counts[g])
            def _(k):
                sums[g * cap_chunks + k] = jnp.zeros((depth, LANES), F32)

    block = field_ref[...].reshape(depth, BLOCK)
    flat[...] = block
    ranges = [chunk_range(marks_ref, g, number, keys_group, cap_chunks) for g in range(3)]
    table = jnp.concatenate([column_table(plan_ref, begin, number) for begin, _ in ranges], axis=1)
    part = jnp.dot(block, table, preferred_element_type=F32)
    for g in range(3):
        sums[ranges[g][0]] += part[:, g * LANES : (g + 1) * LANES]
    for g in range(3):

        @pl.loop(ranges[g][0] + 1, ranges[g][1])
        def _(chunk):
            sums[chunk] += jnp.dot(flat[...], column_table(plan_ref, chunk, number), preferred_element_type=F32)

    @pl.when(number == blocks - 1)
    def _():
        fold = jnp.where(iota((probes, depth), 1) // rows == iota((probes, depth), 0), 1.0, 0.0).astype(BF16)
        for g in range(3):

            @pl.loop(0, counts[g])
            def _(k):
                chunk = g * cap_chunks + k
                scaled = (sums[chunk] * row_pattern(plan_ref, chunk, rows, depth)).astype(BF16)
                value_ref[chunk] = jnp.dot(fold, scaled, preferred_element_type=F32)


def swap_kernel(slabs, top, value_ref, above_ref, below_ref, send_sem, recv_sem):
    probe, me = lax.axis_index("probe"), lax.axis_index("slab")
    width = above_ref.shape[0]
    down, up = lax.rem(me + slabs - 1, slabs), lax.rem(me + 1, slabs)
    barrier = pltpu.get_barrier_semaphore()
    for peer in (down, up):
        pl.semaphore_signal(barrier, inc=1, device_id=(peer, probe), device_id_type=pl.DeviceIdType.MESH)
    pl.semaphore_wait(barrier, 2)
    copies = []
    for k, (peer, begin, target) in enumerate(((down, 0, above_ref), (up, top, below_ref))):
        copies.append(
            pltpu.make_async_remote_copy(
                src_ref=value_ref.at[begin : begin + width],
                dst_ref=target,
                send_sem=send_sem.at[k],
                recv_sem=recv_sem.at[k],
                device_id=(peer, probe),
                device_id_type=pl.DeviceIdType.MESH,
            )
        )
    for copy in copies:
        copy.start()
    for copy in copies:
        copy.wait()


def swap(slabs, cap_chunks, width, number, value):
    part = (width, *value.shape[1:])
    any_space = pl.BlockSpec(memory_space=pl.ANY)
    above, below = pl.pallas_call(
        functools.partial(swap_kernel, slabs, 2 * cap_chunks),
        out_shape=(jax.ShapeDtypeStruct(part, F32), jax.ShapeDtypeStruct(part, F32)),
        in_specs=[any_space],
        out_specs=(any_space, any_space),
        scratch_shapes=[pltpu.SemaphoreType.DMA((2,)), pltpu.SemaphoreType.DMA((2,))],
        compiler_params=pltpu.CompilerParams(collective_id=number, has_side_effects=True),
        name="swap",
    )(value)
    return above, below


def merge_kernel(cap_chunks, blocks, value_ref, above_ref, below_ref, plan_ref, marks_ref, spread_ref, packed_ref, squares, parts):
    slabs = packed_ref.shape[0]
    outgoing, probes, _ = parts.shape
    lines = outgoing // slabs
    keys_group = 2 * blocks
    squares[...] = jnp.zeros_like(squares)
    parts[...] = jnp.zeros_like(parts)
    for g in range(3):
        count = group_chunks(marks_ref, g, keys_group, g * cap_chunks * LANES)

        @pl.loop(0, count)
        def _(k):
            chunk = g * cap_chunks + k
            value = value_ref[chunk]
            if g == 0:
                value = value + below_ref[k]
            if g == 2:
                value = value + above_ref[k]
            line = pl.ds(chunk, 1)
            spread = value * (plan_ref[6, line, :] + plan_ref[7, line, :])
            spread_ref[chunk] = spread.astype(BF16)
            if g > 0:
                squares[...] += spread * value
                high = plan_ref[9, line, :].astype(jnp.int32)
                low = plan_ref[10, line, :].astype(jnp.int32)
                place = jnp.where(iota((LANES, LANES), 0) == low, 1.0, 0.0).astype(BF16)
                stack = jnp.concatenate([jnp.where(high == d, value, 0.0) for d in range(outgoing)], axis=0).astype(BF16)
                parts[...] += nt_dot(stack, place).reshape(outgoing, probes, LANES)

    folded = squares[:8, :]
    for d in range(8, probes, 8):
        folded = folded + squares[d : d + 8, :]
    for d in range(slabs):
        for e in range(lines):
            packed_ref[d, e * probes : (e + 1) * probes, :] = parts[d * lines + e]
        packed_ref[d, lines * probes :, :] = folded


def unpack_kernel(groups, scale, packed_ref, places_ref, observed_ref, mean_ref, traces, send_sem, recv_sem):
    slab, me = lax.axis_index("slab"), lax.axis_index("probe")
    slabs = packed_ref.shape[0]
    probes, owned = observed_ref.shape
    lines = places_ref.shape[0] // slabs
    barrier = pltpu.get_barrier_semaphore()
    for k in range(1, groups):
        peer = lax.rem(me + k, groups)
        pl.semaphore_signal(barrier, inc=1, device_id=(slab, peer), device_id_type=pl.DeviceIdType.MESH)
    own = packed_ref[0, lines * probes :, :]
    for d in range(1, slabs):
        own = own + packed_ref[d, lines * probes :, :]
    traces[me] = own
    pl.semaphore_wait(barrier, groups - 1)

    def tile(k, source, peer):
        return pltpu.make_async_remote_copy(
            src_ref=traces.at[me],
            dst_ref=traces.at[source],
            send_sem=send_sem.at[k],
            recv_sem=recv_sem.at[k],
            device_id=(slab, peer),
            device_id_type=pl.DeviceIdType.MESH,
        )

    for k in range(1, groups):
        tile(k, me, lax.rem(me + k, groups)).start()
    total = jnp.zeros((probes, owned), F32)
    for d in range(slabs):
        for e in range(lines):
            at = d * lines + e
            place = jnp.where(iota((owned, LANES), 0) == places_ref[at : at + 1, :], 1.0, 0.0).astype(BF16)
            total = total + nt_dot(packed_ref[d, e * probes : (e + 1) * probes, :].astype(BF16), place)
    observed_ref[...] = total
    for k in range(1, groups):
        source = lax.rem(me + groups - k, groups)
        tile(k, source, source).wait()
    summed = jnp.sum(jnp.sum(traces[...], axis=0), axis=0, keepdims=True)
    mean_ref[...] = jnp.broadcast_to(jnp.sum(summed, axis=1, keepdims=True) * scale, mean_ref.shape)


def adjoint_kernel(cap_chunks, blocks, spread_ref, plan_ref, marks_ref, out_ref, sources, total):
    probes, rows, _ = out_ref.shape
    depth = probes * rows
    keys_group = 2 * blocks
    number = pl.program_id(0)

    @pl.when(number == 0)
    def _():
        raise_rows = jnp.where(iota((depth, probes), 0) // rows == iota((depth, probes), 1), 1.0, 0.0).astype(BF16)
        for g in range(3):
            count = group_chunks(marks_ref, g, keys_group, g * cap_chunks * LANES)

            @pl.loop(0, count)
            def _(k):
                chunk = g * cap_chunks + k
                raised = jnp.dot(raise_rows, spread_ref[chunk], preferred_element_type=F32)
                sources[chunk] = (raised * row_pattern(plan_ref, chunk, rows, depth)).astype(BF16)

    ranges = [chunk_range(marks_ref, g, number, keys_group, cap_chunks) for g in range(3)]
    table = jnp.concatenate([column_table(plan_ref, begin, number) for begin, _ in ranges], axis=1)
    source = jnp.concatenate([sources[begin] for begin, _ in ranges], axis=1)
    total[...] = nt_dot(source, table)
    for g in range(3):

        @pl.loop(ranges[g][0] + 1, ranges[g][1])
        def _(chunk):
            total[...] += nt_dot(sources[chunk], column_table(plan_ref, chunk, number))

    out_ref[...] = total[...].astype(BF16).reshape(probes, rows, BLOCK)


def body(slab_count, probe_groups, probe_fields, sensor_rows, sensor_cols, row_frac, col_frac, sensor_weights, owner_order):
    probes, rows, width = probe_fields.shape
    sensors = sensor_rows.shape[0]
    depth = probes * rows
    lines = sensors // LANES
    blocks = width // BLOCK
    keys = 6 * blocks
    most = min(sensors, 4 * sensors // slab_count)
    cap_chunks = -(-most // (8 * LANES)) * 8
    chunks = 3 * cap_chunks
    pair_lines = -(-most // (slab_count * LANES))
    outgoing = slab_count * pair_lines
    me = jnp.reshape(lax.axis_index("slab"), (1,)).astype(jnp.int32)
    boxed = [x.reshape(lines, LANES) for x in (sensor_rows, sensor_cols, row_frac, col_frac, sensor_weights, owner_order)]
    vmem = pl.BlockSpec(memory_space=VMEM)
    smem = pl.BlockSpec(memory_space=SMEM)
    plan, marks, places, peak = pl.pallas_call(
        functools.partial(plan_kernel, rows, cap_chunks, blocks, slab_count, pair_lines),
        out_shape=(
            jax.ShapeDtypeStruct((FIELDS, chunks, LANES), F32),
            jax.ShapeDtypeStruct((2, -(-keys // LANES) * LANES), jnp.int32),
            jax.ShapeDtypeStruct((outgoing, LANES), jnp.int32),
            jax.ShapeDtypeStruct((8, LANES), jnp.int32),
        ),
        in_specs=[smem] + [vmem] * 6,
        out_specs=(vmem, vmem, vmem, vmem),
        compiler_params=LIMIT,
        name="plan",
    )(me, *boxed)
    value = pl.pallas_call(
        functools.partial(forward_kernel, cap_chunks, blocks),
        out_shape=jax.ShapeDtypeStruct((chunks, probes, LANES), F32),
        grid=(blocks,),
        in_specs=[pl.BlockSpec((probes, rows, BLOCK), lambda n: (0, 0, n)), vmem, smem],
        out_specs=vmem,
        scratch_shapes=[VMEM((chunks, depth, LANES), F32), VMEM((depth, BLOCK), BF16)],
        compiler_params=LIMIT,
        name="forward",
    )(probe_fields, plan, marks)
    few = min(cap_chunks, -(-5 * most // (4 * rows * LANES)))

    def merged(above, below):
        return pl.pallas_call(
            functools.partial(merge_kernel, cap_chunks, blocks),
            out_shape=(
                jax.ShapeDtypeStruct((chunks, probes, LANES), BF16),
                jax.ShapeDtypeStruct((slab_count, pair_lines * probes + 8, LANES), F32),
            ),
            in_specs=[vmem, vmem, vmem, vmem, smem],
            out_specs=(vmem, vmem),
            scratch_shapes=[VMEM((probes, LANES), F32), VMEM((outgoing, probes, LANES), F32)],
            compiler_params=LIMIT,
            name="merge",
        )(value, above, below, plan, marks)

    spread, packed = lax.cond(
        peak[0, 0] <= few * LANES,
        lambda: merged(*swap(slab_count, cap_chunks, few, 0, value)),
        lambda: merged(*swap(slab_count, cap_chunks, cap_chunks, 1, value)),
    )
    arrived = lax.all_to_all(packed, "slab", 0, 0, tiled=True)
    adjoint = pl.pallas_call(
        functools.partial(adjoint_kernel, cap_chunks, blocks),
        out_shape=jax.ShapeDtypeStruct((probes, rows, width), BF16),
        grid=(blocks,),
        in_specs=[vmem, vmem, smem],
        out_specs=pl.BlockSpec((probes, rows, BLOCK), lambda n: (0, 0, n)),
        scratch_shapes=[
            VMEM((chunks, depth, LANES), BF16),
            VMEM((depth, BLOCK), F32),
        ],
        compiler_params=LIMIT,
        cost_estimate=pl.CostEstimate(flops=4 * 10**9, bytes_accessed=8 * 10**6, transcendentals=0),
        name="adjoint",
    )(spread, plan, marks)
    observed, mean = pl.pallas_call(
        functools.partial(unpack_kernel, probe_groups, 1.0 / (probes * probe_groups * sensors)),
        out_shape=(
            jax.ShapeDtypeStruct((probes, sensors // slab_count), F32),
            jax.ShapeDtypeStruct((1, LANES), F32),
        ),
        in_specs=[vmem, vmem],
        out_specs=(vmem, vmem),
        scratch_shapes=[
            VMEM((probe_groups, 8, LANES), F32),
            pltpu.SemaphoreType.DMA((probe_groups,)),
            pltpu.SemaphoreType.DMA((probe_groups,)),
        ],
        compiler_params=pltpu.CompilerParams(collective_id=2, has_side_effects=True, vmem_limit_bytes=40 * 1024 * 1024),
        name="unpack",
    )(arrived, places)
    return adjoint, observed, mean[0, 0]


def solution(mesh):
    placed = (P("probe", "slab", None), P(), P(), P(), P(), P(), P())
    return jax.shard_map(
        functools.partial(body, mesh.shape["slab"], mesh.shape["probe"]),
        mesh=mesh,
        in_specs=placed,
        out_specs=(P("probe", "slab", None), P("probe", "slab"), P()),
        check_vma=False,
    )
```

```python
import functools

import jax
import jax.numpy as jnp
from jax import lax
from jax.experimental import pallas as pl
from jax.experimental.pallas import tpu as pltpu
from jax.sharding import PartitionSpec as P

LANES = 128
BLOCK = 2048
HALF = 256
FIELDS = 11
F32 = jnp.float32
BF16 = jnp.bfloat16
NT = (((1,), (1,)), ((), ()))
VMEM = pltpu.VMEM
SMEM = pltpu.SMEM
LIMIT = pltpu.CompilerParams(vmem_limit_bytes=60 * 1024 * 1024)


def iota(shape, dim):
    return lax.broadcasted_iota(jnp.int32, shape, dim)


def nt_dot(a, b):
    return lax.dot_general(a, b, NT, preferred_element_type=F32)


def plan_kernel(rows, cap_chunks, blocks, slabs, pair_lines, me_ref, r_ref, c_ref, rf_ref, cf_ref, w_ref, order_ref, plan_ref, marks_ref, places_ref, peak_ref):
    lines = r_ref.shape[0]
    sensors = lines * LANES
    step = min(4, lines)
    me = me_ref[0]
    first = me * rows
    owned = lines * LANES // slabs
    keys_group = 2 * blocks
    keys = 3 * keys_group
    chunks = 3 * cap_chunks

    def wide(x, i):
        return jnp.concatenate([x[i + j : i + j + 1, :] for j in range(step)], axis=1)

    order = order_ref[...]
    slot = iota((lines, LANES), 0) * LANES + iota((lines, LANES), 1)
    found = jnp.zeros((2 * lines, LANES), F32)
    for i in range(0, lines, step):
        target = wide(order, i)
        mine = wide(slot, i)
        here = iota((lines, step * LANES), 0) == (target >> 7)
        stack = jnp.concatenate(
            [jnp.where(here, (mine >> 7).astype(F32), 0.0), jnp.where(here, (mine & 127).astype(F32), 0.0)], axis=0
        ).astype(BF16)
        place = jnp.where(iota((LANES, step * LANES), 0) == (target & 127), 1.0, 0.0).astype(BF16)
        found = found + nt_dot(stack, place)
    slot_hi = found[:lines, :]
    slot_lo = found[lines:, :]

    r = r_ref[...]
    c = c_ref[...]
    rel = r - first + 1
    valid = (rel >= 0) & (rel <= rows)
    group = jnp.where(rel == 0, 0, jnp.where(rel == rows, 2, 1))
    block = c // BLOCK
    inner = c - block * BLOCK
    half = c // HALF
    slot_of = (slot_hi * LANES + slot_lo).astype(jnp.int32)
    owner = slot_of // owned
    home = r // rows
    send_key = jnp.where(home == me, owner, -1)
    recv_key = jnp.where(owner == me, home, -1)
    edge = jnp.where(r - home * rows == rows - 1, home, -1)
    edges = jnp.zeros((slabs, LANES), F32)
    for i in range(lines):
        edges = edges + jnp.where(iota((slabs, LANES), 0) == edge[i : i + 1, :], 1.0, 0.0)
    peak = jnp.max(jnp.sum(edges, axis=1, keepdims=True), axis=0, keepdims=True)
    peak_ref[...] = jnp.broadcast_to(peak, (8, LANES)).astype(jnp.int32)
    key = group * keys_group + 2 * block + jnp.where(inner == BLOCK - 1, 1, 0)
    key = jnp.where(valid, key, -1)

    count = jnp.zeros((keys, 1), F32)
    for i in range(lines):
        count = count + jnp.sum(jnp.where(iota((keys, LANES), 0) == key[i : i + 1, :], 1.0, 0.0), axis=1, keepdims=True)
    big = jnp.floor(count * (1.0 / 64.0))
    small = count - 64.0 * big
    ka, kb = iota((keys, keys), 0), iota((keys, keys), 1)
    below = jnp.where((kb < ka) & (kb // keys_group == ka // keys_group), 1.0, 0.0).astype(BF16)
    start = 64.0 * jnp.dot(below, jnp.broadcast_to(big, (keys, LANES)).astype(BF16), preferred_element_type=F32)
    start = start + jnp.dot(below, jnp.broadcast_to(small, (keys, LANES)).astype(BF16), preferred_element_type=F32)
    start = start + ((iota((keys, LANES), 0) // keys_group) * (cap_chunks * LANES)).astype(F32)
    wide_keys = marks_ref.shape[1]
    diagonal = iota((keys, wide_keys), 0) == iota((keys, wide_keys), 1)
    marks_ref[...] = jnp.concatenate(
        [jnp.sum(jnp.where(diagonal, x, 0.0), axis=0, keepdims=True) for x in (start[:, :1], start[:, :1] + count)], axis=0
    ).astype(jnp.int32)

    upper = jnp.where(iota((LANES, LANES), 0) < iota((LANES, LANES), 1), 1.0, 0.0).astype(BF16)
    carry = jnp.concatenate([start[:, :1], jnp.zeros((2 * slabs, 1), F32)], axis=0)
    spots, sends, recvs = [], [], []
    for i in range(lines):
        hot = jnp.concatenate(
            [
                jnp.where(iota((keys, LANES), 0) == key[i : i + 1, :], 1.0, 0.0),
                jnp.where(iota((slabs, LANES), 0) == send_key[i : i + 1, :], 1.0, 0.0),
                jnp.where(iota((slabs, LANES), 0) == recv_key[i : i + 1, :], 1.0, 0.0),
            ],
            axis=0,
        )
        before = jnp.dot(hot.astype(BF16), upper, preferred_element_type=F32)
        ranks = hot * (before + carry)
        spots.append(jnp.sum(ranks[:keys], axis=0, keepdims=True))
        sends.append(jnp.sum(ranks[keys : keys + slabs], axis=0, keepdims=True))
        recvs.append(jnp.sum(ranks[keys + slabs :], axis=0, keepdims=True))
        carry = carry + jnp.sum(hot, axis=1, keepdims=True)
    spot = jnp.concatenate(spots, axis=0).astype(jnp.int32)
    spot = jnp.where(valid, spot, -1)
    send = jnp.concatenate(sends, axis=0).astype(jnp.int32)
    recv = jnp.concatenate(recvs, axis=0).astype(jnp.int32)
    send_line = jnp.where(send_key >= 0, owner * pair_lines + (send >> 7), 200)
    recv_line = jnp.where(recv_key >= 0, home * pair_lines + (recv >> 7), -1)

    rf = rf_ref[...]
    cf = cf_ref[...]
    w = w_ref[...]
    rf_top = rf.astype(BF16).astype(F32)
    w_top = w.astype(BF16).astype(F32)
    values = [
        half.astype(F32),
        (c - half * HALF).astype(F32),
        (1.0 - cf).astype(BF16).astype(F32),
        cf.astype(BF16).astype(F32),
        rf_top,
        rf - rf_top,
        w_top,
        w - w_top,
        rel.astype(F32),
        send_line.astype(F32),
        (send & 127).astype(F32),
    ]
    total = jnp.zeros((FIELDS * chunks, LANES), F32)
    for i in range(0, lines, step):
        target = wide(spot, i)
        here = iota((chunks, step * LANES), 0) == (target >> 7)
        stack = jnp.concatenate([jnp.where(here, wide(v, i), 0.0) for v in values], axis=0).astype(BF16)
        place = jnp.where(iota((LANES, step * LANES), 0) == (target & 127), 1.0, 0.0).astype(BF16)
        total = total + nt_dot(stack, place)
    for f in range(FIELDS):
        plan_ref[f] = total[f * chunks : (f + 1) * chunks, :]

    slot_here = slot_of - me * owned
    received = slabs * pair_lines
    found = jnp.zeros((2 * received, LANES), F32)
    for i in range(0, lines, step):
        here = iota((received, step * LANES), 0) == wide(recv_line, i)
        target = wide(slot_here, i)
        stack = jnp.concatenate(
            [jnp.where(here, (target >> 7).astype(F32), 0.0), jnp.where(here, (target & 127).astype(F32), 0.0)], axis=0
        ).astype(BF16)
        place = jnp.where(iota((LANES, step * LANES), 0) == (wide(recv, i) & 127), 1.0, 0.0).astype(BF16)
        found = found + nt_dot(stack, place)
    places_ref[...] = (found[:received] * LANES + found[received:]).astype(jnp.int32)


def column_table(plan_ref, chunk, number):
    line = pl.ds(chunk, 1)
    column = plan_ref[0, line, :] * HALF + plan_ref[1, line, :] - (number * BLOCK).astype(F32)
    low = plan_ref[2, line, :].astype(BF16)
    high = plan_ref[3, line, :].astype(BF16)
    cells = iota((HALF, LANES), 0).astype(F32).astype(BF16)
    pieces = []
    for begin in range(0, BLOCK, HALF):
        near = jnp.clip(column - begin, -2.0, HALF).astype(BF16)
        after = jnp.clip(column - (begin - 1), -2.0, HALF).astype(BF16)
        pieces.append(jnp.where(cells == near, low, jnp.where(cells == after, high, jnp.zeros((), BF16))))
    return jnp.concatenate(pieces, axis=0)


def row_pattern(plan_ref, chunk, rows, depth):
    line = pl.ds(chunk, 1)
    rf = plan_ref[4, line, :] + plan_ref[5, line, :]
    rel = plan_ref[8, line, :].astype(jnp.int32)
    row = iota((depth, LANES), 0) % rows + 1
    return jnp.where(row == rel, 1.0 - rf, jnp.where(row == rel + 1, rf, 0.0))


def group_chunks(marks_ref, group, keys_group, base):
    count = (marks_ref[1, (group + 1) * keys_group - 1] - base + LANES - 1) // LANES
    return jnp.maximum(count, 1)


def chunk_range(marks_ref, group, number, keys_group, cap_chunks):
    at = group * keys_group + 2 * number
    begin = marks_ref[0, jnp.maximum(at - 1, group * keys_group)]
    end = marks_ref[1, at + 1]
    base = group * cap_chunks
    last = base + group_chunks(marks_ref, group, keys_group, base * LANES) - 1
    return jnp.minimum(begin // LANES, last), jnp.where(end > begin, (end + LANES - 1) // LANES, 0)


def forward_kernel(cap_chunks, blocks, field_ref, plan_ref, marks_ref, value_ref, sums, flat):
    probes, rows, _ = field_ref.shape
    depth = probes * rows
    keys_group = 2 * blocks
    number = pl.program_id(0)
    counts = [group_chunks(marks_ref, g, keys_group, g * cap_chunks * LANES) for g in range(3)]

    @pl.when(number == 0)
    def _():
        for g in range(3):

            @pl.loop(0, counts[g])
            def _(k):
                sums[g * cap_chunks + k] = jnp.zeros((depth, LANES), F32)

    block = field_ref[...].reshape(depth, BLOCK)
    flat[...] = block
    ranges = [chunk_range(marks_ref, g, number, keys_group, cap_chunks) for g in range(3)]
    table = jnp.concatenate([column_table(plan_ref, begin, number) for begin, _ in ranges], axis=1)
    part = jnp.dot(block, table, preferred_element_type=F32)
    for g in range(3):
        sums[ranges[g][0]] += part[:, g * LANES : (g + 1) * LANES]
    for g in range(3):

        @pl.loop(ranges[g][0] + 1, ranges[g][1])
        def _(chunk):
            sums[chunk] += jnp.dot(flat[...], column_table(plan_ref, chunk, number), preferred_element_type=F32)

    @pl.when(number == blocks - 1)
    def _():
        fold = jnp.where(iota((probes, depth), 1) // rows == iota((probes, depth), 0), 1.0, 0.0).astype(BF16)
        for g in range(3):

            @pl.loop(0, counts[g])
            def _(k):
                chunk = g * cap_chunks + k
                scaled = (sums[chunk] * row_pattern(plan_ref, chunk, rows, depth)).astype(BF16)
                value_ref[chunk] = jnp.dot(fold, scaled, preferred_element_type=F32)


def swap_kernel(slabs, top, value_ref, above_ref, below_ref, send_sem, recv_sem):
    probe, me = lax.axis_index("probe"), lax.axis_index("slab")
    width = above_ref.shape[0]
    down, up = lax.rem(me + slabs - 1, slabs), lax.rem(me + 1, slabs)
    barrier = pltpu.get_barrier_semaphore()
    for peer in (down, up):
        pl.semaphore_signal(barrier, inc=1, device_id=(peer, probe), device_id_type=pl.DeviceIdType.MESH)
    pl.semaphore_wait(barrier, 2)
    copies = []
    for k, (peer, begin, target) in enumerate(((down, 0, above_ref), (up, top, below_ref))):
        copies.append(
            pltpu.make_async_remote_copy(
                src_ref=value_ref.at[begin : begin + width],
                dst_ref=target,
                send_sem=send_sem.at[k],
                recv_sem=recv_sem.at[k],
                device_id=(peer, probe),
                device_id_type=pl.DeviceIdType.MESH,
            )
        )
    for copy in copies:
        copy.start()
    for copy in copies:
        copy.wait()


def swap(slabs, cap_chunks, width, number, value):
    part = (width, *value.shape[1:])
    any_space = pl.BlockSpec(memory_space=pl.ANY)
    above, below = pl.pallas_call(
        functools.partial(swap_kernel, slabs, 2 * cap_chunks),
        out_shape=(jax.ShapeDtypeStruct(part, F32), jax.ShapeDtypeStruct(part, F32)),
        in_specs=[any_space],
        out_specs=(any_space, any_space),
        scratch_shapes=[pltpu.SemaphoreType.DMA((2,)), pltpu.SemaphoreType.DMA((2,))],
        compiler_params=pltpu.CompilerParams(collective_id=number, has_side_effects=True),
        name="swap",
    )(value)
    return above, below


def merge_kernel(cap_chunks, blocks, value_ref, above_ref, below_ref, plan_ref, marks_ref, spread_ref, packed_ref, squares, parts):
    slabs = packed_ref.shape[0]
    outgoing, probes, _ = parts.shape
    lines = outgoing // slabs
    keys_group = 2 * blocks
    squares[...] = jnp.zeros_like(squares)
    parts[...] = jnp.zeros_like(parts)
    for g in range(3):
        count = group_chunks(marks_ref, g, keys_group, g * cap_chunks * LANES)

        @pl.loop(0, count)
        def _(k):
            chunk = g * cap_chunks + k
            value = value_ref[chunk]
            if g == 0:
                value = value + below_ref[k]
            if g == 2:
                value = value + above_ref[k]
            line = pl.ds(chunk, 1)
            spread = value * (plan_ref[6, line, :] + plan_ref[7, line, :])
            spread_ref[chunk] = spread.astype(BF16)
            if g > 0:
                squares[...] += spread * value
                high = plan_ref[9, line, :].astype(jnp.int32)
                low = plan_ref[10, line, :].astype(jnp.int32)
                place = jnp.where(iota((LANES, LANES), 0) == low, 1.0, 0.0).astype(BF16)
                stack = jnp.concatenate([jnp.where(high == d, value, 0.0) for d in range(outgoing)], axis=0).astype(BF16)
                parts[...] += nt_dot(stack, place).reshape(outgoing, probes, LANES)

    folded = squares[:8, :]
    for d in range(8, probes, 8):
        folded = folded + squares[d : d + 8, :]
    for d in range(slabs):
        for e in range(lines):
            packed_ref[d, e * probes : (e + 1) * probes, :] = parts[d * lines + e]
        packed_ref[d, lines * probes :, :] = folded


def unpack_kernel(groups, scale, packed_ref, places_ref, observed_ref, mean_ref, traces, send_sem, recv_sem):
    slab, me = lax.axis_index("slab"), lax.axis_index("probe")
    slabs = packed_ref.shape[0]
    probes, owned = observed_ref.shape
    lines = places_ref.shape[0] // slabs
    barrier = pltpu.get_barrier_semaphore()
    for k in range(1, groups):
        peer = lax.rem(me + k, groups)
        pl.semaphore_signal(barrier, inc=1, device_id=(slab, peer), device_id_type=pl.DeviceIdType.MESH)
    own = packed_ref[0, lines * probes :, :]
    for d in range(1, slabs):
        own = own + packed_ref[d, lines * probes :, :]
    traces[me] = own
    pl.semaphore_wait(barrier, groups - 1)

    def tile(k, source, peer):
        return pltpu.make_async_remote_copy(
            src_ref=traces.at[me],
            dst_ref=traces.at[source],
            send_sem=send_sem.at[k],
            recv_sem=recv_sem.at[k],
            device_id=(slab, peer),
            device_id_type=pl.DeviceIdType.MESH,
        )

    for k in range(1, groups):
        tile(k, me, lax.rem(me + k, groups)).start()
    total = jnp.zeros((probes, owned), F32)
    for d in range(slabs):
        for e in range(lines):
            at = d * lines + e
            place = jnp.where(iota((owned, LANES), 0) == places_ref[at : at + 1, :], 1.0, 0.0).astype(BF16)
            total = total + nt_dot(packed_ref[d, e * probes : (e + 1) * probes, :].astype(BF16), place)
    observed_ref[...] = total
    for k in range(1, groups):
        source = lax.rem(me + groups - k, groups)
        tile(k, source, source).wait()
    summed = jnp.sum(jnp.sum(traces[...], axis=0), axis=0, keepdims=True)
    mean_ref[...] = jnp.broadcast_to(jnp.sum(summed, axis=1, keepdims=True) * scale, mean_ref.shape)


def adjoint_kernel(cap_chunks, blocks, spread_ref, plan_ref, marks_ref, out_ref, sources, total):
    probes, rows, _ = out_ref.shape
    depth = probes * rows
    keys_group = 2 * blocks
    number = pl.program_id(0)

    @pl.when(number == 0)
    def _():
        raise_rows = jnp.where(iota((depth, probes), 0) // rows == iota((depth, probes), 1), 1.0, 0.0).astype(BF16)
        for g in range(3):
            count = group_chunks(marks_ref, g, keys_group, g * cap_chunks * LANES)

            @pl.loop(0, count)
            def _(k):
                chunk = g * cap_chunks + k
                raised = jnp.dot(raise_rows, spread_ref[chunk], preferred_element_type=F32)
                sources[chunk] = (raised * row_pattern(plan_ref, chunk, rows, depth)).astype(BF16)

    ranges = [chunk_range(marks_ref, g, number, keys_group, cap_chunks) for g in range(3)]
    table = jnp.concatenate([column_table(plan_ref, begin, number) for begin, _ in ranges], axis=1)
    source = jnp.concatenate([sources[begin] for begin, _ in ranges], axis=1)
    total[...] = nt_dot(source, table)
    for g in range(3):

        @pl.loop(ranges[g][0] + 1, ranges[g][1])
        def _(chunk):
            total[...] += nt_dot(sources[chunk], column_table(plan_ref, chunk, number))

    out_ref[...] = total[...].astype(BF16).reshape(probes, rows, BLOCK)


def body(slab_count, probe_groups, probe_fields, sensor_rows, sensor_cols, row_frac, col_frac, sensor_weights, owner_order):
    probes, rows, width = probe_fields.shape
    sensors = sensor_rows.shape[0]
    depth = probes * rows
    lines = sensors // LANES
    blocks = width // BLOCK
    keys = 6 * blocks
    most = min(sensors, 4 * sensors // slab_count)
    cap_chunks = -(-most // (8 * LANES)) * 8
    chunks = 3 * cap_chunks
    pair_lines = -(-most // (slab_count * LANES))
    outgoing = slab_count * pair_lines
    me = jnp.reshape(lax.axis_index("slab"), (1,)).astype(jnp.int32)
    boxed = [x.reshape(lines, LANES) for x in (sensor_rows, sensor_cols, row_frac, col_frac, sensor_weights, owner_order)]
    vmem = pl.BlockSpec(memory_space=VMEM)
    smem = pl.BlockSpec(memory_space=SMEM)
    plan, marks, places, peak = pl.pallas_call(
        functools.partial(plan_kernel, rows, cap_chunks, blocks, slab_count, pair_lines),
        out_shape=(
            jax.ShapeDtypeStruct((FIELDS, chunks, LANES), F32),
            jax.ShapeDtypeStruct((2, -(-keys // LANES) * LANES), jnp.int32),
            jax.ShapeDtypeStruct((outgoing, LANES), jnp.int32),
            jax.ShapeDtypeStruct((8, LANES), jnp.int32),
        ),
        in_specs=[smem] + [vmem] * 6,
        out_specs=(vmem, vmem, vmem, vmem),
        compiler_params=LIMIT,
        name="plan",
    )(me, *boxed)
    value = pl.pallas_call(
        functools.partial(forward_kernel, cap_chunks, blocks),
        out_shape=jax.ShapeDtypeStruct((chunks, probes, LANES), F32),
        grid=(blocks,),
        in_specs=[pl.BlockSpec((probes, rows, BLOCK), lambda n: (0, 0, n)), vmem, smem],
        out_specs=vmem,
        scratch_shapes=[VMEM((chunks, depth, LANES), F32), VMEM((depth, BLOCK), BF16)],
        compiler_params=LIMIT,
        name="forward",
    )(probe_fields, plan, marks)
    few = min(cap_chunks, -(-5 * most // (4 * rows * LANES)))

    def merged(above, below):
        return pl.pallas_call(
            functools.partial(merge_kernel, cap_chunks, blocks),
            out_shape=(
                jax.ShapeDtypeStruct((chunks, probes, LANES), BF16),
                jax.ShapeDtypeStruct((slab_count, pair_lines * probes + 8, LANES), F32),
            ),
            in_specs=[vmem, vmem, vmem, vmem, smem],
            out_specs=(vmem, vmem),
            scratch_shapes=[VMEM((probes, LANES), F32), VMEM((outgoing, probes, LANES), F32)],
            compiler_params=LIMIT,
            name="merge",
        )(value, above, below, plan, marks)

    spread, packed = lax.cond(
        peak[0, 0] <= few * LANES,
        lambda: merged(*swap(slab_count, cap_chunks, few, 0, value)),
        lambda: merged(*swap(slab_count, cap_chunks, cap_chunks, 1, value)),
    )
    arrived = lax.all_to_all(packed, "slab", 0, 0, tiled=True)
    adjoint = pl.pallas_call(
        functools.partial(adjoint_kernel, cap_chunks, blocks),
        out_shape=jax.ShapeDtypeStruct((probes, rows, width), BF16),
        grid=(blocks,),
        in_specs=[vmem, vmem, smem],
        out_specs=pl.BlockSpec((probes, rows, BLOCK), lambda n: (0, 0, n)),
        scratch_shapes=[
            VMEM((chunks, depth, LANES), BF16),
            VMEM((depth, BLOCK), F32),
        ],
        compiler_params=LIMIT,
        cost_estimate=pl.CostEstimate(flops=4 * 10**9, bytes_accessed=8 * 10**6, transcendentals=0),
        name="adjoint",
    )(spread, plan, marks)
    observed, mean = pl.pallas_call(
        functools.partial(unpack_kernel, probe_groups, 1.0 / (probes * probe_groups * sensors)),
        out_shape=(
            jax.ShapeDtypeStruct((probes, sensors // slab_count), F32),
            jax.ShapeDtypeStruct((1, LANES), F32),
        ),
        in_specs=[vmem, vmem],
        out_specs=(vmem, vmem),
        scratch_shapes=[
            VMEM((probe_groups, 8, LANES), F32),
            pltpu.SemaphoreType.DMA((probe_groups,)),
            pltpu.SemaphoreType.DMA((probe_groups,)),
        ],
        compiler_params=pltpu.CompilerParams(collective_id=2, has_side_effects=True, vmem_limit_bytes=40 * 1024 * 1024),
        name="unpack",
    )(arrived, places)
    return adjoint, observed, mean[0, 0]


def solution(mesh):
    placed = (P("probe", "slab", None), P(), P(), P(), P(), P(), P())
    return jax.shard_map(
        functools.partial(body, mesh.shape["slab"], mesh.shape["probe"]),
        mesh=mesh,
        in_specs=placed,
        out_specs=(P("probe", "slab", None), P("probe", "slab"), P()),
        check_vma=False,
    )
```

```python
import functools

import jax
import jax.numpy as jnp
from jax import lax
from jax.experimental import pallas as pl
from jax.experimental.pallas import tpu as pltpu
from jax.sharding import PartitionSpec as P

LANES = 128
BLOCK = 1024
HALF = 256
FIELDS = 11
F32 = jnp.float32
BF16 = jnp.bfloat16
NT = (((1,), (1,)), ((), ()))
VMEM = pltpu.VMEM
SMEM = pltpu.SMEM
LIMIT = pltpu.CompilerParams(vmem_limit_bytes=60 * 1024 * 1024)


def iota(shape, dim):
    return lax.broadcasted_iota(jnp.int32, shape, dim)


def nt_dot(a, b):
    return lax.dot_general(a, b, NT, preferred_element_type=F32)


def plan_kernel(rows, cap_chunks, blocks, slabs, pair_lines, me_ref, r_ref, c_ref, rf_ref, cf_ref, w_ref, order_ref, plan_ref, marks_ref, places_ref, peak_ref):
    lines = r_ref.shape[0]
    sensors = lines * LANES
    step = min(4, lines)
    me = me_ref[0]
    first = me * rows
    owned = lines * LANES // slabs
    keys_group = 2 * blocks
    keys = 3 * keys_group
    chunks = 3 * cap_chunks

    def wide(x, i):
        return jnp.concatenate([x[i + j : i + j + 1, :] for j in range(step)], axis=1)

    order = order_ref[...]
    slot = iota((lines, LANES), 0) * LANES + iota((lines, LANES), 1)
    found = jnp.zeros((2 * lines, LANES), F32)
    for i in range(0, lines, step):
        target = wide(order, i)
        mine = wide(slot, i)
        here = iota((lines, step * LANES), 0) == (target >> 7)
        stack = jnp.concatenate(
            [jnp.where(here, (mine >> 7).astype(F32), 0.0), jnp.where(here, (mine & 127).astype(F32), 0.0)], axis=0
        ).astype(BF16)
        place = jnp.where(iota((LANES, step * LANES), 0) == (target & 127), 1.0, 0.0).astype(BF16)
        found = found + nt_dot(stack, place)
    slot_hi = found[:lines, :]
    slot_lo = found[lines:, :]

    r = r_ref[...]
    c = c_ref[...]
    rel = r - first + 1
    valid = (rel >= 0) & (rel <= rows)
    group = jnp.where(rel == 0, 0, jnp.where(rel == rows, 2, 1))
    block = c // BLOCK
    inner = c - block * BLOCK
    half = c // HALF
    slot_of = (slot_hi * LANES + slot_lo).astype(jnp.int32)
    owner = slot_of // owned
    home = r // rows
    send_key = jnp.where(home == me, owner, -1)
    recv_key = jnp.where(owner == me, home, -1)
    edge = jnp.where(r - home * rows == rows - 1, home, -1)
    edges = jnp.zeros((slabs, LANES), F32)
    for i in range(lines):
        edges = edges + jnp.where(iota((slabs, LANES), 0) == edge[i : i + 1, :], 1.0, 0.0)
    peak_ref[0] = jnp.max(jnp.sum(edges, axis=1, keepdims=True)).astype(jnp.int32)
    key = group * keys_group + 2 * block + jnp.where(inner == BLOCK - 1, 1, 0)
    key = jnp.where(valid, key, -1)

    count = jnp.zeros((keys, 1), F32)
    for i in range(lines):
        count = count + jnp.sum(jnp.where(iota((keys, LANES), 0) == key[i : i + 1, :], 1.0, 0.0), axis=1, keepdims=True)
    big = jnp.floor(count * (1.0 / 64.0))
    small = count - 64.0 * big
    ka, kb = iota((keys, keys), 0), iota((keys, keys), 1)
    below = jnp.where((kb < ka) & (kb // keys_group == ka // keys_group), 1.0, 0.0).astype(BF16)
    start = 64.0 * jnp.dot(below, jnp.broadcast_to(big, (keys, LANES)).astype(BF16), preferred_element_type=F32)
    start = start + jnp.dot(below, jnp.broadcast_to(small, (keys, LANES)).astype(BF16), preferred_element_type=F32)
    start = start + ((iota((keys, LANES), 0) // keys_group) * (cap_chunks * LANES)).astype(F32)
    wide_keys = marks_ref.shape[1]
    diagonal = iota((keys, wide_keys), 0) == iota((keys, wide_keys), 1)
    marks_ref[...] = jnp.concatenate(
        [jnp.sum(jnp.where(diagonal, x, 0.0), axis=0, keepdims=True) for x in (start[:, :1], start[:, :1] + count)], axis=0
    ).astype(jnp.int32)

    upper = jnp.where(iota((LANES, LANES), 0) < iota((LANES, LANES), 1), 1.0, 0.0).astype(BF16)
    carry = jnp.concatenate([start[:, :1], jnp.zeros((2 * slabs, 1), F32)], axis=0)
    spots, sends, recvs = [], [], []
    for i in range(lines):
        hot = jnp.concatenate(
            [
                jnp.where(iota((keys, LANES), 0) == key[i : i + 1, :], 1.0, 0.0),
                jnp.where(iota((slabs, LANES), 0) == send_key[i : i + 1, :], 1.0, 0.0),
                jnp.where(iota((slabs, LANES), 0) == recv_key[i : i + 1, :], 1.0, 0.0),
            ],
            axis=0,
        )
        before = jnp.dot(hot.astype(BF16), upper, preferred_element_type=F32)
        ranks = hot * (before + carry)
        spots.append(jnp.sum(ranks[:keys], axis=0, keepdims=True))
        sends.append(jnp.sum(ranks[keys : keys + slabs], axis=0, keepdims=True))
        recvs.append(jnp.sum(ranks[keys + slabs :], axis=0, keepdims=True))
        carry = carry + jnp.sum(hot, axis=1, keepdims=True)
    spot = jnp.concatenate(spots, axis=0).astype(jnp.int32)
    spot = jnp.where(valid, spot, -1)
    send = jnp.concatenate(sends, axis=0).astype(jnp.int32)
    recv = jnp.concatenate(recvs, axis=0).astype(jnp.int32)
    send_line = jnp.where(send_key >= 0, owner * pair_lines + (send >> 7), 200)
    recv_line = jnp.where(recv_key >= 0, home * pair_lines + (recv >> 7), -1)

    rf = rf_ref[...]
    cf = cf_ref[...]
    w = w_ref[...]
    rf_top = rf.astype(BF16).astype(F32)
    w_top = w.astype(BF16).astype(F32)
    values = [
        half.astype(F32),
        (c - half * HALF).astype(F32),
        (1.0 - cf).astype(BF16).astype(F32),
        cf.astype(BF16).astype(F32),
        rf_top,
        rf - rf_top,
        w_top,
        w - w_top,
        rel.astype(F32),
        send_line.astype(F32),
        (send & 127).astype(F32),
    ]
    total = jnp.zeros((FIELDS * chunks, LANES), F32)
    for i in range(0, lines, step):
        target = wide(spot, i)
        here = iota((chunks, step * LANES), 0) == (target >> 7)
        stack = jnp.concatenate([jnp.where(here, wide(v, i), 0.0) for v in values], axis=0).astype(BF16)
        place = jnp.where(iota((LANES, step * LANES), 0) == (target & 127), 1.0, 0.0).astype(BF16)
        total = total + nt_dot(stack, place)
    for f in range(FIELDS):
        plan_ref[f] = total[f * chunks : (f + 1) * chunks, :]

    slot_here = slot_of - me * owned
    received = slabs * pair_lines
    found = jnp.zeros((2 * received, LANES), F32)
    for i in range(0, lines, step):
        here = iota((received, step * LANES), 0) == wide(recv_line, i)
        target = wide(slot_here, i)
        stack = jnp.concatenate(
            [jnp.where(here, (target >> 7).astype(F32), 0.0), jnp.where(here, (target & 127).astype(F32), 0.0)], axis=0
        ).astype(BF16)
        place = jnp.where(iota((LANES, step * LANES), 0) == (wide(recv, i) & 127), 1.0, 0.0).astype(BF16)
        found = found + nt_dot(stack, place)
    places_ref[...] = (found[:received] * LANES + found[received:]).astype(jnp.int32)


def column_table(plan_ref, chunk, number):
    line = pl.ds(chunk, 1)
    column = plan_ref[0, line, :] * HALF + plan_ref[1, line, :] - (number * BLOCK).astype(F32)
    low = plan_ref[2, line, :].astype(BF16)
    high = plan_ref[3, line, :].astype(BF16)
    cells = iota((HALF, LANES), 0).astype(F32).astype(BF16)
    pieces = []
    for begin in range(0, BLOCK, HALF):
        near = jnp.clip(column - begin, -2.0, HALF).astype(BF16)
        after = jnp.clip(column - (begin - 1), -2.0, HALF).astype(BF16)
        pieces.append(jnp.where(cells == near, low, jnp.where(cells == after, high, jnp.zeros((), BF16))))
    return jnp.concatenate(pieces, axis=0)


def row_pattern(plan_ref, chunk, rows, depth):
    line = pl.ds(chunk, 1)
    rf = plan_ref[4, line, :] + plan_ref[5, line, :]
    rel = plan_ref[8, line, :].astype(jnp.int32)
    row = iota((depth, LANES), 0) % rows + 1
    return jnp.where(row == rel, 1.0 - rf, jnp.where(row == rel + 1, rf, 0.0))


def group_chunks(marks_ref, group, keys_group, base):
    count = (marks_ref[1, (group + 1) * keys_group - 1] - base + LANES - 1) // LANES
    return jnp.maximum(count, 1)


def chunk_range(marks_ref, group, number, keys_group, cap_chunks):
    at = group * keys_group + 2 * number
    begin = marks_ref[0, jnp.maximum(at - 1, group * keys_group)]
    end = marks_ref[1, at + 1]
    base = group * cap_chunks
    last = base + group_chunks(marks_ref, group, keys_group, base * LANES) - 1
    return jnp.minimum(begin // LANES, last), jnp.where(end > begin, (end + LANES - 1) // LANES, 0)


def forward_kernel(cap_chunks, blocks, field_ref, plan_ref, marks_ref, value_ref, sums, flat):
    probes, rows, _ = field_ref.shape
    depth = probes * rows
    keys_group = 2 * blocks
    number = pl.program_id(0)
    counts = [group_chunks(marks_ref, g, keys_group, g * cap_chunks * LANES) for g in range(3)]

    @pl.when(number == 0)
    def _():
        for g in range(3):

            @pl.loop(0, counts[g])
            def _(k):
                sums[g * cap_chunks + k] = jnp.zeros((depth, LANES), F32)

    block = field_ref[...].reshape(depth, BLOCK)
    flat[...] = block
    ranges = [chunk_range(marks_ref, g, number, keys_group, cap_chunks) for g in range(3)]
    table = jnp.concatenate([column_table(plan_ref, begin, number) for begin, _ in ranges], axis=1)
    part = jnp.dot(block, table, preferred_element_type=F32)
    for g in range(3):
        sums[ranges[g][0]] += part[:, g * LANES : (g + 1) * LANES]
    for g in range(3):

        @pl.loop(ranges[g][0] + 1, ranges[g][1])
        def _(chunk):
            sums[chunk] += jnp.dot(flat[...], column_table(plan_ref, chunk, number), preferred_element_type=F32)

    @pl.when(number == blocks - 1)
    def _():
        fold = jnp.where(iota((probes, depth), 1) // rows == iota((probes, depth), 0), 1.0, 0.0).astype(BF16)
        for g in range(3):

            @pl.loop(0, counts[g])
            def _(k):
                chunk = g * cap_chunks + k
                scaled = (sums[chunk] * row_pattern(plan_ref, chunk, rows, depth)).astype(BF16)
                value_ref[chunk] = jnp.dot(fold, scaled, preferred_element_type=F32)


def swap_kernel(slabs, top, value_ref, above_ref, below_ref, send_sem, recv_sem):
    probe, me = lax.axis_index("probe"), lax.axis_index("slab")
    width = above_ref.shape[0]
    down, up = lax.rem(me + slabs - 1, slabs), lax.rem(me + 1, slabs)
    barrier = pltpu.get_barrier_semaphore()
    for peer in (down, up):
        pl.semaphore_signal(barrier, inc=1, device_id=(peer, probe), device_id_type=pl.DeviceIdType.MESH)
    pl.semaphore_wait(barrier, 2)
    copies = []
    for k, (peer, begin, target) in enumerate(((down, 0, above_ref), (up, top, below_ref))):
        copies.append(
            pltpu.make_async_remote_copy(
                src_ref=value_ref.at[begin : begin + width],
                dst_ref=target,
                send_sem=send_sem.at[k],
                recv_sem=recv_sem.at[k],
                device_id=(peer, probe),
                device_id_type=pl.DeviceIdType.MESH,
            )
        )
    for copy in copies:
        copy.start()
    for copy in copies:
        copy.wait()


def swap(slabs, cap_chunks, width, number, value):
    part = (width, *value.shape[1:])
    any_space = pl.BlockSpec(memory_space=pl.ANY)
    above, below = pl.pallas_call(
        functools.partial(swap_kernel, slabs, 2 * cap_chunks),
        out_shape=(jax.ShapeDtypeStruct(part, F32), jax.ShapeDtypeStruct(part, F32)),
        in_specs=[any_space],
        out_specs=(any_space, any_space),
        scratch_shapes=[pltpu.SemaphoreType.DMA((2,)), pltpu.SemaphoreType.DMA((2,))],
        compiler_params=pltpu.CompilerParams(collective_id=number, has_side_effects=True),
        name="swap",
    )(value)
    return above, below


def merge_kernel(cap_chunks, blocks, value_ref, above_ref, below_ref, plan_ref, marks_ref, spread_ref, packed_ref, squares, parts):
    slabs = packed_ref.shape[0]
    outgoing, probes, _ = parts.shape
    lines = outgoing // slabs
    keys_group = 2 * blocks
    squares[...] = jnp.zeros_like(squares)
    parts[...] = jnp.zeros_like(parts)
    for g in range(3):
        count = group_chunks(marks_ref, g, keys_group, g * cap_chunks * LANES)

        @pl.loop(0, count)
        def _(k):
            chunk = g * cap_chunks + k
            value = value_ref[chunk]
            if g == 0:
                value = value + below_ref[k]
            if g == 2:
                value = value + above_ref[k]
            line = pl.ds(chunk, 1)
            spread = value * (plan_ref[6, line, :] + plan_ref[7, line, :])
            spread_ref[chunk] = spread.astype(BF16)
            if g > 0:
                squares[...] += spread * value
                high = plan_ref[9, line, :].astype(jnp.int32)
                low = plan_ref[10, line, :].astype(jnp.int32)
                place = jnp.where(iota((LANES, LANES), 0) == low, 1.0, 0.0).astype(BF16)
                stack = jnp.concatenate([jnp.where(high == d, value, 0.0) for d in range(outgoing)], axis=0).astype(BF16)
                parts[...] += nt_dot(stack, place).reshape(outgoing, probes, LANES)

    folded = squares[:8, :]
    for d in range(8, probes, 8):
        folded = folded + squares[d : d + 8, :]
    for d in range(slabs):
        for e in range(lines):
            packed_ref[d, e * probes : (e + 1) * probes, :] = parts[d * lines + e]
        packed_ref[d, lines * probes :, :] = folded


def unpack_kernel(groups, scale, packed_ref, places_ref, observed_ref, mean_ref, traces, send_sem, recv_sem):
    slab, me = lax.axis_index("slab"), lax.axis_index("probe")
    slabs = packed_ref.shape[0]
    probes, owned = observed_ref.shape
    lines = places_ref.shape[0] // slabs
    barrier = pltpu.get_barrier_semaphore()
    for k in range(1, groups):
        peer = lax.rem(me + k, groups)
        pl.semaphore_signal(barrier, inc=1, device_id=(slab, peer), device_id_type=pl.DeviceIdType.MESH)
    own = packed_ref[0, lines * probes :, :]
    for d in range(1, slabs):
        own = own + packed_ref[d, lines * probes :, :]
    traces[me] = own
    pl.semaphore_wait(barrier, groups - 1)

    def tile(k, source, peer):
        return pltpu.make_async_remote_copy(
            src_ref=traces.at[me],
            dst_ref=traces.at[source],
            send_sem=send_sem.at[k],
            recv_sem=recv_sem.at[k],
            device_id=(slab, peer),
            device_id_type=pl.DeviceIdType.MESH,
        )

    for k in range(1, groups):
        tile(k, me, lax.rem(me + k, groups)).start()
    total = jnp.zeros((probes, owned), F32)
    for d in range(slabs):
        for e in range(lines):
            at = d * lines + e
            place = jnp.where(iota((owned, LANES), 0) == places_ref[at : at + 1, :], 1.0, 0.0).astype(BF16)
            total = total + nt_dot(packed_ref[d, e * probes : (e + 1) * probes, :].astype(BF16), place)
    observed_ref[...] = total
    for k in range(1, groups):
        source = lax.rem(me + groups - k, groups)
        tile(k, source, source).wait()
    summed = jnp.sum(jnp.sum(traces[...], axis=0), axis=0, keepdims=True)
    mean_ref[...] = jnp.broadcast_to(jnp.sum(summed, axis=1, keepdims=True) * scale, mean_ref.shape)


def adjoint_kernel(cap_chunks, blocks, spread_ref, plan_ref, marks_ref, out_ref, sources, total):
    probes, rows, _ = out_ref.shape
    depth = probes * rows
    keys_group = 2 * blocks
    number = pl.program_id(0)

    @pl.when(number == 0)
    def _():
        raise_rows = jnp.where(iota((depth, probes), 0) // rows == iota((depth, probes), 1), 1.0, 0.0).astype(BF16)
        for g in range(3):
            count = group_chunks(marks_ref, g, keys_group, g * cap_chunks * LANES)

            @pl.loop(0, count)
            def _(k):
                chunk = g * cap_chunks + k
                raised = jnp.dot(raise_rows, spread_ref[chunk], preferred_element_type=F32)
                sources[chunk] = (raised * row_pattern(plan_ref, chunk, rows, depth)).astype(BF16)

    ranges = [chunk_range(marks_ref, g, number, keys_group, cap_chunks) for g in range(3)]
    table = jnp.concatenate([column_table(plan_ref, begin, number) for begin, _ in ranges], axis=1)
    source = jnp.concatenate([sources[begin] for begin, _ in ranges], axis=1)
    total[...] = nt_dot(source, table)
    for g in range(3):

        @pl.loop(ranges[g][0] + 1, ranges[g][1])
        def _(chunk):
            total[...] += nt_dot(sources[chunk], column_table(plan_ref, chunk, number))

    out_ref[...] = total[...].astype(BF16).reshape(probes, rows, BLOCK)


def body(slab_count, probe_groups, probe_fields, sensor_rows, sensor_cols, row_frac, col_frac, sensor_weights, owner_order):
    probes, rows, width = probe_fields.shape
    sensors = sensor_rows.shape[0]
    depth = probes * rows
    lines = sensors // LANES
    blocks = width // BLOCK
    keys = 6 * blocks
    most = min(sensors, 4 * sensors // slab_count)
    cap_chunks = -(-most // (8 * LANES)) * 8
    chunks = 3 * cap_chunks
    pair_lines = -(-most // (slab_count * LANES))
    outgoing = slab_count * pair_lines
    me = jnp.reshape(lax.axis_index("slab"), (1,)).astype(jnp.int32)
    boxed = [x.reshape(lines, LANES) for x in (sensor_rows, sensor_cols, row_frac, col_frac, sensor_weights, owner_order)]
    vmem = pl.BlockSpec(memory_space=VMEM)
    smem = pl.BlockSpec(memory_space=SMEM)
    plan, marks, places, peak = pl.pallas_call(
        functools.partial(plan_kernel, rows, cap_chunks, blocks, slab_count, pair_lines),
        out_shape=(
            jax.ShapeDtypeStruct((FIELDS, chunks, LANES), F32),
            jax.ShapeDtypeStruct((2, -(-keys // LANES) * LANES), jnp.int32),
            jax.ShapeDtypeStruct((outgoing, LANES), jnp.int32),
            jax.ShapeDtypeStruct((1,), jnp.int32),
        ),
        in_specs=[smem] + [vmem] * 6,
        out_specs=(vmem, vmem, vmem, smem),
        compiler_params=LIMIT,
        name="plan",
    )(me, *boxed)
    value = pl.pallas_call(
        functools.partial(forward_kernel, cap_chunks, blocks),
        out_shape=jax.ShapeDtypeStruct((chunks, probes, LANES), F32),
        grid=(blocks,),
        in_specs=[pl.BlockSpec((probes, rows, BLOCK), lambda n: (0, 0, n)), vmem, smem],
        out_specs=vmem,
        scratch_shapes=[VMEM((chunks, depth, LANES), F32), VMEM((depth, BLOCK), BF16)],
        compiler_params=LIMIT,
        name="forward",
    )(probe_fields, plan, marks)
    few = min(cap_chunks, -(-5 * most // (4 * rows * LANES)))

    def merged(above, below):
        return pl.pallas_call(
            functools.partial(merge_kernel, cap_chunks, blocks),
            out_shape=(
                jax.ShapeDtypeStruct((chunks, probes, LANES), BF16),
                jax.ShapeDtypeStruct((slab_count, pair_lines * probes + 8, LANES), F32),
            ),
            in_specs=[vmem, vmem, vmem, vmem, smem],
            out_specs=(vmem, vmem),
            scratch_shapes=[VMEM((probes, LANES), F32), VMEM((outgoing, probes, LANES), F32)],
            compiler_params=LIMIT,
            name="merge",
        )(value, above, below, plan, marks)

    spread, packed = lax.cond(
        peak[0] <= few * LANES,
        lambda: merged(*swap(slab_count, cap_chunks, few, 0, value)),
        lambda: merged(*swap(slab_count, cap_chunks, cap_chunks, 1, value)),
    )
    arrived = lax.all_to_all(packed, "slab", 0, 0, tiled=True)
    adjoint = pl.pallas_call(
        functools.partial(adjoint_kernel, cap_chunks, blocks),
        out_shape=jax.ShapeDtypeStruct((probes, rows, width), BF16),
        grid=(blocks,),
        in_specs=[vmem, vmem, smem],
        out_specs=pl.BlockSpec((probes, rows, BLOCK), lambda n: (0, 0, n)),
        scratch_shapes=[
            VMEM((chunks, depth, LANES), BF16),
            VMEM((depth, BLOCK), F32),
        ],
        compiler_params=LIMIT,
        cost_estimate=pl.CostEstimate(flops=4 * 10**9, bytes_accessed=8 * 10**6, transcendentals=0),
        name="adjoint",
    )(spread, plan, marks)
    observed, mean = pl.pallas_call(
        functools.partial(unpack_kernel, probe_groups, 1.0 / (probes * probe_groups * sensors)),
        out_shape=(
            jax.ShapeDtypeStruct((probes, sensors // slab_count), F32),
            jax.ShapeDtypeStruct((1, LANES), F32),
        ),
        in_specs=[vmem, vmem],
        out_specs=(vmem, vmem),
        scratch_shapes=[
            VMEM((probe_groups, 8, LANES), F32),
            pltpu.SemaphoreType.DMA((probe_groups,)),
            pltpu.SemaphoreType.DMA((probe_groups,)),
        ],
        compiler_params=pltpu.CompilerParams(collective_id=2, has_side_effects=True, vmem_limit_bytes=40 * 1024 * 1024),
        name="unpack",
    )(arrived, places)
    return adjoint, observed, mean[0, 0]


def solution(mesh):
    placed = (P("probe", "slab", None), P(), P(), P(), P(), P(), P())
    return jax.shard_map(
        functools.partial(body, mesh.shape["slab"], mesh.shape["probe"]),
        mesh=mesh,
        in_specs=placed,
        out_specs=(P("probe", "slab", None), P("probe", "slab"), P()),
        check_vma=False,
    )
```
